32 devices in a mesh: dp: 16 (over z, y, core), tensor: 2 (over x).
Axes of the slice: x: 2, y: 2, z: 4, core: 2. Of those that a mesh axis runs over, the one named last changes fastest.
Arguments:
- tokens: bfloat16 [4096, 768], P(('dp', 'tensor')), may hold values from -6 to 6
- segments: int32 [4096], P('dp'), may hold values from 0 to 4095, as said below
- positions: int32 [4096], P('dp'), may hold values from 0 to 255, as said below
- cotangent: bfloat16 [4096, 768], P(('dp', 'tensor')), may hold values from -6 to 6
- qkv_weight: bfloat16 [1, 768, 2304], P(None, 'dp', 'tensor'), may hold values from -1 to 1
- qkv_bias: bfloat16 [1, 2304], P(None, ('tensor', 'dp')), may hold values from -3 to 3
- out_weight: bfloat16 [1, 768, 768], P(None, 'tensor', 'dp'), may hold values from -0.625 to 0.625
- out_bias: bfloat16 [1, 768], P(None, 'dp'), may hold values from -3 to 3
- up_weight: bfloat16 [1, 768, 3072], P(None, 'dp', 'tensor'), may hold values from -0.21875 to 0.21875
- up_bias: bfloat16 [1, 3072], P(None, ('tensor', 'dp')), may hold values from -3 to 3
- down_weight: bfloat16 [1, 3072, 768], P(None, 'tensor', 'dp'), may hold values from -0.109375 to 0.109375
- down_bias: bfloat16 [1, 768], P(None, 'dp'), may hold values from -3 to 3
- norm1_gain: bfloat16 [1, 768], P(None, 'dp'), may hold values from 0.5 to 1.5
- norm1_bias: bfloat16 [1, 768], P(None, 'dp'), may hold values from -2 to 2
- norm2_gain: bfloat16 [1, 768], P(None, 'dp'), may hold values from 0.5 to 1.5
- norm2_bias: bfloat16 [1, 768], P(None, 'dp'), may hold values from -2 to 2
Outputs:
- hidden_out: bfloat16 [1, 4096, 768], P(None, ('dp', 'tensor'))
- input_grad: float32 [4096, 768], P(('dp', 'tensor'))
- grad_qkv_weight: float32 [1, 768, 2304], P(None, 'dp', 'tensor')
- grad_qkv_bias: float32 [1, 2304], P(None, ('tensor', 'dp'))
- grad_out_weight: float32 [1, 768, 768], P(None, 'tensor', 'dp')
- grad_out_bias: float32 [1, 768], P(None, 'dp')
- grad_up_weight: float32 [1, 768, 3072], P(None, 'dp', 'tensor')
- grad_up_bias: float32 [1, 3072], P(None, ('tensor', 'dp'))
- grad_down_weight: float32 [1, 3072, 768], P(None, 'tensor', 'dp')
- grad_down_bias: float32 [1, 768], P(None, 'dp')
- grad_norm1_gain: float32 [1, 768], P(None, 'dp')
- grad_norm1_bias: float32 [1, 768], P(None, 'dp')
- grad_norm2_gain: float32 [1, 768], P(None, 'dp')
- grad_norm2_bias: float32 [1, 768], P(None, 'dp')
The draws below stay inside these ranges and needn't reach their ends.
Inputs may be any that keep to these rules, and one draw needn't show every extreme that they name: `segments`: segment numbers never fall along the array, a new segment begins at the first token of every sequence of 256 tokens, and the last token of the array forms a segment of its own. `positions`: A token's position is its distance to the first token of its segment.
All inputs are finite; a program needn't handle non-finite values.
Results may differ from the reference program's by a relative error of at most 0.0094.
Values may be sent and summed in bfloat16 or wider, within the bound.
A program may use at most 128 MiB of HBM per device.

```python
import jax
import jax.numpy as jnp
from jax import lax

D = 768
HEADS = 12
HEAD = 64
ROT = 16
FF = 3072
LAYERS = 1
SEQ = 256
TOKENS = 4096


def segment_plan(key):
    coin_draw = jax.random.randint(jax.random.fold_in(key, 11), (TOKENS,), 0, 48)
    slot_index = jnp.arange(TOKENS, dtype=jnp.int32)
    starts = (coin_draw == 0) & (slot_index >= SEQ) | (slot_index % SEQ == 0) | (slot_index == TOKENS - 1)
    first_slot = lax.cummax(jnp.where(starts, slot_index, 0), axis=0)
    return (first_slot.astype(jnp.int32), (slot_index - first_slot).astype(jnp.int32))


def draw_segments(key, part):
    return segment_plan(key)[0]


def draw_positions(key, part):
    return segment_plan(key)[1]


def draw_qkv_weight(key, part):
    return (jnp.clip(jax.random.normal(key, (LAYERS, D, 3 * D), jnp.float32), -6.0, 6.0) * D ** (-0.5)).astype(jnp.bfloat16)


def raised(array, stream_key, source, target, shards_of, factor):
    def block_of(axis_at):
        return (jnp.arange(array.shape[axis_at]) // (array.shape[axis_at] // shards_of)).reshape((-1,) + (1,) * (array.ndim - 1 - axis_at))

    one_side = jax.random.permutation(stream_key, shards_of)[block_of(target)]
    far = (block_of(target) + shards_of // 2) % shards_of
    return jnp.where((block_of(source) == one_side) | (block_of(source) == far), factor * array, array)


def steps_of(rng, shape, split, least, largest):
    def one(axis_at, parts):
        heights = jax.random.uniform(jax.random.fold_in(jax.random.fold_in(rng, 6), axis_at), (parts,), jnp.float32, least / len(split), largest / len(split))
        return jnp.repeat(jnp.exp(heights), shape[axis_at] // parts).reshape((-1,) + (1,) * (len(shape) - axis_at - 1))

    factor_of = one(*split[0])
    for cut in split[1:]:
        factor_of = factor_of * one(*cut)
    return factor_of


def centred(own_key, dims, deviation, most, split=(), kind=jnp.bfloat16):
    values = jax.random.normal(own_key, dims, jnp.float32) * deviation
    if len(split) > 0:
        values = steps_of(own_key, dims, split, -0.22, 0.18) * values
    return jnp.clip(values, min=-most, max=most).astype(kind)


def heavy_noise(stream_key, dims, deviation, most, shards, heavy, held_as=jnp.bfloat16):
    entries = deviation * jax.random.normal(stream_key, dims, jnp.float32)
    if shards:
        entries = entries * steps_of(stream_key, dims, shards, -0.22, 0.18)
    return jnp.clip(raised(entries, jax.random.fold_in(stream_key, 3), *heavy), -most, most).astype(held_as)


def setup_inputs(seed: int = 0) -> dict:
    seeds = jax.random.split(jax.random.key(seed), 17)
    return {
        "tokens": centred(seeds[0], (TOKENS, D), 1.0, 6.0, ((0, 32),)),
        "segments": draw_segments(jax.random.fold_in(seeds[16], 71), 0),
        "positions": draw_positions(jax.random.fold_in(seeds[16], 71), 0),
        "cotangent": heavy_noise(seeds[3], (TOKENS, D), 1.0, 6.0, ((0, 32),), (0, 1, 32, 2.75)),
        "qkv_weight": draw_qkv_weight(jax.random.fold_in(seeds[16], 71), 0),
        "qkv_bias": centred(seeds[5], (LAYERS, 3 * D), 0.5, 3.0, ((1, 32),)),
        "out_weight": centred(seeds[6], (LAYERS, D, D), (D // 8) ** -0.5, 0.625, ((1, 2), (2, 16))),
        "out_bias": centred(seeds[7], (LAYERS, D), 0.5, 3.0, ((1, 16),)),
        "up_weight": centred(seeds[8], (LAYERS, D, FF), D ** -0.5, 0.21875, ((1, 16), (2, 2))),
        "up_bias": centred(seeds[9], (LAYERS, FF), 0.5, 3.0, ((1, 32),)),
        "down_weight": centred(seeds[10], (LAYERS, FF, D), FF ** -0.5, 0.109375, ((1, 2), (2, 16))),
        "down_bias": centred(seeds[11], (LAYERS, D), 0.5, 3.0, ((1, 16),)),
        "norm1_gain": jnp.clip(1.0 + 0.1 * jax.random.normal(seeds[12], (LAYERS, D), jnp.float32), 0.5, 1.5).astype(jnp.bfloat16),
        "norm1_bias": centred(seeds[13], (LAYERS, D), 0.3, 2.0, ((1, 16),)),
        "norm2_gain": jnp.clip(1.0 + 0.1 * jax.random.normal(seeds[14], (LAYERS, D), jnp.float32), 0.5, 1.5).astype(jnp.bfloat16),
        "norm2_bias": centred(seeds[15], (LAYERS, D), 0.3, 2.0, ((1, 16),)),
    }


EPS = 1e-05

def rotary_tables(pos_ids):
    half_rot = ROT // 2
    freq_index = jnp.arange(half_rot, dtype=jnp.float32)
    inverse = jnp.power(jnp.float32(10000.0), -2.0 * freq_index / ROT)
    angles = pos_ids.astype(jnp.float32)[:, None] * inverse[None, :]
    cos_tab = jnp.concatenate([jnp.cos(angles), jnp.cos(angles)], axis=1)
    sin_tab = jnp.concatenate([jnp.sin(angles), jnp.sin(angles)], axis=1)
    return (cos_tab, sin_tab)

def rotate(values, cos_tab, sin_tab):
    half_rot = ROT // 2
    rotary = values[..., :ROT]
    turned = jnp.concatenate([-rotary[..., half_rot:], rotary[..., :half_rot]], axis=-1)
    rotated = rotary * cos_tab[:, None, :] + turned * sin_tab[:, None, :]
    return jnp.concatenate([rotated, values[..., ROT:]], axis=-1)

def unrotate(grad_vals, cos_tab, sin_tab):
    half_rot = ROT // 2
    rotary = grad_vals[..., :ROT]
    scaled = rotary * sin_tab[:, None, :]
    back_part = jnp.concatenate([scaled[..., half_rot:], -scaled[..., :half_rot]], axis=-1)
    return jnp.concatenate([rotary * cos_tab[:, None, :] + back_part, grad_vals[..., ROT:]], axis=-1)

def layernorm(values, gain_row, bias_row):
    centre = values - lax.optimization_barrier(jnp.mean(values, axis=-1, keepdims=True))
    inv_std = lax.rsqrt(lax.optimization_barrier(jnp.mean(centre * centre, axis=-1, keepdims=True)) + EPS)
    normed = centre * inv_std
    return (normed * gain_row + bias_row, normed, inv_std)

def norm_back(upstream, normed, inv_std, gain_row):
    scaled = upstream * gain_row
    mean_term = lax.optimization_barrier(jnp.mean(scaled, axis=-1, keepdims=True))
    proj_term = lax.optimization_barrier(jnp.mean(scaled * normed, axis=-1, keepdims=True))
    grad_in = inv_std * (scaled - mean_term - normed * proj_term)
    return (grad_in, lax.optimization_barrier(jnp.sum(upstream * normed, axis=0)), lax.optimization_barrier(jnp.sum(upstream, axis=0)))

def gelu_slope(hidden_pre):
    cumul_part = 0.5 * (1.0 + jax.scipy.special.erf(hidden_pre * 0.7071067811865476))
    return cumul_part + hidden_pre * jnp.exp(-0.5 * hidden_pre * hidden_pre) * 0.3989422804014327

def seq_mask(seg_ids):
    slot_index = jnp.arange(seg_ids.shape[0])
    return (slot_index[None, :] <= slot_index[:, None]) & (seg_ids[None, :] == seg_ids[:, None])

def attention_scores(query_rot, key_rot, allowed):
    scores = jnp.einsum('qhd,khd->hqk', query_rot.astype(jnp.float32), key_rot.astype(jnp.float32)) * HEAD ** (-0.5)
    return jnp.where(allowed[None], scores, -jnp.inf)

def layer_forward(rows_in, allowed, cos_tab, sin_tab, params):
    qkv_w, qkv_b, out_w, out_b, up_w, up_b, down_w, down_b, gain_one, bias_one, gain_two, bias_two = params
    seq_len = rows_in.shape[0]
    residual = rows_in.astype(jnp.float32)
    normed_one, unit_one, inv_one = layernorm(residual, gain_one.astype(jnp.float32), bias_one.astype(jnp.float32))
    normed_two, unit_two, inv_two = layernorm(residual, gain_two.astype(jnp.float32), bias_two.astype(jnp.float32))
    normed_one = normed_one.astype(jnp.bfloat16)
    normed_two = normed_two.astype(jnp.bfloat16)
    projected = jnp.dot(normed_one, qkv_w, preferred_element_type=jnp.float32) + qkv_b.astype(jnp.float32)
    projected = projected.reshape(seq_len, HEADS, 3, HEAD)
    query_rot = rotate(projected[:, :, 0], cos_tab, sin_tab).astype(jnp.bfloat16)
    key_rot = rotate(projected[:, :, 1], cos_tab, sin_tab).astype(jnp.bfloat16)
    value_rows = projected[:, :, 2].astype(jnp.bfloat16)
    scores = attention_scores(query_rot, key_rot, allowed)
    row_peak = lax.optimization_barrier(jnp.max(scores, axis=-1, keepdims=True))
    row_total = lax.optimization_barrier(jnp.sum(jnp.exp(scores - row_peak), axis=-1, keepdims=True))
    log_total = row_peak + jnp.log(row_total)
    weights_bf = jnp.exp(scores - log_total).astype(jnp.bfloat16)
    attended = jnp.einsum('hqk,khd->qhd', weights_bf.astype(jnp.float32), value_rows.astype(jnp.float32)).astype(jnp.bfloat16)
    attended_flat = attended.reshape(seq_len, D)
    hidden_pre = jnp.dot(normed_two, up_w, preferred_element_type=jnp.float32) + up_b.astype(jnp.float32)
    hidden_act = jax.nn.gelu(hidden_pre, approximate=False).astype(jnp.bfloat16)
    branches = jnp.dot(attended_flat, out_w, preferred_element_type=jnp.float32) + jnp.dot(hidden_act, down_w, preferred_element_type=jnp.float32)
    output = (residual + branches + out_b.astype(jnp.float32) + down_b.astype(jnp.float32)).astype(jnp.bfloat16)
    saved_state = (unit_one, inv_one, unit_two, inv_two, normed_one, normed_two, query_rot, key_rot, value_rows, attended, log_total, hidden_pre, hidden_act)
    return (output, saved_state)

def layer_backward(upstream, saved_state, allowed, cos_tab, sin_tab, params):
    qkv_w, qkv_b, out_w, out_b, up_w, up_b, down_w, down_b, gain_one, bias_one, gain_two, bias_two = params
    unit_one, inv_one, unit_two, inv_two, normed_one, normed_two, query_rot, key_rot, value_rows, attended, log_total, hidden_pre, hidden_act = saved_state
    seq_len = upstream.shape[0]
    upstream_bf = upstream.astype(jnp.bfloat16)
    bias_grad = lax.optimization_barrier(jnp.sum(upstream, axis=0))
    grad_down = jnp.dot(hidden_act.T, upstream_bf, preferred_element_type=jnp.float32)
    hidden_grad = (jnp.dot(upstream_bf, down_w.T, preferred_element_type=jnp.float32) * gelu_slope(hidden_pre)).astype(jnp.bfloat16)
    grad_up = jnp.dot(normed_two.T, hidden_grad, preferred_element_type=jnp.float32)
    grad_upbias = lax.optimization_barrier(jnp.sum(hidden_grad.astype(jnp.float32), axis=0))
    two_grad = jnp.dot(hidden_grad, up_w.T, preferred_element_type=jnp.float32)
    attended_flat = attended.reshape(seq_len, D)
    grad_out = jnp.dot(attended_flat.T, upstream_bf, preferred_element_type=jnp.float32)
    attended_grad = jnp.dot(upstream_bf, out_w.T, preferred_element_type=jnp.float32).astype(jnp.bfloat16).reshape(seq_len, HEADS, HEAD)
    scores = attention_scores(query_rot, key_rot, allowed)
    weights_full = jnp.where(allowed[None], jnp.exp(scores - log_total), 0.0)
    weights_bf = weights_full.astype(jnp.bfloat16)
    row_delta = jnp.einsum('qhd,qhd->hq', attended.astype(jnp.float32), attended_grad.astype(jnp.float32))
    value_grad = jnp.einsum('hqk,qhd->khd', weights_bf.astype(jnp.float32), attended_grad.astype(jnp.float32))
    weight_grad = jnp.einsum('qhd,khd->hqk', attended_grad.astype(jnp.float32), value_rows.astype(jnp.float32))
    score_grad = (weights_full * (weight_grad - row_delta[:, :, None]) * HEAD ** (-0.5)).astype(jnp.bfloat16)
    query_grad = jnp.einsum('hqk,khd->qhd', score_grad.astype(jnp.float32), key_rot.astype(jnp.float32))
    key_grad = jnp.einsum('hqk,qhd->khd', score_grad.astype(jnp.float32), query_rot.astype(jnp.float32))
    stacked = jnp.stack([unrotate(query_grad, cos_tab, sin_tab), unrotate(key_grad, cos_tab, sin_tab), value_grad], axis=2)
    stacked = stacked.reshape(seq_len, 3 * D).astype(jnp.bfloat16)
    grad_qkv = jnp.dot(normed_one.T, stacked, preferred_element_type=jnp.float32)
    grad_qkvbias = lax.optimization_barrier(jnp.sum(stacked.astype(jnp.float32), axis=0))
    one_grad = jnp.dot(stacked, qkv_w.T, preferred_element_type=jnp.float32)
    in_one, gain_one_grad, bias_one_grad = norm_back(one_grad, unit_one, inv_one, gain_one.astype(jnp.float32))
    in_two, gain_two_grad, bias_two_grad = norm_back(two_grad, unit_two, inv_two, gain_two.astype(jnp.float32))
    rows_grad = upstream + in_one + in_two
    return (rows_grad, (grad_qkv, grad_qkvbias, grad_out, bias_grad, grad_up, grad_upbias, grad_down, gain_one_grad, bias_one_grad, gain_two_grad, bias_two_grad))

def reference(tokens, segments, positions, cotangent, qkv_weight, qkv_bias, out_weight, out_bias, up_weight, up_bias, down_weight, down_bias, norm1_gain, norm1_bias, norm2_gain, norm2_bias):
    sources = (qkv_weight, qkv_bias, out_weight, out_bias, up_weight, up_bias, down_weight, down_bias, norm1_gain, norm1_bias, norm2_gain, norm2_bias)
    param_sets = [tuple((source[layer_idx] for source in sources)) for layer_idx in range(LAYERS)]
    seq_count = tokens.shape[0] // SEQ

    def one_sequence(carry_acc, inputs):
        seq_rows, seg_ids, pos_ids, cot_rows = inputs
        cos_tab, sin_tab = rotary_tables(pos_ids)
        allowed = seq_mask(seg_ids)
        outputs = []
        saves = []
        current = seq_rows
        for layer_idx in range(LAYERS):
            current, saved_state = layer_forward(current, allowed, cos_tab, sin_tab, param_sets[layer_idx])
            outputs.append(current)
            saves.append(saved_state)
        upstream = cot_rows.astype(jnp.float32)
        new_carry = list(carry_acc)
        for layer_idx in reversed(range(LAYERS)):
            upstream, layer_grads = layer_backward(upstream, saves[layer_idx], allowed, cos_tab, sin_tab, param_sets[layer_idx])
            new_carry[layer_idx] = tuple((old_sum + new_term for old_sum, new_term in zip(carry_acc[layer_idx], layer_grads)))
        return (tuple(new_carry), (jnp.stack(outputs), upstream))
    grad_shapes = ((D, 3 * D), (3 * D,), (D, D), (D,), (D, FF), (FF,), (FF, D), (D,), (D,), (D,), (D,))
    zero_grads = tuple((tuple((jnp.zeros(shape_item, jnp.float32) for shape_item in grad_shapes)) for layer_idx in range(LAYERS)))
    final_acc, (hidden_seq, grad_seq) = lax.scan(one_sequence, zero_grads, (tokens.reshape(seq_count, SEQ, D), segments.reshape(seq_count, SEQ), positions.reshape(seq_count, SEQ), cotangent.reshape(seq_count, SEQ, D)))
    hidden_out = jnp.transpose(hidden_seq, (1, 0, 2, 3)).reshape(LAYERS, seq_count * SEQ, D)
    input_grad = grad_seq.reshape(seq_count * SEQ, D)

    def stacked_grad(member):
        return jnp.stack([final_acc[layer_idx][member] for layer_idx in range(LAYERS)])
    return (hidden_out, input_grad, stacked_grad(0), stacked_grad(1), stacked_grad(2), stacked_grad(3), stacked_grad(4), stacked_grad(5), stacked_grad(6), stacked_grad(3), stacked_grad(7), stacked_grad(8), stacked_grad(9), stacked_grad(10))
```

```python
import functools

import jax
import jax.numpy as jnp
from jax import lax
from jax.experimental import pallas as pl
from jax.experimental.pallas import tpu as pltpu
from jax.sharding import PartitionSpec as P

HEAD = 64
ROT = 16
EPS = 1e-05
F32 = jnp.float32
BF16 = jnp.bfloat16
VMEM = pltpu.VMEM


def up128(n):
    return -(-n // 128) * 128


class Sizes:
    def __init__(self, rows, up_q, qkv_q, out_q, qkvb, upb):
        self.rows, self.up_q, self.qkv_q, self.out_q = rows, up_q, qkv_q, out_q
        self.qkvb, self.upb = qkvb, upb
        self.qb_cols, self.ub_cols = -(-qkvb // rows), -(-upb // rows)
        self.down = up_q
        self.qkv = 2 * up_q
        self.small = self.qkv + qkv_q
        self.n_small = 6 + self.qb_cols + self.ub_cols
        self.out = up128(self.small + self.n_small)
        self.cols = up128(self.out + out_q)
        self.tile = self.small // 128 * 128
        self.tile_end = self.out

    def pack(self, up, down, qkv, small, out):
        lead = up.shape[:-1]
        gap = self.out - self.small - small.shape[-1]
        tail = self.cols - self.out - self.out_q
        parts = [up, down, qkv, small, jnp.zeros(lead + (gap,), BF16), out]
        if tail:
            parts.append(jnp.zeros(lead + (tail,), BF16))
        return jnp.concatenate([p.astype(BF16) for p in parts], axis=-1)


def places(n_outer):
    dp = lax.axis_index("dp")
    x = lax.axis_index("tensor")
    core = lax.rem(dp, 2)
    chip = dp // 2
    inner = lax.rem(chip, 2)
    outer = chip // 2
    return dp, x, core, chip, inner, outer


def dev(chip, core, x):
    return {"dp": chip * 2 + core, "tensor": x}


def greet(partners, outer, n_outer, up, down):
    barrier = pltpu.get_barrier_semaphore()

    def tell(partner):
        pl.semaphore_signal(
            barrier, inc=1, device_id=partner, device_id_type=pl.DeviceIdType.MESH
        )

    for partner in partners:
        tell(partner)
    pl.when(outer < n_outer - 1)(lambda: tell(up))
    pl.when(outer > 0)(lambda: tell(down))
    chained = jnp.minimum(outer, 1) + jnp.minimum(n_outer - 1 - outer, 1)
    pl.semaphore_wait(barrier, len(partners) + chained)


def rcopy(src, dst, send, recv, where):
    return pltpu.make_async_remote_copy(
        src_ref=src,
        dst_ref=dst,
        send_sem=send,
        recv_sem=recv,
        device_id=where,
        device_id_type=pl.DeviceIdType.MESH,
    )


def partner_list(n_outer):
    dp, x, core, chip, inner, outer = places(n_outer)
    sibling = dev(chip, 1 - core, x)
    across = dev(chip, core, 1 - x)
    diagonal = dev(chip, 1 - core, 1 - x)
    inner_peer = dev(outer * 2 + 1 - inner, core, x)
    up = dev((outer + 1) * 2 + inner, core, x)
    down = dev((outer - 1) * 2 + inner, core, x)
    return sibling, across, diagonal, inner_peer, up, down


def gather_kernel(
    n_outer, p_ref, a_ref, w_ref, t_ref, loc_sem, grp_s, grp_r, sib_s, sib_r, ch_s, ch_r, in_s, in_r
):
    dp, x, core, chip, inner, outer = places(n_outer)
    sibling, across, diagonal, inner_peer, up, down = partner_list(n_outer)
    own_w = pltpu.make_async_copy(p_ref.at[core], w_ref.at[chip, core], loc_sem.at[0])
    own_t = pltpu.make_async_copy(a_ref, t_ref.at[core, x], loc_sem.at[1])
    own_w.start()
    own_t.start()
    greet([sibling, across, diagonal, inner_peer], outer, n_outer, up, down)
    sib = rcopy(p_ref.at[1 - core], w_ref.at[chip, core], sib_s, sib_r, sibling)
    sib.start()
    own_w.wait()
    sib.wait_recv()
    last = n_outer - 1

    def chain(way, step):
        block = outer - step if way == 0 else outer + step
        there = (outer < last) & (block >= 0) if way == 0 else (outer > 0) & (block <= last)
        spot = w_ref.at[block * 2 + inner]
        where = up if way == 0 else down
        return there, lambda: rcopy(spot, spot, ch_s.at[way, step], ch_r.at[way, step], where)

    def arrival(way, step):
        block = outer - 1 - step if way == 0 else outer + 1 + step
        there = block >= 0 if way == 0 else block <= last
        spot = w_ref.at[block * 2 + inner]
        return there, lambda: rcopy(spot, spot, ch_s.at[way, step], ch_r.at[way, step], up)

    def forward(way, step, mine):
        block = outer - 1 - step if way == 0 else outer + 1 + step
        there = block >= 0 if way == 0 else block <= last
        spot = w_ref.at[block * 2 + (inner if mine else 1 - inner)]
        return there, lambda: rcopy(spot, spot, in_s.at[way, step], in_r.at[way, step], inner_peer)

    def act(pair, what):
        there, copy = pair
        pl.when(there)(lambda: what(copy()))

    def start(copy):
        copy.start()

    for way in range(2):
        act(chain(way, 0), start)
    own = w_ref.at[chip]
    mine = rcopy(own, own, in_s.at[0, last], in_r.at[0, last], inner_peer)
    mine.start()
    group = []
    for slot, where in enumerate((sibling, across, diagonal)):
        copy = rcopy(a_ref, t_ref.at[core, x], grp_s.at[slot], grp_r.at[slot], where)
        copy.start()
        group.append(copy)
    for step in range(last):
        for way in range(2):
            act(arrival(way, step), lambda copy: copy.wait_recv())
            if step + 1 < last:
                act(chain(way, step + 1), start)
            act(forward(way, step, True), start)
    for copy in group:
        copy.wait_recv()
    mine.wait_recv()
    for step in range(last):
        for way in range(2):
            act(forward(way, step, False), lambda copy: copy.wait_recv())
    own_t.wait()
    sib.wait_send()
    mine.wait_send()
    for copy in group:
        copy.wait_send()
    for step in range(last):
        for way in range(2):
            act(chain(way, step), lambda copy: copy.wait_send())
            act(forward(way, step, True), lambda copy: copy.wait_send())


def scatter_kernel(
    sizes,
    n_outer,
    n2t_ref,
    cott_ref,
    n1t_ref,
    du_ref,
    act_ref,
    dqkv_ref,
    att_ref,
    small_ref,
    h_ref,
    d_ref,
    r_ref,
    hs_ref,
    ds_ref,
    x_ref,
    first_buf,
    b1,
    send_buf,
    cbuf,
    acc,
    hr,
    small_out,
    small_in,
    grp_s,
    grp_r,
    in_s,
    in_r,
    ch_s,
    ch_r,
    sib_s,
    sib_r,
    sm_s,
    sm_r,
):
    dp, x, core, chip, inner, outer = places(n_outer)
    sibling, across, diagonal, inner_peer, up, down = partner_list(n_outer)
    last = n_outer - 1
    rows = sizes.rows
    lo, hi = sizes.tile, sizes.tile_end

    def block(target, put):
        def product(left, right):
            if rows % 16 == 0:
                lhs = left[target].reshape(2 * rows, -1)
                out = jnp.dot(lhs, right[...], preferred_element_type=F32)
                return out.reshape(2, rows, -1)
            return jnp.stack(
                [
                    jnp.dot(left[target, side], right[...], preferred_element_type=F32)
                    for side in range(2)
                ]
            )

        put(0, sizes.down, product(n2t_ref, du_ref))
        put(sizes.down, sizes.qkv, product(cott_ref, act_ref))
        part = product(n1t_ref, dqkv_ref)
        cut = lo - sizes.qkv
        put(sizes.qkv, lo, part[:, :, :cut])
        put(lo, hi, part[:, :, cut:] + small_ref[target])
        end = sizes.out + sizes.out_q
        put(sizes.out, end, product(cott_ref, att_ref))
        if end < sizes.cols:
            put(end, sizes.cols, jnp.zeros((2, rows, sizes.cols - end), F32))

    def to_acc(start, stop, value):
        acc[:, :, start:stop] = value

    greet([sibling, across, diagonal, inner_peer], outer, n_outer, up, down)
    group = []
    spots = ((sibling, 1 - core, x), (across, core, 1 - x), (diagonal, 1 - core, 1 - x))
    for slot, (where, to_core, to_x) in enumerate(spots):
        for kind, part in enumerate((h_ref, d_ref)):
            copy = rcopy(
                part.at[to_core, to_x],
                hr.at[kind, slot],
                grp_s.at[kind, slot],
                grp_r.at[kind, slot],
                where,
            )
            copy.start()
            group.append(copy)

    def in_order(what):
        @pl.loop(0, last)
        def _(tick):
            back = last - tick
            pl.when(outer <= tick)(lambda: what(0, outer + back))
            pl.when(outer >= back)(lambda: what(1, outer - back))

    def exchange(target):
        return rcopy(
            first_buf.at[target], b1.at[target], in_s.at[target], in_r.at[target], inner_peer
        )

    def passing(way, target):
        return rcopy(
            send_buf.at[target],
            cbuf.at[way, target],
            ch_s.at[way, target],
            ch_r.at[way, target],
            up if way == 0 else down,
        )

    def send_first(target):
        def put(start, stop, value):
            first_buf[target, :, :, start:stop] = value.astype(BF16)

        block(target * 2 + 1 - inner, put)
        exchange(target).start()

    def send_second(way, target):
        block(target * 2 + inner, to_acc)
        exchange(target).wait_recv()
        acc[...] += b1[target].astype(F32)
        started = outer > 0 if way == 0 else outer < last

        @pl.when(started)
        def _():
            passing(way, target).wait_recv()
            acc[...] += cbuf[way, target].astype(F32)

        send_buf[target] = acc[...].astype(BF16)
        passing(way, target).start()

    in_order(lambda way, target: send_first(target))
    send_first(outer)
    in_order(send_second)
    for copy in group:
        copy.wait_recv()
    for kind, (part, out) in enumerate(((h_ref, hs_ref), (d_ref, ds_ref))):
        out[...] = (
            part[core, x].astype(F32)
            + hr[kind, 0].astype(F32)
            + hr[kind, 1].astype(F32)
            + hr[kind, 2].astype(F32)
        )
    block(chip, to_acc)
    exchange(outer).wait_recv()
    acc[...] += b1[outer].astype(F32)
    for way in range(2):

        @pl.when(outer > 0 if way == 0 else outer < last)
        def _():
            passing(way, outer).wait_recv()
            acc[...] += cbuf[way, outer].astype(F32)

    sib = rcopy(acc.at[1 - core], r_ref.at[core], sib_s, sib_r, sibling)
    sib.start()
    r_ref[core] = acc[core]
    sib.wait_recv()
    small_out[...] = r_ref[0, :, lo:hi] + r_ref[1, :, lo:hi]
    small = rcopy(small_out, small_in, sm_s, sm_r, across)
    small.start()
    small.wait_recv()
    x_ref[0] = small_out[...]
    x_ref[1] = small_out[...] + small_in[...]
    sib.wait_send()
    small.wait_send()
    for copy in group:
        copy.wait_send()
    exchange(outer).wait_send()

    def sent(way, target):
        exchange(target).wait_send()
        passing(way, target).wait_send()

    in_order(sent)


def gather(sizes, n_outer, packed, rows):
    dma = pltpu.SemaphoreType.DMA
    full = pl.BlockSpec(memory_space=VMEM)
    return pl.pallas_call(
        functools.partial(gather_kernel, n_outer),
        out_shape=(
            jax.ShapeDtypeStruct((2 * n_outer, 2) + packed.shape[1:], BF16),
            jax.ShapeDtypeStruct((2, 2) + rows.shape, BF16),
        ),
        in_specs=[full, full],
        out_specs=(full, full),
        scratch_shapes=[
            dma((2,)),
            dma((3,)),
            dma((3,)),
            dma,
            dma,
            dma((2, n_outer)),
            dma((2, n_outer)),
            dma((2, n_outer)),
            dma((2, n_outer)),
        ],
        compiler_params=pltpu.CompilerParams(
            collective_id=0, has_side_effects=True, vmem_limit_bytes=60 * 2**20
        ),
        name="gather",
    )(packed, rows)


def scatter(sizes, n_outer, operands, mixed, back):
    dma = pltpu.SemaphoreType.DMA
    full = pl.BlockSpec(memory_space=VMEM)
    block = (2, sizes.rows, sizes.cols)
    width = sizes.tile_end - sizes.tile
    return pl.pallas_call(
        functools.partial(scatter_kernel, sizes, n_outer),
        out_shape=(
            jax.ShapeDtypeStruct(block, F32),
            jax.ShapeDtypeStruct(mixed.shape[2:], F32),
            jax.ShapeDtypeStruct(mixed.shape[2:], F32),
            jax.ShapeDtypeStruct((2, sizes.rows, width), F32),
        ),
        in_specs=[full] * (len(operands) + 2),
        out_specs=(full, full, full, full),
        scratch_shapes=[
            VMEM((n_outer,) + block, BF16),
            VMEM((n_outer,) + block, BF16),
            VMEM((n_outer,) + block, BF16),
            VMEM((2, n_outer) + block, BF16),
            VMEM(block, F32),
            VMEM((2, 3) + mixed.shape[2:], BF16),
            VMEM((sizes.rows, width), F32),
            VMEM((sizes.rows, width), F32),
            dma((2, 3)),
            dma((2, 3)),
            dma((n_outer,)),
            dma((n_outer,)),
            dma((2, n_outer)),
            dma((2, n_outer)),
            dma,
            dma,
            dma,
            dma,
        ],
        compiler_params=pltpu.CompilerParams(
            collective_id=1, has_side_effects=True, vmem_limit_bytes=60 * 2**20
        ),
        name="scatter",
    )(*operands, mixed, back)


def rotary_tables(pos_ids):
    half_rot = ROT // 2
    freq_index = jnp.arange(half_rot, dtype=F32)
    inverse = jnp.power(F32(10000.0), -2.0 * freq_index / ROT)
    angles = pos_ids[..., None] * inverse
    cos_tab = jnp.concatenate([jnp.cos(angles), jnp.cos(angles)], axis=-1)
    sin_tab = jnp.concatenate([jnp.sin(angles), jnp.sin(angles)], axis=-1)
    return (cos_tab[:, None], sin_tab[:, None])


def rotate(values, cos_tab, sin_tab):
    half_rot = ROT // 2
    rotary = values[..., :ROT]
    turned = jnp.concatenate([-rotary[..., half_rot:], rotary[..., :half_rot]], axis=-1)
    return jnp.concatenate([rotary * cos_tab + turned * sin_tab, values[..., ROT:]], axis=-1)


def unrotate(grad_vals, cos_tab, sin_tab):
    half_rot = ROT // 2
    rotary = grad_vals[..., :ROT]
    scaled = rotary * sin_tab
    back_part = jnp.concatenate([scaled[..., half_rot:], -scaled[..., :half_rot]], axis=-1)
    return jnp.concatenate([rotary * cos_tab + back_part, grad_vals[..., ROT:]], axis=-1)


def unit_rows(values):
    centre = values - jnp.mean(values, axis=-1, keepdims=True)
    inv_std = lax.rsqrt(jnp.mean(centre * centre, axis=-1, keepdims=True) + EPS)
    return centre * inv_std, inv_std


def dot(a, b, ca, cb):
    return lax.dot_general(a, b, (((ca,), (cb,)), ((), ())), preferred_element_type=F32)


def fold(vector, count, rows, cols):
    per = vector.shape[0] // count
    padded = jnp.pad(vector.reshape(count, per), ((0, 0), (0, rows * cols - per)))
    return padded.reshape(count, rows, cols)


class Shape:
    def __init__(self, n, rows, own, width, seq, qkv, out, up, qkvb, upb):
        self.n, self.rows, self.own, self.width, self.seq = n, rows, own, width, seq
        self.qkv, self.out, self.up, self.qkvb, self.upb = qkv, out, up, qkvb, upb
        self.heads = out // HEAD
        self.att = qkv + out
        self.tokens = 4 * own
        self.cols = (self.att + 128, up, up)
        self.gcols = (self.att, up, up)

    def fits(self):
        aligned = [self.own, self.width, self.seq, self.att, self.up]
        return (
            self.rows % 16 == 0
            and all(size % 128 == 0 for size in aligned)
            and self.own * 2 == self.seq
            and self.att <= self.up
            and self.width <= self.up
            and max(self.rows, self.qkvb, self.upb) <= 128
            and self.n >= 2
            and (self.n * 4) * self.rows == self.width
        )


def fused_kernel(
    S,
    tok_ref,
    cot_ref,
    pos_ref,
    qkv_ref,
    out_ref,
    up_ref,
    down_ref,
    g1_ref,
    b1_ref,
    g2_ref,
    b2_ref,
    ob_ref,
    db_ref,
    qb_ref,
    ub_ref,
    red_a,
    red_u,
    red_d,
    hs_ref,
    bs_ref,
    small_ref,
    prm_ref,
    pk_a,
    pk_u,
    pk_d,
    w_a,
    w_u,
    w_d,
    tbuf,
    cbuf,
    pbuf,
    smrow,
    bias,
    unit,
    n1,
    n2,
    mask,
    rot_c,
    rot_s,
    proj,
    qh,
    kh,
    vh,
    doh,
    att,
    dqk,
    dqkv,
    outw,
    act,
    slope,
    du,
    grad_a,
    grad_u,
    grad_d,
    sb_a,
    sb_u,
    sb_d,
    rb_a,
    rb_u,
    rb_d,
    cs_a,
    cs_u,
    cs_d,
    ci_a,
    ci_u,
    ci_d,
    ys_a,
    ys_u,
    ys_d,
    yr_a,
    yr_u,
    yr_d,
    mine,
    mix_s,
    mix_r,
    sm_s,
    sm_r,
    gy_s,
    gy_r,
    gc_s,
    gc_r,
    gf_s,
    gf_r,
    tk_s,
    tk_r,
    ps_s,
    ps_r,
    ss_s,
    ss_r,
    sc_s,
    sc_r,
    sy_s,
    sy_r,
    mx_s,
    mx_r,
    st_s,
    st_r,
):
    n, rows, own, width = S.n, S.rows, S.own, S.width
    last = n - 1
    dp = lax.axis_index("dp")
    x = lax.axis_index("tensor")
    core = lax.rem(dp, 2)
    y = lax.rem(dp // 2, 2)
    z = dp // 4

    def at(zz, yy, cc, xx):
        return {"dp": zz * 4 + yy * 2 + cc, "tensor": xx}

    sibling = at(z, y, 1 - core, x)
    across = at(z, y, core, 1 - x)
    ypeer = at(z, 1 - y, core, x)
    diagonal = at(z, 1 - y, core, 1 - x)
    up, down = at(z + 1, y, core, x), at(z - 1, y, core, x)
    pk, w = (pk_a, pk_u, pk_d), (w_a, w_u, w_d)
    grad = (grad_a, grad_u, grad_d)
    sb, rb = (sb_a, sb_u, sb_d), (rb_a, rb_u, rb_d)
    cs, ci = (cs_a, cs_u, cs_d), (ci_a, ci_u, ci_d)
    ysb, yrb = (ys_a, ys_u, ys_d), (yr_a, yr_u, yr_d)
    red = (red_a, red_u, red_d)
    sends = []

    def begin(copy):
        copy.start()
        sends.append(copy)
        return copy

    def iota(shape, axis):
        return lax.broadcasted_iota(jnp.int32, shape, axis)

    eye = jnp.where(iota((rows, rows), 0) == iota((rows, rows), 1), 1.0, 0.0).astype(BF16)

    def flip(block):
        return dot(eye, block, 1, 1).astype(BF16)

    smrow[...] = jnp.zeros_like(smrow)
    for row, part in enumerate((g1_ref, b1_ref, g2_ref, b2_ref, ob_ref, db_ref, qb_ref, ub_ref)):
        smrow[row : row + 1, : part.shape[1]] = part[...].astype(F32)
    for q in range(2):
        pk_a[q, :, : S.qkv] = qkv_ref[:, q * S.qkv : (q + 1) * S.qkv]
        pk_a[q, :, S.qkv : S.att] = flip(out_ref[q * S.out : (q + 1) * S.out, :])
        pk_a[q, :, S.att :] = smrow[...].astype(BF16)
    row_pos = pos_ref[...].astype(F32)
    pbuf[y] = jnp.broadcast_to(row_pos, pbuf.shape[1:])

    barrier = pltpu.get_barrier_semaphore()

    def tell(partner):
        pl.semaphore_signal(
            barrier, inc=1, device_id=partner, device_id_type=pl.DeviceIdType.MESH
        )

    for partner in (sibling, across, ypeer, diagonal):
        tell(partner)
    pl.when(z < last)(lambda: tell(up))
    pl.when(z > 0)(lambda: tell(down))
    pl.semaphore_wait(barrier, 4 + jnp.minimum(z, 1) + jnp.minimum(last - z, 1))

    def y_copy(k):
        return rcopy(pk[k].at[1 - y], w[k].at[z, y, core], gy_s.at[k], gy_r.at[k], ypeer)

    def chain_copy(k, way, step):
        block = z - step if way == 0 else z + step
        there = (z < last) & (block >= 0) if way == 0 else (z > 0) & (block <= last)
        spot = w[k].at[block, :, core]
        where = up if way == 0 else down
        return there, lambda: rcopy(spot, spot, gc_s.at[k, way, step], gc_r.at[k, way, step], where)

    def fan_copy(k, block):
        spot = w[k].at[block, :, core]
        return rcopy(spot, spot, gf_s.at[k, block], gf_r.at[k, block], sibling)

    def arrived(way, step):
        block = z - 1 - step if way == 0 else z + 1 + step
        return block, (block >= 0 if way == 0 else block <= last)

    def own_part(k):
        w[k][z, y, core] = pk[k][y]

    def start_own(k):
        y_copy(k).wait_recv()
        for way in range(2):
            there, copy = chain_copy(k, way, 0)
            pl.when(there)(lambda: copy().start())
        fan_copy(k, z).start()

    def relay(k, step):
        for way in range(2):
            block, there = arrived(way, step)

            @pl.when(there)
            def _():
                spot = w[k].at[block, :, core]
                rcopy(spot, spot, gc_s.at[k, way, step], gc_r.at[k, way, step], up).wait_recv()

            if step + 1 < last:
                more, copy = chain_copy(k, way, step + 1)
                pl.when(more)(lambda: copy().start())
            pl.when(there)(lambda: fan_copy(k, block).start())

    def gathered(k):
        for block in range(n):
            spot = w[k].at[block, :, 1 - core]
            rcopy(spot, spot, gf_s.at[k, block], gf_r.at[k, block], sibling).wait_recv()

    peers = ((across, y, 1 - x), (ypeer, 1 - y, x), (diagonal, 1 - y, 1 - x))

    begin(y_copy(0))
    pos_copy = begin(rcopy(pbuf.at[y], pbuf.at[y], ps_s, ps_r, ypeer))
    group = []
    for kind, (src, dst) in enumerate(((tok_ref, tbuf), (cot_ref, cbuf))):
        for slot, (where, _, _) in enumerate(peers):
            group.append(
                begin(rcopy(src, dst.at[y, x], tk_s.at[kind, slot], tk_r.at[kind, slot], where))
            )
        if kind == 0:
            own_part(0)
            for q in range(2):
                pk_u[q] = up_ref[:, q * S.up : (q + 1) * S.up]
            begin(y_copy(1))
            own_part(1)
    start_own(0)
    for q in range(2):
        pk_d[q] = flip(down_ref[q * S.up : (q + 1) * S.up, :])
    begin(y_copy(2))
    own_part(2)
    tbuf[y, x] = tok_ref[...]
    cbuf[y, x] = cot_ref[...]

    lane = iota((own, 128), 1)
    spin = lax.rem(lane, HEAD)

    def tables():
        pos_copy.wait_recv()
        freq = jnp.zeros((1, 128), F32)
        which = lax.rem(iota((1, 128), 1), ROT // 2)
        for i in range(ROT // 2):
            freq = jnp.where(which == i, 10000.0 ** (-2.0 * i / ROT), freq)
        query = iota((S.seq, S.seq), 0).astype(F32)
        key = iota((S.seq, S.seq), 1).astype(F32)
        spin_s = lax.rem(iota((S.seq, 128), 1), HEAD)
        for s in range(2):
            line = jnp.where(query == key, pbuf[s, 0:1, :], 0.0)
            column = jnp.sum(line, axis=1, keepdims=True)
            seen = (key <= query) & (key >= query - column)
            mask[s] = jnp.where(seen, 0.0, -jnp.inf)
            angles = column * freq
            sines = jnp.sin(angles)
            rot_c[s * S.seq : (s + 1) * S.seq] = jnp.where(spin_s < ROT, jnp.cos(angles), 1.0)
            rot_s[s * S.seq : (s + 1) * S.seq] = jnp.where(
                spin_s < ROT // 2, -sines, jnp.where(spin_s < ROT, sines, 0.0)
            )

    def blocks(body):
        pl.loop(0, 4)(lambda g: body(g, pl.ds(pl.multiple_of(g * own, own), own)))

    def units():
        def body(g, part):
            unit[part] = unit_rows(tbuf[g // 2, lax.rem(g, 2)].astype(F32))[0]

        blocks(body)

    def params():
        total = jnp.zeros((8, S.up), F32)
        for j in range(4 * n):
            piece = w_a[j // 4, (j // 2) % 2, j % 2, 0:16, S.att :].astype(F32)[0:8]
            wide = jnp.concatenate([piece, jnp.zeros((8, S.up - 128), F32)], axis=1)
            total = total + (pltpu.roll(wide, j * rows, 1) if j else wide)
        prm_ref[...] = total[:, :width]
        q_total = jnp.zeros((8, S.up), F32)
        u_total = jnp.zeros((8, S.up), F32)
        for j in range(2 * n):
            there = y * (n // 2) + j // 4
            piece = w_a[there, (j // 2) % 2, j % 2, 0:16, S.att :].astype(F32)[0:8]
            wide = jnp.concatenate([piece, jnp.zeros((8, S.up - 128), F32)], axis=1)
            q_total = q_total + (pltpu.roll(wide, j * S.qkvb, 1) if j else wide)
            u_total = u_total + (pltpu.roll(wide, j * S.upb, 1) if j else wide)
        bias[0:8] = q_total
        bias[8:16] = u_total

    def flat(ref, start, stop):
        return ref[:, :, :, :, start:stop].reshape(4 * n * rows, stop - start)

    def norms():
        def body(g, part):
            value = unit[part]
            n1[part] = (value * prm_ref[0:1] + prm_ref[1:2]).astype(BF16)
            n2[part] = (value * prm_ref[2:3] + prm_ref[3:4]).astype(BF16)

        blocks(body)

    def turn(values, part, sign):
        ahead, behind = pltpu.roll(values, 128 - ROT // 2, 1), pltpu.roll(values, ROT // 2, 1)
        other = jnp.where(spin < ROT // 2, ahead, behind) * rot_s[part]
        return values * rot_c[part] + (other if sign > 0 else -other)

    def project():
        outw[...] = flat(w_a, S.qkv, S.att)

        def body(g, part):
            proj[...] = dot(n1[part], flat(w_a, 0, S.qkv), 1, 0) + bias[6:7, : S.qkv]
            for h in range(S.heads):
                base = h * 3 * HEAD
                pair = turn(proj[:, base : base + 2 * HEAD], part, 1).astype(BF16)
                qh[h, part] = pair[:, :HEAD]
                kh[h, part] = pair[:, HEAD:]
                vh[h, part] = proj[:, base + 2 * HEAD : base + 3 * HEAD].astype(BF16)
            grads = dot(cbuf[g // 2, lax.rem(g, 2)], outw[...], 1, 0).astype(BF16)
            for h in range(S.heads):
                doh[h, part] = grads[:, h * HEAD : (h + 1) * HEAD]

        blocks(body)

    scale = HEAD ** (-0.5)

    def attend(s, h):
        part = slice(s * S.seq, (s + 1) * S.seq)
        q, k, v, dout = qh[h, part], kh[h, part], vh[h, part], doh[h, part]
        scores = dot(q, k, 1, 1) * scale + mask[s]
        raised = jnp.exp(scores - jnp.max(scores, axis=-1, keepdims=True))
        weights = raised * (1.0 / jnp.sum(raised, axis=-1, keepdims=True))
        weights_bf = weights.astype(BF16)
        got = dot(weights_bf, v, 1, 0).astype(BF16)
        att[part, h * HEAD : (h + 1) * HEAD] = got
        delta = jnp.sum(got.astype(F32) * dout.astype(F32), axis=-1, keepdims=True)
        d_score = (weights * (dot(dout, v, 1, 1) - delta) * scale).astype(BF16)
        dqk[part, :HEAD] = dot(d_score, k, 1, 0)
        dqk[part, HEAD:] = dot(d_score, q, 0, 0)
        base = h * 3 * HEAD
        dqkv[part, base + 2 * HEAD : base + 3 * HEAD] = dot(weights_bf, dout, 0, 0).astype(BF16)
        for half in range(2):
            piece = slice(s * S.seq + half * own, s * S.seq + (half + 1) * own)
            dqkv[piece, base : base + 2 * HEAD] = turn(dqk[piece], piece, -1).astype(BF16)

    def by_columns(left, right, target, start):
        size = right.shape[1]

        @pl.loop(0, width // 128)
        def _(i):
            spot = pl.ds(pl.multiple_of(i * 128, 128), 128)
            if len(left.shape) == 2:
                lhs = left[:, spot]
            else:
                lhs = left[:, :, :, spot].reshape(S.tokens, 128)
            target[spot, start : start + size] = dot(lhs, right[...], 0, 0)

    def grads_a():
        by_columns(n1, dqkv, grad_a, 0)
        by_columns(cbuf, att, grad_a, S.qkv)

    def hidden():
        def body(g, part):
            pre = dot(n2[part], flat(w_u, 0, S.up), 1, 0) + bias[15:16, : S.up]
            cumul = 0.5 * (1.0 + lax.erf(pre * 0.7071067811865476))
            act[part] = (pre * cumul).astype(BF16)
            slope[part] = cumul + pre * jnp.exp(-0.5 * pre * pre) * 0.3989422804014327

        blocks(body)

    def back_hidden():
        def body(g, part):
            d_act = dot(cbuf[g // 2, lax.rem(g, 2)], flat(w_d, 0, S.up), 1, 0)
            du[part] = (d_act * slope[part]).astype(BF16)

        blocks(body)

    def col_sum(values):
        return jnp.sum(values, axis=0, keepdims=True)

    def outputs():
        sm_s[0] = jnp.zeros(sm_s.shape[1:], F32)
        sm_s[0, 4:5, :width] = col_sum(cot_ref[...].astype(F32))

        def body(g, part):
            mixed = dot(att[part], outw[...], 1, 1) + dot(act[part], flat(w_d, 0, S.up), 1, 1)
            mine[0, g] = mixed
            dn2 = dot(du[part], flat(w_u, 0, S.up), 1, 1)
            dn1 = dot(dqkv[part], flat(w_a, 0, S.qkv), 1, 1)
            mine[1, g] = dn1 * prm_ref[0:1] + dn2 * prm_ref[2:3]
            mix_s[0, g] = mine[0, g].astype(BF16)
            mix_s[1, g] = mine[1, g].astype(BF16)
            value = unit[part]
            sm_s[0, 0:1, :width] += col_sum(dn1 * value)
            sm_s[0, 1:2, :width] += col_sum(dn1)
            sm_s[0, 2:3, :width] += col_sum(dn2 * value)
            sm_s[0, 3:4, :width] += col_sum(dn2)
            first = (y == 0).astype(F32)
            qsum, usum = col_sum(dqkv[part].astype(F32)), col_sum(du[part].astype(F32))
            sm_s[0, 5:6, : S.qkv] += qsum * first
            sm_s[0, 6:7, : S.qkv] += qsum * (1.0 - first)
            sm_s[0, 7:8, : S.up] += usum * first
            sm_s[0, 8:9, : S.up] += usum * (1.0 - first)

        blocks(body)

    def sib_copy(k):
        return rcopy(sb[k], rb[k], ss_s.at[k], ss_r.at[k], sibling)

    def place(zz, yy, cc):
        return pl.ds(pl.multiple_of(((zz * 2 + yy) * 2 + cc) * rows, 16), rows)

    def to_sibling(k):
        @pl.loop(0, n)
        def _(zz):
            for yy in range(2):
                sb[k][zz, yy] = grad[k][place(zz, yy, 1 - core)].astype(BF16)

        sib_copy(k).start()

    def passing(k, way, target):
        return rcopy(
            cs[k].at[target],
            ci[k].at[way, target],
            sc_s.at[k, way, target],
            sc_r.at[k, way, target],
            up if way == 0 else down,
        )

    def summed(k, target, yy):
        return grad[k][place(target, yy, core)] + rb[k][target, yy].astype(F32)

    def tick(k, step):
        back = last - step
        if step == 0:
            sib_copy(k).wait_recv()

        def pass_on(way, target, more):
            @pl.when(more)
            def _():
                passing(k, way, target).wait_recv()
                for yy in range(2):
                    total = summed(k, target, yy) + ci[k][way, target, yy].astype(F32)
                    cs[k][target, yy] = total.astype(BF16)

            @pl.when(jnp.logical_not(more))
            def _():
                for yy in range(2):
                    cs[k][target, yy] = summed(k, target, yy).astype(BF16)

            passing(k, way, target).start()

        pl.when(z <= step)(lambda: pass_on(0, z + back, z > 0))
        pl.when(z >= back)(lambda: pass_on(1, z - back, z < last))

    def last_y(k):
        return rcopy(ysb[k], yrb[k], sy_s.at[k], sy_r.at[k], ypeer)

    def final(k):
        pl.when(z > 0)(lambda: passing(k, 0, z).wait_recv())
        pl.when(z < last)(lambda: passing(k, 1, z).wait_recv())

        def total(yy):
            value = summed(k, z, yy)
            low = jnp.where(z > 0, ci[k][0, z, yy].astype(F32), 0.0)
            high = jnp.where(z < last, ci[k][1, z, yy].astype(F32), 0.0)
            return value + low + high

        ysb[k][...] = total(1 - y).astype(BF16)
        last_y(k).start()
        red[k][y] = total(y)

    def final_recv(k):
        last_y(k).wait_recv()
        red[k][1 - y] = yrb[k][...].astype(F32)

    def mix_send():
        for kind in range(2):
            for slot, (where, to_y, to_x) in enumerate(peers):
                begin(
                    rcopy(
                        mix_s.at[kind, to_y * 2 + to_x],
                        mix_r.at[kind, slot],
                        mx_s.at[kind, slot],
                        mx_r.at[kind, slot],
                        where,
                    )
                )

    def mix_recv():
        for kind, target in enumerate((hs_ref, bs_ref)):
            for slot, (where, _, _) in enumerate(peers):
                rcopy(
                    mix_s.at[kind, 0],
                    mix_r.at[kind, slot],
                    mx_s.at[kind, slot],
                    mx_r.at[kind, slot],
                    where,
                ).wait_recv()
            target[...] = (
                mine[kind, y * 2 + x]
                + mix_r[kind, 0].astype(F32)
                + mix_r[kind, 1].astype(F32)
                + mix_r[kind, 2].astype(F32)
            )

    def small_copy(i, where):
        return rcopy(sm_s.at[i], sm_r.at[i], st_s.at[i], st_r.at[i], where)

    def small_pair():
        small_copy(0, sibling).wait_recv()
        sm_s[5] = sm_s[0] + sm_r[0]

    def small_chain():
        for way, where in ((0, up), (1, down)):
            more = z > 0 if way == 0 else z < last
            onward = z < last if way == 0 else z > 0

            @pl.when(more)
            def _():
                small_copy(1 + way, where).wait_recv()

            @pl.when(onward)
            def _():
                sm_s[1 + way] = sm_s[5] + jnp.where(more, sm_r[1 + way], 0.0)
                small_copy(1 + way, where).start()

        low = jnp.where(z > 0, sm_r[1], 0.0)
        high = jnp.where(z < last, sm_r[2], 0.0)
        sm_s[3] = sm_s[5] + low + high
        begin(small_copy(3, ypeer))

    def small_y():
        small_copy(3, ypeer).wait_recv()
        sm_s[4] = sm_s[3] + sm_r[3]
        begin(small_copy(4, across))

    def small_x():
        small_copy(4, across).wait_recv()
        small_ref[0] = sm_s[4]
        small_ref[1] = sm_s[4] + sm_r[4]

    pending = []
    for t in range(last + 2):
        for k in range(3):
            if 0 <= t - k < last:
                pending.append((k, functools.partial(relay, k, t - k)))
                if t - k == 0 and k < 2:
                    pending.append((k + 1, functools.partial(start_own, k + 1)))

    def advance(count):
        for _ in range(count):
            if pending:
                pending.pop(0)[1]()

    def drain(k):
        while any(item[0] == k for item in pending):
            advance(1)

    tables()
    for slot in range(3):
        group[slot].wait_recv()
    advance(1)
    units()
    drain(0)
    gathered(0)
    params()
    norms()
    advance(1)
    for slot in range(3):
        group[3 + slot].wait_recv()
    project()
    advance(1)
    for s in range(2):
        for h in range(S.heads):
            attend(s, h)
            advance(1)
    grads_a()
    to_sibling(0)
    drain(1)
    gathered(1)
    tick(0, 0)
    hidden()
    advance(1)
    if last > 1:
        tick(0, 1)
    by_columns(cbuf, act, grad_d, 0)
    to_sibling(2)
    drain(2)
    gathered(2)
    for step in range(2, last):
        tick(0, step)
    tick(2, 0)
    back_hidden()
    by_columns(n2, du, grad_u, 0)
    to_sibling(1)
    if last > 1:
        tick(2, 1)
    outputs()
    mix_send()
    begin(small_copy(0, sibling))
    tick(1, 0)
    for step in range(2, last):
        tick(2, step)
    if last > 1:
        tick(1, 1)
    final(0)
    small_pair()
    small_chain()
    for step in range(2, last):
        tick(1, step)
    final(2)
    small_y()
    mix_recv()
    final_recv(0)
    final_recv(2)
    small_x()
    final(1)
    final_recv(1)

    for copy in sends:
        copy.wait_send()
    for k in range(3):
        for step in range(last):
            for way in range(2):
                there, copy = chain_copy(k, way, step)
                pl.when(there)(lambda: copy().wait_send())
        for block in range(n):
            fan_copy(k, block).wait_send()
        sib_copy(k).wait_send()
        last_y(k).wait_send()
        for step in range(last):
            back = last - step
            pl.when(z <= step)(lambda: passing(k, 0, z + back).wait_send())
            pl.when(z >= back)(lambda: passing(k, 1, z - back).wait_send())
    pl.when(z < last)(lambda: small_copy(1, up).wait_send())
    pl.when(z > 0)(lambda: small_copy(2, down).wait_send())


def fused(S, operands):
    dma = pltpu.SemaphoreType.DMA
    full = pl.BlockSpec(memory_space=VMEM)
    n, rows, own, width, T = S.n, S.rows, S.own, S.width, S.tokens
    shape = jax.ShapeDtypeStruct
    pieces = [VMEM((2, rows, c), BF16) for c in S.cols]
    weights = [VMEM((n, 2, 2, rows, c), BF16) for c in S.cols]
    grads = [VMEM((width, c), F32) for c in S.gcols]
    parts = [VMEM((n, 2, rows, c), BF16) for c in S.gcols]
    ways = [VMEM((2, n, 2, rows, c), BF16) for c in S.gcols]
    lines = [VMEM((rows, c), BF16) for c in S.gcols]
    return pl.pallas_call(
        functools.partial(fused_kernel, S),
        out_shape=tuple(shape((2, rows, c), F32) for c in S.gcols)
        + (
            shape((own, width), F32),
            shape((own, width), F32),
            shape((2, 16, S.up), F32),
            shape((8, width), F32),
        ),
        in_specs=[full] * len(operands),
        out_specs=(full,) * 7,
        scratch_shapes=pieces
        + weights
        + [
            VMEM((2, 2, own, width), BF16),
            VMEM((2, 2, own, width), BF16),
            VMEM((2, 8, S.seq), F32),
            VMEM((rows, 128), F32),
            VMEM((16, S.up), F32),
            VMEM((T, width), F32),
            VMEM((T, width), BF16),
            VMEM((T, width), BF16),
            VMEM((2, S.seq, S.seq), F32),
            VMEM((T, 128), F32),
            VMEM((T, 128), F32),
            VMEM((own, S.qkv), F32),
            VMEM((S.heads, T, HEAD), BF16),
            VMEM((S.heads, T, HEAD), BF16),
            VMEM((S.heads, T, HEAD), BF16),
            VMEM((S.heads, T, HEAD), BF16),
            VMEM((T, S.out), BF16),
            VMEM((T, 128), F32),
            VMEM((T, S.qkv), BF16),
            VMEM((width, S.out), BF16),
            VMEM((T, S.up), BF16),
            VMEM((T, S.up), F32),
            VMEM((T, S.up), BF16),
        ]
        + grads
        + parts
        + parts
        + parts
        + ways
        + lines
        + lines
        + [
            VMEM((2, 4, own, width), F32),
            VMEM((2, 4, own, width), BF16),
            VMEM((2, 3, own, width), BF16),
            VMEM((6, 16, S.up), F32),
            VMEM((5, 16, S.up), F32),
            dma((3,)),
            dma((3,)),
            dma((3, 2, n)),
            dma((3, 2, n)),
            dma((3, n)),
            dma((3, n)),
            dma((2, 3)),
            dma((2, 3)),
            dma,
            dma,
            dma((3,)),
            dma((3,)),
            dma((3, 2, n)),
            dma((3, 2, n)),
            dma((3,)),
            dma((3,)),
            dma((2, 3)),
            dma((2, 3)),
            dma((5,)),
            dma((5,)),
        ],
        compiler_params=pltpu.CompilerParams(
            collective_id=2, has_side_effects=True, vmem_limit_bytes=56 * 2**20
        ),
        name="fused",
    )(*operands)


def finish_kernel(
    S,
    red_a,
    red_u,
    red_d,
    hs_ref,
    bs_ref,
    small_ref,
    prm_ref,
    tok_ref,
    cot_ref,
    hid_out,
    inp_out,
    qkv_out,
    qkvb_out,
    outw_out,
    g_out,
    up_out,
    upb_out,
    down_out,
    n1g_out,
    n1b_out,
    n2g_out,
    n2b_out,
):
    dp = lax.axis_index("dp")
    rows, width = S.rows, S.width
    for q in range(2):
        qkv_out[:, q * S.qkv : (q + 1) * S.qkv] = red_a[q, :, : S.qkv]
        up_out[:, q * S.up : (q + 1) * S.up] = red_u[q]
        outw_out[q * S.out : (q + 1) * S.out, :] = red_a[q, :, S.qkv : S.att].T
        down_out[q * S.up : (q + 1) * S.up, :] = red_d[q].T
    values = tok_ref[...].astype(F32)
    unit, inv_std = unit_rows(values)
    hid_out[...] = (values + hs_ref[...] + prm_ref[4:5] + prm_ref[5:6]).astype(BF16)
    total = bs_ref[...]
    mean_term = jnp.mean(total, axis=-1, keepdims=True)
    proj_term = jnp.mean(total * unit, axis=-1, keepdims=True)
    inp_out[...] = cot_ref[...].astype(F32) + inv_std * (total - mean_term - unit * proj_term)

    def shift(block, by):
        return pltpu.roll(block, lax.rem(S.up - by, S.up), 1)

    low = shift(small_ref[1, 0:8], dp * rows)
    for row, out in enumerate((n1g_out, n1b_out, n2g_out, n2b_out, g_out)):
        out[...] = low[row : row + 1, :rows]
    half = 2 * S.n
    first = dp < half
    place = lax.rem(dp, half)
    own_a, own_b = small_ref[0, 0:8], small_ref[0, 8:16]
    qkvb = jnp.where(first, own_a[5:6], own_a[6:7])
    upb = jnp.where(first, own_a[7:8], own_b[0:1])
    both = jnp.broadcast_to(qkvb, (8, S.up)), jnp.broadcast_to(upb, (8, S.up))
    qkvb_out[...] = shift(both[0], place * S.qkvb)[0:1, : S.qkvb]
    upb_out[...] = shift(both[1], place * S.upb)[0:1, : S.upb]


def finish(S, operands):
    shape = jax.ShapeDtypeStruct
    row = shape((1, S.rows), F32)
    return pl.pallas_call(
        functools.partial(finish_kernel, S),
        out_shape=(
            shape((S.own, S.width), BF16),
            shape((S.own, S.width), F32),
            shape((S.rows, 2 * S.qkv), F32),
            shape((1, S.qkvb), F32),
            shape((2 * S.out, S.rows), F32),
            row,
            shape((S.rows, 2 * S.up), F32),
            shape((1, S.upb), F32),
            shape((2 * S.up, S.rows), F32),
            row,
            row,
            row,
            row,
        ),
        compiler_params=pltpu.CompilerParams(vmem_limit_bytes=40 * 2**20),
        name="finish",
    )(*operands)


def on_plane(S, args):
    (tokens, segments, positions, cotangent, qkv_weight, qkv_bias, out_weight, out_bias) = args[:8]
    (up_weight, up_bias, down_weight, down_bias, g1, b1, g2, b2) = args[8:]
    made = fused(
        S,
        (
            tokens,
            cotangent,
            positions.reshape(1, -1),
            qkv_weight[0],
            out_weight[0],
            up_weight[0],
            down_weight[0],
            g1,
            b1,
            g2,
            b2,
            out_bias,
            down_bias,
            qkv_bias,
            up_bias,
        ),
    )
    outs = finish(S, tuple(made) + (tokens, cotangent))
    hid, inp, qkv, qkvb, outw, gsum, upw, upb, downw, n1g, n1b, n2g, n2b = outs
    return (
        hid[None],
        inp,
        qkv[None],
        qkvb,
        outw[None],
        gsum,
        upw[None],
        upb,
        downw[None],
        gsum,
        n1g,
        n1b,
        n2g,
        n2b,
    )


def on_device(
    tokens,
    segments,
    positions,
    cotangent,
    qkv_weight,
    qkv_bias,
    out_weight,
    out_bias,
    up_weight,
    up_bias,
    down_weight,
    down_bias,
    norm1_gain,
    norm1_bias,
    norm2_gain,
    norm2_bias,
):
    dp_size = lax.axis_size("dp")
    n_outer = dp_size // 4
    core = lax.rem(lax.axis_index("dp"), 2)
    x = lax.axis_index("tensor")
    own, width = tokens.shape
    rows = qkv_weight.shape[1]
    seq_len = segments.shape[0]
    plane = Shape(
        n_outer,
        rows,
        own,
        width,
        seq_len,
        qkv_weight.shape[2] // 2,
        out_weight.shape[1] // 2,
        up_weight.shape[2] // 2,
        qkv_bias.shape[1],
        up_bias.shape[1],
    )
    if plane.fits():
        return on_plane(
            plane,
            (
                tokens,
                segments,
                positions,
                cotangent,
                qkv_weight,
                qkv_bias,
                out_weight,
                out_bias,
                up_weight,
                up_bias,
                down_weight,
                down_bias,
                norm1_gain,
                norm1_bias,
                norm2_gain,
                norm2_bias,
            ),
        )
    qkv_q, up_q, out_q = (
        qkv_weight.shape[2] // 2,
        up_weight.shape[2] // 2,
        out_weight.shape[1] // 2,
    )
    sizes = Sizes(rows, up_q, qkv_q, out_q, qkv_bias.shape[1], up_bias.shape[1])
    heads = out_q // HEAD

    def halves(w):
        return jnp.swapaxes(w.reshape(rows, 2, -1), 0, 1)

    def halves_t(w):
        return jnp.swapaxes(w.reshape(2, -1, rows), 1, 2)

    small = jnp.concatenate(
        [
            jnp.stack(
                [
                    norm1_gain[0],
                    norm1_bias[0],
                    norm2_gain[0],
                    norm2_bias[0],
                    out_bias[0],
                    down_bias[0],
                ],
                axis=1,
            ),
            fold(qkv_bias[0], 1, rows, sizes.qb_cols)[0],
            fold(up_bias[0], 1, rows, sizes.ub_cols)[0],
        ],
        axis=1,
    )
    packed = sizes.pack(
        halves(up_weight[0]),
        halves_t(down_weight[0]),
        halves(qkv_weight[0]),
        jnp.broadcast_to(small[None], (2,) + small.shape),
        halves_t(out_weight[0]),
    )
    own_pos = lax.dynamic_slice_in_dim(positions, x * own, own, 0).astype(BF16)
    rows_in = jnp.concatenate(
        [tokens, cotangent, jnp.pad(own_pos[:, None], ((0, 0), (0, 127)))], axis=1
    )
    gathered, group_rows = gather(sizes, n_outer, packed, rows_in)

    flat = gathered.reshape(dp_size * rows, sizes.cols)
    up_w = flat[:, :up_q]
    down_wt = flat[:, up_q : 2 * up_q]
    qkv_w = flat[:, sizes.qkv : sizes.qkv + qkv_q]
    out_wt = flat[:, sizes.out : sizes.out + out_q]
    smalls = flat[:, sizes.small : sizes.small + sizes.n_small].astype(F32)
    vecs = smalls[:, :6].T
    by_dev = smalls.reshape(dp_size, rows, sizes.n_small)
    qb = by_dev[:, :, 6 : 6 + sizes.qb_cols].reshape(dp_size, -1)[:, : sizes.qkvb].reshape(-1)
    ub = by_dev[:, :, 6 + sizes.qb_cols :].reshape(dp_size, -1)[:, : sizes.upb].reshape(-1)
    qkv_b = lax.dynamic_slice_in_dim(qb, core * qkv_q, qkv_q, 0)
    up_b = lax.dynamic_slice_in_dim(ub, core * up_q, up_q, 0)

    group_rows = group_rows.reshape(4 * own, -1)
    count = 4 * own
    seqs = count // seq_len
    xs = group_rows[:, :width].astype(F32)
    cot = group_rows[:, width : 2 * width]
    pos = group_rows[:, 2 * width].astype(F32).reshape(seqs, seq_len)
    cos_tab, sin_tab = rotary_tables(pos)
    query_index = jnp.arange(seq_len, dtype=F32)
    key_index = query_index[None, None, :]
    first_key = query_index[None, :] - pos
    allowed = (
        (key_index <= query_index[None, :, None]) & (key_index >= first_key[:, :, None])
    )[:, None]

    unit, _ = unit_rows(xs)
    n1 = (unit * vecs[0] + vecs[1]).astype(BF16)
    n2 = (unit * vecs[2] + vecs[3]).astype(BF16)
    projected = (dot(n1, qkv_w, 1, 0) + qkv_b).reshape(seqs, seq_len, heads, 3, HEAD)
    projected = jnp.transpose(projected, (3, 0, 2, 1, 4))
    query = rotate(projected[0], cos_tab, sin_tab).astype(BF16)
    key = rotate(projected[1], cos_tab, sin_tab).astype(BF16)
    value = projected[2].astype(BF16)
    scale = HEAD ** (-0.5)

    def ein(spec, a, b):
        return jnp.einsum(spec, a, b, preferred_element_type=F32)

    scores = jnp.where(allowed, ein("shqd,shkd->shqk", query, key) * scale, -jnp.inf)
    peak = jnp.max(scores, axis=-1, keepdims=True)
    log_total = peak + jnp.log(jnp.sum(jnp.exp(scores - peak), axis=-1, keepdims=True))
    weights = jnp.exp(scores - log_total)
    weights_bf = weights.astype(BF16)
    attended = ein("shqk,shkd->shqd", weights_bf, value).astype(BF16)
    attended_flat = jnp.swapaxes(attended, 1, 2).reshape(count, out_q)
    pre = dot(n2, up_w, 1, 0) + up_b
    cumul = 0.5 * (1.0 + jax.scipy.special.erf(pre * 0.7071067811865476))
    act = (pre * cumul).astype(BF16)
    slope = cumul + pre * jnp.exp(-0.5 * pre * pre) * 0.3989422804014327
    mixed = dot(attended_flat, out_wt, 1, 1) + dot(act, down_wt, 1, 1)

    du = (dot(cot, down_wt, 1, 0) * slope).astype(BF16)
    g_upb = jnp.sum(du.astype(F32), axis=0)
    dn2 = dot(du, up_w, 1, 1)
    d_att = dot(cot, out_wt, 1, 0).astype(BF16).reshape(seqs, seq_len, heads, HEAD)
    d_att = jnp.swapaxes(d_att, 1, 2)
    delta = jnp.sum(attended.astype(F32) * d_att.astype(F32), axis=-1, keepdims=True)
    d_value = ein("shqk,shqd->shkd", weights_bf, d_att)
    d_weight = ein("shqd,shkd->shqk", d_att, value)
    d_score = (weights * (d_weight - delta) * scale).astype(BF16)
    d_query = unrotate(ein("shqk,shkd->shqd", d_score, key), cos_tab, sin_tab)
    d_key = unrotate(ein("shqk,shqd->shkd", d_score, query), cos_tab, sin_tab)
    d_qkv = jnp.stack([d_query, d_key, d_value], axis=0).astype(BF16)
    d_qkv = jnp.transpose(d_qkv, (1, 3, 2, 0, 4)).reshape(count, qkv_q)
    g_qkvb = jnp.sum(d_qkv.astype(F32), axis=0)
    dn1 = dot(d_qkv, qkv_w, 1, 1)
    back = dn1 * vecs[0] + dn2 * vecs[2]
    up_rows = cotangent.astype(F32)
    norm_rows = jnp.stack(
        [
            jnp.sum(dn1 * unit, axis=0),
            jnp.sum(dn1, axis=0),
            jnp.sum(dn2 * unit, axis=0),
            jnp.sum(dn2, axis=0),
            jnp.sum(up_rows, axis=0),
            jnp.zeros((width,), F32),
        ],
        axis=1,
    ).reshape(dp_size, rows, 6)
    own_half = jnp.arange(2)[:, None] == core
    qb_full = jnp.where(own_half, g_qkvb[None], 0.0).reshape(-1)
    ub_full = jnp.where(own_half, g_upb[None], 0.0).reshape(-1)
    small_grads = jnp.concatenate(
        [
            norm_rows,
            fold(qb_full, dp_size, rows, sizes.qb_cols),
            fold(ub_full, dp_size, rows, sizes.ub_cols),
        ],
        axis=2,
    )
    small_grads = jnp.pad(
        small_grads,
        (
            (0, 0),
            (0, 0),
            (sizes.small - sizes.tile, sizes.tile_end - sizes.small - sizes.n_small),
        ),
    ).reshape(dp_size // 2, 2, rows, -1)

    def turned(values):
        return values.T.reshape(dp_size // 2, 2, rows, count)

    operands = (
        turned(n2),
        turned(cot),
        turned(n1),
        du,
        act,
        jnp.pad(d_qkv, ((0, 0), (0, sizes.out - sizes.small))),
        attended_flat,
        small_grads,
    )
    reduced, mixed_sum, total, small_sum = scatter(
        sizes,
        n_outer,
        operands,
        mixed.astype(BF16).reshape(2, 2, own, width),
        back.astype(BF16).reshape(2, 2, own, width),
    )

    own_x = tokens.astype(F32)
    own_unit, own_inv = unit_rows(own_x)
    hidden = (own_x + mixed_sum + vecs[4] + vecs[5]).astype(BF16)
    mean_term = jnp.mean(total, axis=-1, keepdims=True)
    proj_term = jnp.mean(total * own_unit, axis=-1, keepdims=True)
    input_grad = up_rows + own_inv * (total - mean_term - own_unit * proj_term)

    def columns(start, size):
        return jnp.swapaxes(reduced[:, :, start : start + size], 0, 1).reshape(rows, 2 * size)

    def columns_t(start, size):
        return jnp.swapaxes(reduced[:, :, start : start + size], 1, 2).reshape(2 * size, rows)

    off = sizes.small - sizes.tile
    fin = small_sum[1, :, off : off + 6].T
    qb_out = small_sum[0, :, off + 6 : off + 6 + sizes.qb_cols].reshape(-1)[: sizes.qkvb]
    ub_at = off + 6 + sizes.qb_cols
    ub_out = small_sum[0, :, ub_at : ub_at + sizes.ub_cols].reshape(-1)[: sizes.upb]
    return (
        hidden[None],
        input_grad,
        columns(sizes.qkv, qkv_q)[None],
        qb_out[None],
        columns_t(sizes.out, out_q)[None],
        fin[4][None],
        columns(0, up_q)[None],
        ub_out[None],
        columns_t(sizes.down, up_q)[None],
        fin[4][None],
        fin[0][None],
        fin[1][None],
        fin[2][None],
        fin[3][None],
    )


def solution(mesh):
    in_specs = (
        P(("dp", "tensor"), None),
        P("dp"),
        P("dp"),
        P(("dp", "tensor"), None),
        P(None, "dp", "tensor"),
        P(None, ("tensor", "dp")),
        P(None, "tensor", "dp"),
        P(None, "dp"),
        P(None, "dp", "tensor"),
        P(None, ("tensor", "dp")),
        P(None, "tensor", "dp"),
        P(None, "dp"),
        P(None, "dp"),
        P(None, "dp"),
        P(None, "dp"),
        P(None, "dp"),
    )
    out_specs = (
        P(None, ("dp", "tensor"), None),
        P(("dp", "tensor"), None),
        P(None, "dp", "tensor"),
        P(None, ("tensor", "dp")),
        P(None, "tensor", "dp"),
        P(None, "dp"),
        P(None, "dp", "tensor"),
        P(None, ("tensor", "dp")),
        P(None, "tensor", "dp"),
        P(None, "dp"),
        P(None, "dp"),
        P(None, "dp"),
        P(None, "dp"),
        P(None, "dp"),
    )
    return jax.shard_map(
        on_device, mesh=mesh, in_specs=in_specs, out_specs=out_specs, check_vma=False
    )
```

```python
import functools

import jax
import jax.numpy as jnp
from jax import lax
from jax.experimental import pallas as pl
from jax.experimental.pallas import tpu as pltpu
from jax.sharding import PartitionSpec as P

HEAD = 64
ROT = 16
EPS = 1e-05
F32 = jnp.float32
BF16 = jnp.bfloat16
VMEM = pltpu.VMEM


def up128(n):
    return -(-n // 128) * 128


class Sizes:
    def __init__(self, rows, up_q, qkv_q, out_q, qkvb, upb):
        self.rows, self.up_q, self.qkv_q, self.out_q = rows, up_q, qkv_q, out_q
        self.qkvb, self.upb = qkvb, upb
        self.qb_cols, self.ub_cols = -(-qkvb // rows), -(-upb // rows)
        self.down = up_q
        self.qkv = 2 * up_q
        self.small = self.qkv + qkv_q
        self.n_small = 6 + self.qb_cols + self.ub_cols
        self.out = up128(self.small + self.n_small)
        self.cols = up128(self.out + out_q)
        self.tile = self.small // 128 * 128
        self.tile_end = self.out

    def pack(self, up, down, qkv, small, out):
        lead = up.shape[:-1]
        gap = self.out - self.small - small.shape[-1]
        tail = self.cols - self.out - self.out_q
        parts = [up, down, qkv, small, jnp.zeros(lead + (gap,), BF16), out]
        if tail:
            parts.append(jnp.zeros(lead + (tail,), BF16))
        return jnp.concatenate([p.astype(BF16) for p in parts], axis=-1)


def places(n_outer):
    dp = lax.axis_index("dp")
    x = lax.axis_index("tensor")
    core = lax.rem(dp, 2)
    chip = dp // 2
    inner = lax.rem(chip, 2)
    outer = chip // 2
    return dp, x, core, chip, inner, outer


def dev(chip, core, x):
    return {"dp": chip * 2 + core, "tensor": x}


def greet(partners, outer, n_outer, up, down):
    barrier = pltpu.get_barrier_semaphore()

    def tell(partner):
        pl.semaphore_signal(
            barrier, inc=1, device_id=partner, device_id_type=pl.DeviceIdType.MESH
        )

    for partner in partners:
        tell(partner)
    pl.when(outer < n_outer - 1)(lambda: tell(up))
    pl.when(outer > 0)(lambda: tell(down))
    chained = jnp.minimum(outer, 1) + jnp.minimum(n_outer - 1 - outer, 1)
    pl.semaphore_wait(barrier, len(partners) + chained)


def rcopy(src, dst, send, recv, where):
    return pltpu.make_async_remote_copy(
        src_ref=src,
        dst_ref=dst,
        send_sem=send,
        recv_sem=recv,
        device_id=where,
        device_id_type=pl.DeviceIdType.MESH,
    )


def partner_list(n_outer):
    dp, x, core, chip, inner, outer = places(n_outer)
    sibling = dev(chip, 1 - core, x)
    across = dev(chip, core, 1 - x)
    diagonal = dev(chip, 1 - core, 1 - x)
    inner_peer = dev(outer * 2 + 1 - inner, core, x)
    up = dev((outer + 1) * 2 + inner, core, x)
    down = dev((outer - 1) * 2 + inner, core, x)
    return sibling, across, diagonal, inner_peer, up, down


def gather_kernel(
    n_outer, p_ref, a_ref, w_ref, t_ref, loc_sem, grp_s, grp_r, sib_s, sib_r, ch_s, ch_r, in_s, in_r
):
    dp, x, core, chip, inner, outer = places(n_outer)
    sibling, across, diagonal, inner_peer, up, down = partner_list(n_outer)
    own_w = pltpu.make_async_copy(p_ref.at[core], w_ref.at[chip, core], loc_sem.at[0])
    own_t = pltpu.make_async_copy(a_ref, t_ref.at[core, x], loc_sem.at[1])
    own_w.start()
    own_t.start()
    greet([sibling, across, diagonal, inner_peer], outer, n_outer, up, down)
    sib = rcopy(p_ref.at[1 - core], w_ref.at[chip, core], sib_s, sib_r, sibling)
    sib.start()
    own_w.wait()
    sib.wait_recv()
    last = n_outer - 1

    def chain(way, step):
        block = outer - step if way == 0 else outer + step
        there = (outer < last) & (block >= 0) if way == 0 else (outer > 0) & (block <= last)
        spot = w_ref.at[block * 2 + inner]
        where = up if way == 0 else down
        return there, lambda: rcopy(spot, spot, ch_s.at[way, step], ch_r.at[way, step], where)

    def arrival(way, step):
        block = outer - 1 - step if way == 0 else outer + 1 + step
        there = block >= 0 if way == 0 else block <= last
        spot = w_ref.at[block * 2 + inner]
        return there, lambda: rcopy(spot, spot, ch_s.at[way, step], ch_r.at[way, step], up)

    def forward(way, step, mine):
        block = outer - 1 - step if way == 0 else outer + 1 + step
        there = block >= 0 if way == 0 else block <= last
        spot = w_ref.at[block * 2 + (inner if mine else 1 - inner)]
        return there, lambda: rcopy(spot, spot, in_s.at[way, step], in_r.at[way, step], inner_peer)

    def act(pair, what):
        there, copy = pair
        pl.when(there)(lambda: what(copy()))

    def start(copy):
        copy.start()

    for way in range(2):
        act(chain(way, 0), start)
    own = w_ref.at[chip]
    mine = rcopy(own, own, in_s.at[0, last], in_r.at[0, last], inner_peer)
    mine.start()
    group = []
    for slot, where in enumerate((sibling, across, diagonal)):
        copy = rcopy(a_ref, t_ref.at[core, x], grp_s.at[slot], grp_r.at[slot], where)
        copy.start()
        group.append(copy)
    for step in range(last):
        for way in range(2):
            act(arrival(way, step), lambda copy: copy.wait_recv())
            if step + 1 < last:
                act(chain(way, step + 1), start)
            act(forward(way, step, True), start)
    for copy in group:
        copy.wait_recv()
    mine.wait_recv()
    for step in range(last):
        for way in range(2):
            act(forward(way, step, False), lambda copy: copy.wait_recv())
    own_t.wait()
    sib.wait_send()
    mine.wait_send()
    for copy in group:
        copy.wait_send()
    for step in range(last):
        for way in range(2):
            act(chain(way, step), lambda copy: copy.wait_send())
            act(forward(way, step, True), lambda copy: copy.wait_send())


def scatter_kernel(
    sizes,
    n_outer,
    n2t_ref,
    cott_ref,
    n1t_ref,
    du_ref,
    act_ref,
    dqkv_ref,
    att_ref,
    small_ref,
    h_ref,
    d_ref,
    r_ref,
    hs_ref,
    ds_ref,
    x_ref,
    first_buf,
    b1,
    send_buf,
    cbuf,
    acc,
    hr,
    small_out,
    small_in,
    grp_s,
    grp_r,
    in_s,
    in_r,
    ch_s,
    ch_r,
    sib_s,
    sib_r,
    sm_s,
    sm_r,
):
    dp, x, core, chip, inner, outer = places(n_outer)
    sibling, across, diagonal, inner_peer, up, down = partner_list(n_outer)
    last = n_outer - 1
    rows = sizes.rows
    lo, hi = sizes.tile, sizes.tile_end

    def block(target, put):
        def product(left, right):
            if rows % 16 == 0:
                lhs = left[target].reshape(2 * rows, -1)
                out = jnp.dot(lhs, right[...], preferred_element_type=F32)
                return out.reshape(2, rows, -1)
            return jnp.stack(
                [
                    jnp.dot(left[target, side], right[...], preferred_element_type=F32)
                    for side in range(2)
                ]
            )

        put(0, sizes.down, product(n2t_ref, du_ref))
        put(sizes.down, sizes.qkv, product(cott_ref, act_ref))
        part = product(n1t_ref, dqkv_ref)
        cut = lo - sizes.qkv
        put(sizes.qkv, lo, part[:, :, :cut])
        put(lo, hi, part[:, :, cut:] + small_ref[target])
        end = sizes.out + sizes.out_q
        put(sizes.out, end, product(cott_ref, att_ref))
        if end < sizes.cols:
            put(end, sizes.cols, jnp.zeros((2, rows, sizes.cols - end), F32))

    def to_acc(start, stop, value):
        acc[:, :, start:stop] = value

    greet([sibling, across, diagonal, inner_peer], outer, n_outer, up, down)
    group = []
    spots = ((sibling, 1 - core, x), (across, core, 1 - x), (diagonal, 1 - core, 1 - x))
    for slot, (where, to_core, to_x) in enumerate(spots):
        for kind, part in enumerate((h_ref, d_ref)):
            copy = rcopy(
                part.at[to_core, to_x],
                hr.at[kind, slot],
                grp_s.at[kind, slot],
                grp_r.at[kind, slot],
                where,
            )
            copy.start()
            group.append(copy)

    def in_order(what):
        @pl.loop(0, last)
        def _(tick):
            back = last - tick
            pl.when(outer <= tick)(lambda: what(0, outer + back))
            pl.when(outer >= back)(lambda: what(1, outer - back))

    def exchange(target):
        return rcopy(
            first_buf.at[target], b1.at[target], in_s.at[target], in_r.at[target], inner_peer
        )

    def passing(way, target):
        return rcopy(
            send_buf.at[target],
            cbuf.at[way, target],
            ch_s.at[way, target],
            ch_r.at[way, target],
            up if way == 0 else down,
        )

    def send_first(target):
        def put(start, stop, value):
            first_buf[target, :, :, start:stop] = value.astype(BF16)

        block(target * 2 + 1 - inner, put)
        exchange(target).start()

    def send_second(way, target):
        block(target * 2 + inner, to_acc)
        exchange(target).wait_recv()
        acc[...] += b1[target].astype(F32)
        started = outer > 0 if way == 0 else outer < last

        @pl.when(started)
        def _():
            passing(way, target).wait_recv()
            acc[...] += cbuf[way, target].astype(F32)

        send_buf[target] = acc[...].astype(BF16)
        passing(way, target).start()

    in_order(lambda way, target: send_first(target))
    send_first(outer)
    in_order(send_second)
    for copy in group:
        copy.wait_recv()
    for kind, (part, out) in enumerate(((h_ref, hs_ref), (d_ref, ds_ref))):
        out[...] = (
            part[core, x].astype(F32)
            + hr[kind, 0].astype(F32)
            + hr[kind, 1].astype(F32)
            + hr[kind, 2].astype(F32)
        )
    block(chip, to_acc)
    exchange(outer).wait_recv()
    acc[...] += b1[outer].astype(F32)
    for way in range(2):

        @pl.when(outer > 0 if way == 0 else outer < last)
        def _():
            passing(way, outer).wait_recv()
            acc[...] += cbuf[way, outer].astype(F32)

    sib = rcopy(acc.at[1 - core], r_ref.at[core], sib_s, sib_r, sibling)
    sib.start()
    r_ref[core] = acc[core]
    sib.wait_recv()
    small_out[...] = r_ref[0, :, lo:hi] + r_ref[1, :, lo:hi]
    small = rcopy(small_out, small_in, sm_s, sm_r, across)
    small.start()
    small.wait_recv()
    x_ref[0] = small_out[...]
    x_ref[1] = small_out[...] + small_in[...]
    sib.wait_send()
    small.wait_send()
    for copy in group:
        copy.wait_send()
    exchange(outer).wait_send()

    def sent(way, target):
        exchange(target).wait_send()
        passing(way, target).wait_send()

    in_order(sent)


def gather(sizes, n_outer, packed, rows):
    dma = pltpu.SemaphoreType.DMA
    full = pl.BlockSpec(memory_space=VMEM)
    return pl.pallas_call(
        functools.partial(gather_kernel, n_outer),
        out_shape=(
            jax.ShapeDtypeStruct((2 * n_outer, 2) + packed.shape[1:], BF16),
            jax.ShapeDtypeStruct((2, 2) + rows.shape, BF16),
        ),
        in_specs=[full, full],
        out_specs=(full, full),
        scratch_shapes=[
            dma((2,)),
            dma((3,)),
            dma((3,)),
            dma,
            dma,
            dma((2, n_outer)),
            dma((2, n_outer)),
            dma((2, n_outer)),
            dma((2, n_outer)),
        ],
        compiler_params=pltpu.CompilerParams(
            collective_id=0, has_side_effects=True, vmem_limit_bytes=60 * 2**20
        ),
        name="gather",
    )(packed, rows)


def scatter(sizes, n_outer, operands, mixed, back):
    dma = pltpu.SemaphoreType.DMA
    full = pl.BlockSpec(memory_space=VMEM)
    block = (2, sizes.rows, sizes.cols)
    width = sizes.tile_end - sizes.tile
    return pl.pallas_call(
        functools.partial(scatter_kernel, sizes, n_outer),
        out_shape=(
            jax.ShapeDtypeStruct(block, F32),
            jax.ShapeDtypeStruct(mixed.shape[2:], F32),
            jax.ShapeDtypeStruct(mixed.shape[2:], F32),
            jax.ShapeDtypeStruct((2, sizes.rows, width), F32),
        ),
        in_specs=[full] * (len(operands) + 2),
        out_specs=(full, full, full, full),
        scratch_shapes=[
            VMEM((n_outer,) + block, BF16),
            VMEM((n_outer,) + block, BF16),
            VMEM((n_outer,) + block, BF16),
            VMEM((2, n_outer) + block, BF16),
            VMEM(block, F32),
            VMEM((2, 3) + mixed.shape[2:], BF16),
            VMEM((sizes.rows, width), F32),
            VMEM((sizes.rows, width), F32),
            dma((2, 3)),
            dma((2, 3)),
            dma((n_outer,)),
            dma((n_outer,)),
            dma((2, n_outer)),
            dma((2, n_outer)),
            dma,
            dma,
            dma,
            dma,
        ],
        compiler_params=pltpu.CompilerParams(
            collective_id=1, has_side_effects=True, vmem_limit_bytes=60 * 2**20
        ),
        name="scatter",
    )(*operands, mixed, back)


def rotary_tables(pos_ids):
    half_rot = ROT // 2
    freq_index = jnp.arange(half_rot, dtype=F32)
    inverse = jnp.power(F32(10000.0), -2.0 * freq_index / ROT)
    angles = pos_ids[..., None] * inverse
    cos_tab = jnp.concatenate([jnp.cos(angles), jnp.cos(angles)], axis=-1)
    sin_tab = jnp.concatenate([jnp.sin(angles), jnp.sin(angles)], axis=-1)
    return (cos_tab[:, None], sin_tab[:, None])


def rotate(values, cos_tab, sin_tab):
    half_rot = ROT // 2
    rotary = values[..., :ROT]
    turned = jnp.concatenate([-rotary[..., half_rot:], rotary[..., :half_rot]], axis=-1)
    return jnp.concatenate([rotary * cos_tab + turned * sin_tab, values[..., ROT:]], axis=-1)


def unrotate(grad_vals, cos_tab, sin_tab):
    half_rot = ROT // 2
    rotary = grad_vals[..., :ROT]
    scaled = rotary * sin_tab
    back_part = jnp.concatenate([scaled[..., half_rot:], -scaled[..., :half_rot]], axis=-1)
    return jnp.concatenate([rotary * cos_tab + back_part, grad_vals[..., ROT:]], axis=-1)


def unit_rows(values):
    centre = values - jnp.mean(values, axis=-1, keepdims=True)
    inv_std = lax.rsqrt(jnp.mean(centre * centre, axis=-1, keepdims=True) + EPS)
    return centre * inv_std, inv_std


def dot(a, b, ca, cb):
    return lax.dot_general(a, b, (((ca,), (cb,)), ((), ())), preferred_element_type=F32)


def fold(vector, count, rows, cols):
    per = vector.shape[0] // count
    padded = jnp.pad(vector.reshape(count, per), ((0, 0), (0, rows * cols - per)))
    return padded.reshape(count, rows, cols)


CHAIN = 4


class Shape:
    def __init__(self, n, rows, own, width, seq, qkv, out, up, qkvb, upb):
        self.n, self.rows, self.own, self.width, self.seq = n, rows, own, width, seq
        self.qkv, self.out, self.up, self.qkvb, self.upb = qkv, out, up, qkvb, upb
        self.heads = out // HEAD
        self.att = qkv + out
        self.tokens = 4 * own
        self.cols = (self.att, up, up // 2, up // 2)
        self.gcols = (self.att, up, up // 2, up // 2)

    def fits(self):
        aligned = [self.own, self.width, self.seq, self.att, self.up]
        return (
            self.rows % 16 == 0
            and all(size % 128 == 0 for size in aligned)
            and self.up % 256 == 0
            and self.n == CHAIN
            and self.own * 2 == self.seq
            and self.att <= self.up
            and self.width <= self.up
            and max(self.rows, self.qkvb, self.upb) <= 128
            and self.n >= 2
            and (self.n * 4) * self.rows == self.width
        )


def fused_kernel(S, *refs):
    refs = list(refs)

    def take(count):
        got = refs[:count]
        del refs[:count]
        return got

    tok_ref, cot_ref, pos_ref, qkv_ref, out_ref, up_ref, down_ref = take(7)
    small_params = take(8)
    red = take(4)
    hs_ref, bs_ref, small_ref, prm_ref = take(4)
    pk, qkv_v, out_v = take(3)
    w = take(4)
    tbuf, cbuf, pbuf, smrow, bias, unit, n1, n2, mask, rot_c, rot_s = take(11)
    sbuf, ct, ut, n1t, n2t = take(5)
    proj, qh, kh, vh, doh, att, dqk, dqkv, outw, act, slope = take(11)
    du = take(2)
    grad, sb, rb, cs, ci, ysb, yrb = (take(4) for _ in range(7))
    mine, mix_s, mix_r, mix_t, mix_u, sm_s, sm_z, sm_r = take(8)
    ld, gy_s, gy_r, gc_s, gc_r, gf_s, gf_r, tk_s, tk_r, ps_s, ps_r = take(11)
    ss_s, ss_r, sc_s, sc_r, sy_s, sy_r, mx_s, mx_r, st_s, st_r, sz_s, sz_r = take(12)
    py_s, py_r, pz_s, pz_r, pf_s, pf_r = take(6)
    w_a, w_u = w[:2]
    n, rows, own, width = S.n, S.rows, S.own, S.width
    last = n - 1
    dp = lax.axis_index("dp")
    x = lax.axis_index("tensor")
    core = lax.rem(dp, 2)
    y = lax.rem(dp // 2, 2)
    z = dp // 4

    def at(zz, yy, cc, xx):
        return {"dp": zz * 4 + yy * 2 + cc, "tensor": xx}

    sibling = at(z, y, 1 - core, x)
    across = at(z, y, core, 1 - x)
    ypeer = at(z, 1 - y, core, x)
    up, down = at(z + 1, y, core, x), at(z - 1, y, core, x)
    sends = []

    def begin(copy):
        copy.start()
        sends.append(copy)
        return copy

    def iota(shape, axis):
        return lax.broadcasted_iota(jnp.int32, shape, axis)

    def load(i, src, dst):
        copy = pltpu.make_async_copy(src, dst, ld.at[i])
        copy.start()
        return copy

    def cut(ref, start, size):
        return ref.at[:, pl.ds(pl.multiple_of(start, 128), size)]

    half = S.up // 2

    def part_of(k, q):
        if k == 0:
            return pk.at[q]
        if k == 1:
            return cut(up_ref, q * S.up, S.up)
        return cut(down_ref, q * S.up + (k - 2) * half, half)

    loads = [load(0, qkv_ref, qkv_v), load(1, out_ref, out_v)]
    own_loads = [load(1 + k, part_of(k, y), w[k].at[z, y, core]) for k in range(1, 4)]
    own_rows = [load(5, tok_ref, tbuf.at[y, x]), load(6, cot_ref, cbuf.at[y, x])]
    row_pos = pos_ref[...].astype(F32)
    pbuf[y] = jnp.broadcast_to(row_pos, pbuf.shape[1:])
    smrow[...] = jnp.zeros_like(smrow)
    for row, part in enumerate(small_params):
        smrow[row : row + 1, : part.shape[1]] = part[...].astype(F32)
    for copy in loads:
        copy.wait()
    for q in range(2):
        pk[q, :, : S.qkv] = qkv_v[:, q * S.qkv : (q + 1) * S.qkv]
        pk[q, :, S.qkv : S.att] = out_v[:, q * S.out : (q + 1) * S.out]
    w[0][z, y, core] = pk[y]
    sbuf[z, y, core] = smrow[...].astype(BF16)

    barrier = pltpu.get_barrier_semaphore()

    def tell(partner):
        pl.semaphore_signal(
            barrier, inc=1, device_id=partner, device_id_type=pl.DeviceIdType.MESH
        )

    for partner in (sibling, across, ypeer):
        tell(partner)
    for step in range(1, n):
        tell(at(lax.rem(z + step, n), y, core, x))
    pl.semaphore_wait(barrier, 3 + last)

    def y_copy(k):
        return rcopy(part_of(k, 1 - y), w[k].at[z, y, core], gy_s.at[k], gy_r.at[k], ypeer)

    def spot_of(k, block):
        if k < 2:
            return w[0].at[block, y if k == 0 else 1 - y, core]
        return w[k - 1].at[block, :, core]

    def chain_copy(k, way, step):
        block = z - step if way == 0 else z + step
        there = (z < last) & (block >= 0) if way == 0 else (z > 0) & (block <= last)
        where = up if way == 0 else down

        def copy():
            spot = spot_of(k, block)
            return rcopy(spot, spot, gc_s.at[k, way, step], gc_r.at[k, way, step], where)

        return there, copy

    def fan_copy(k, block):
        spot = spot_of(k, block)
        return rcopy(spot, spot, gf_s.at[k, block], gf_r.at[k, block], sibling)

    def arrived(way, step):
        block = z - 1 - step if way == 0 else z + 1 + step
        return block, (block >= 0 if way == 0 else block <= last)

    def start_own(k):
        if k > 1:
            own_loads[k - 2].wait()
        if k:
            y_copy(k - 1).wait_recv()
        for way in range(2):
            there, copy = chain_copy(k, way, 0)
            pl.when(there)(lambda: copy().start())
        fan_copy(k, z).start()

    def relay(k, step):
        for way in range(2):
            block, there = arrived(way, step)

            @pl.when(there)
            def _():
                spot = spot_of(k, block)
                rcopy(spot, spot, gc_s.at[k, way, step], gc_r.at[k, way, step], up).wait_recv()

            if step + 1 < last:
                more, copy = chain_copy(k, way, step + 1)
                pl.when(more)(lambda: copy().start())
            pl.when(there)(lambda: fan_copy(k, block).start())

    def gathered(k):
        for block in range(n):
            if k < 2:
                spot = w[0].at[block, y if k == 0 else 1 - y, 1 - core]
            else:
                spot = w[k - 1].at[block, :, 1 - core]
            rcopy(spot, spot, gf_s.at[k, block], gf_r.at[k, block], sibling).wait_recv()

    def params_y():
        mine_spot = sbuf.at[z, y, core]
        return rcopy(mine_spot, mine_spot, py_s, py_r, ypeer)

    def params_z(step, block):
        spot = sbuf.at[block, :, core]
        where = at(lax.rem(z + step, n), y, core, x)
        return rcopy(spot, spot, pz_s.at[step - 1], pz_r.at[step - 1], where)

    def params_fan(which):
        spot = sbuf.at[:, :, which]
        return rcopy(spot, spot, pf_s, pf_r, sibling)

    def params_send():
        params_y().wait_recv()
        for step in range(1, n):
            begin(params_z(step, z))

    def params_fan_out():
        for step in range(1, n):
            params_z(step, lax.rem(z - step + n, n)).wait_recv()
        begin(params_fan(core))

    def send_y(k):
        begin(y_copy(k))

    low, high = pl.ds(0, own // 2), pl.ds(own // 2, own // 2)

    def row_copy(kind, slot):
        src, dst = ((tok_ref, tbuf), (cot_ref, cbuf))[kind]
        where = across if slot in (0, 3) else ypeer
        if slot == 2:
            src, dst = dst.at[y, 1 - x, low], dst.at[y, 1 - x, low]
        elif slot == 3:
            src, dst = dst.at[1 - y, x, high], dst.at[1 - y, x, high]
        else:
            dst = dst.at[y, x]
        return rcopy(src, dst, tk_s.at[kind, slot], tk_r.at[kind, slot], where)

    def send_rows(kind):
        begin(row_copy(kind, 0))
        begin(row_copy(kind, 1))

    def pass_rows(kind):
        row_copy(kind, 0).wait_recv()
        begin(row_copy(kind, 2))
        row_copy(kind, 1).wait_recv()
        begin(row_copy(kind, 3))

    def have_rows(kind):
        own_rows[kind].wait()
        row_copy(kind, 2).wait_recv()
        row_copy(kind, 3).wait_recv()

    begin(params_y())
    pos_copy = begin(rcopy(pbuf.at[y], pbuf.at[y], ps_s, ps_r, ypeer))

    lane = iota((own, 128), 1)
    spin = lax.rem(lane, HEAD)

    def tables():
        pos_copy.wait_recv()
        freq = jnp.zeros((1, 128), F32)
        which = lax.rem(iota((1, 128), 1), ROT // 2)
        for i in range(ROT // 2):
            freq = jnp.where(which == i, 10000.0 ** (-2.0 * i / ROT), freq)
        query = iota((S.seq, S.seq), 0).astype(F32)
        key = iota((S.seq, S.seq), 1).astype(F32)
        spin_s = lax.rem(iota((S.seq, 128), 1), HEAD)
        for s in range(2):
            line = jnp.where(query == key, pbuf[s, 0:1, :], 0.0)
            column = jnp.sum(line, axis=1, keepdims=True)
            seen = (key <= query) & (key >= query - column)
            mask[s] = jnp.where(seen, 0.0, -jnp.inf)
            angles = column * freq
            sines = jnp.sin(angles)
            rot_c[s * S.seq : (s + 1) * S.seq] = jnp.where(spin_s < ROT, jnp.cos(angles), 1.0)
            rot_s[s * S.seq : (s + 1) * S.seq] = jnp.where(
                spin_s < ROT // 2, -sines, jnp.where(spin_s < ROT, sines, 0.0)
            )

    def blocks(body):
        pl.loop(0, 4)(lambda g: body(g, pl.ds(pl.multiple_of(g * own, own), own)))

    def units():
        def body(g, part):
            value = unit_rows(tbuf[g // 2, lax.rem(g, 2)].astype(F32))[0]
            unit[part] = value
            ut[:, part] = value.T

        blocks(body)

    def turn_cot():
        def body(g, part):
            ct[:, part] = cbuf[g // 2, lax.rem(g, 2)].T

        blocks(body)

    def params():
        params_fan(1 - core).wait_recv()
        total = jnp.zeros((8, S.up), F32)
        for j in range(4 * n):
            piece = sbuf[j // 4, (j // 2) % 2, j % 2].astype(F32)[0:8]
            wide = jnp.concatenate([piece, jnp.zeros((8, S.up - 128), F32)], axis=1)
            total = total + (pltpu.roll(wide, j * rows, 1) if j else wide)
        prm_ref[...] = total[:, :width]
        q_total = jnp.zeros((8, S.up), F32)
        u_total = jnp.zeros((8, S.up), F32)
        for j in range(2 * n):
            there = y * (n // 2) + j // 4
            piece = sbuf[there, (j // 2) % 2, j % 2].astype(F32)[0:8]
            wide = jnp.concatenate([piece, jnp.zeros((8, S.up - 128), F32)], axis=1)
            q_total = q_total + (pltpu.roll(wide, j * S.qkvb, 1) if j else wide)
            u_total = u_total + (pltpu.roll(wide, j * S.upb, 1) if j else wide)
        bias[0:8] = q_total
        bias[8:16] = u_total

    def flat(ref, start, stop):
        return ref[:, :, :, :, start:stop].reshape(4 * n * rows, stop - start)

    def norms():
        def body(g, part):
            value = unit[part]
            n1[part] = (value * prm_ref[0:1] + prm_ref[1:2]).astype(BF16)
            n2[part] = (value * prm_ref[2:3] + prm_ref[3:4]).astype(BF16)

        blocks(body)

    def norms_turned():
        tall = jnp.concatenate([prm_ref[...], jnp.zeros((120, width), F32)], axis=0)
        tall = tall.T
        for i in range(width // 128):
            spot = slice(i * 128, (i + 1) * 128)
            value, param = ut[spot], tall[spot]
            n1t[spot] = (value * param[:, 0:1] + param[:, 1:2]).astype(BF16)
            n2t[spot] = (value * param[:, 2:3] + param[:, 3:4]).astype(BF16)

    def turn(values, part, sign):
        ahead, behind = pltpu.roll(values, 128 - ROT // 2, 1), pltpu.roll(values, ROT // 2, 1)
        other = jnp.where(spin < ROT // 2, ahead, behind) * rot_s[part]
        return values * rot_c[part] + (other if sign > 0 else -other)

    def project():
        outw[...] = flat(w_a, S.qkv, S.att)

        def body(g, part):
            proj[...] = dot(n1[part], flat(w_a, 0, S.qkv), 1, 0) + bias[6:7, : S.qkv]
            for h in range(S.heads):
                base = h * 3 * HEAD
                pair = turn(proj[:, base : base + 2 * HEAD], part, 1).astype(BF16)
                qh[h, part] = pair[:, :HEAD]
                kh[h, part] = pair[:, HEAD:]
                vh[h, part] = proj[:, base + 2 * HEAD : base + 3 * HEAD].astype(BF16)
        blocks(body)

    def project_back():
        def body(g, part):
            grads = dot(cbuf[g // 2, lax.rem(g, 2)], outw[...], 1, 0).astype(BF16)
            for h in range(S.heads):
                doh[h, part] = grads[:, h * HEAD : (h + 1) * HEAD]

        blocks(body)

    scale = HEAD ** (-0.5)

    def attend(s, h):
        part = slice(s * S.seq, (s + 1) * S.seq)
        q, k, v, dout = qh[h, part], kh[h, part], vh[h, part], doh[h, part]
        scores = dot(q, k, 1, 1) * scale + mask[s]
        raised = jnp.exp(scores - jnp.max(scores, axis=-1, keepdims=True))
        weights = raised * (1.0 / jnp.sum(raised, axis=-1, keepdims=True))
        weights_bf = weights.astype(BF16)
        got = dot(weights_bf, v, 1, 0).astype(BF16)
        att[part, h * HEAD : (h + 1) * HEAD] = got
        delta = jnp.sum(got.astype(F32) * dout.astype(F32), axis=-1, keepdims=True)
        d_score = (weights * (dot(dout, v, 1, 1) - delta) * scale).astype(BF16)
        dqk[part, :HEAD] = dot(d_score, k, 1, 0)
        dqk[part, HEAD:] = dot(d_score, q, 0, 0)
        base = h * 3 * HEAD
        dqkv[part, base + 2 * HEAD : base + 3 * HEAD] = dot(weights_bf, dout, 0, 0).astype(BF16)
        for half in range(2):
            piece = slice(s * S.seq + half * own, s * S.seq + (half + 1) * own)
            dqkv[piece, base : base + 2 * HEAD] = turn(dqk[piece], piece, -1).astype(BF16)

    def weight_grad(left, right, target, start):
        size = right.shape[1]

        @pl.loop(0, width // 128)
        def _(i):
            spot = pl.ds(pl.multiple_of(i * 128, 128), 128)
            target[spot, start : start + size] = dot(left[spot], right[...], 1, 0)

    def hidden():
        def body(g, part):
            pre = dot(n2[part], flat(w_u, 0, S.up), 1, 0) + bias[15:16, : S.up]
            cumul = 0.5 * (1.0 + lax.erf(pre * 0.7071067811865476))
            act[part] = (pre * cumul).astype(BF16)
            slope[part] = cumul + pre * jnp.exp(-0.5 * pre * pre) * 0.3989422804014327

        blocks(body)

    def back_hidden(i):
        def body(g, part):
            d_act = dot(cbuf[g // 2, lax.rem(g, 2)], flat(w[2 + i], 0, half), 1, 0)
            value = (d_act * slope[part, i * half : (i + 1) * half]).astype(BF16)
            du[i][part] = value
            sm_s[0, 6:7, i * half : (i + 1) * half] += col_sum(value.astype(F32))

        blocks(body)

    def col_sum(values):
        return jnp.sum(values, axis=0, keepdims=True)

    def early():
        sm_s[0] = jnp.zeros(sm_s.shape[1:], F32)
        sm_s[0, 4:5, :width] = col_sum(cot_ref_v().astype(F32))

        def body(g, part):
            mine[0, g] = dot(att[part], outw[...], 1, 1)
            grads = dqkv[part]
            dn1 = dot(grads, flat(w_a, 0, S.qkv), 1, 1)
            mine[1, g] = dn1 * prm_ref[0:1]
            sm_s[0, 0:1, :width] += col_sum(dn1 * unit[part])
            sm_s[0, 1:2, :width] += col_sum(dn1)
            sm_s[0, 5:6, : S.qkv] += col_sum(grads.astype(F32))

        blocks(body)

    def cot_ref_v():
        return cbuf[y, x]

    def mixed():
        def body(g, part):
            value = mine[0, g]
            for i in range(2):
                columns = act[part, i * half : (i + 1) * half]
                value = value + dot(columns, flat(w[2 + i], 0, half), 1, 1)
            mine[0, g] = value
            mix_s[0, g // 2, lax.rem(g, 2)] = value.astype(BF16)

        blocks(body)

    def backward():
        def body(g, part):
            dn2 = dot(du[0][part], flat(w_u, 0, half), 1, 1)
            dn2 = dn2 + dot(du[1][part], flat(w_u, half, S.up), 1, 1)
            value = mine[1, g] + dn2 * prm_ref[2:3]
            mine[1, g] = value
            mix_s[1, g // 2, lax.rem(g, 2)] = value.astype(BF16)
            sm_s[0, 2:3, :width] += col_sum(dn2 * unit[part])
            sm_s[0, 3:4, :width] += col_sum(dn2)

        blocks(body)

    def sib_copy(k):
        return rcopy(sb[k], rb[k], ss_s.at[k], ss_r.at[k], sibling)

    def place(zz, yy, cc):
        return pl.ds(pl.multiple_of(((zz * 2 + yy) * 2 + cc) * rows, 16), rows)

    def to_sibling(k):
        @pl.loop(0, n)
        def _(zz):
            for yy in range(2):
                sb[k][zz, yy] = grad[k][place(zz, yy, 1 - core)].astype(BF16)

        sib_copy(k).start()

    def passing(k, way, target):
        return rcopy(
            cs[k].at[target],
            ci[k].at[way, target],
            sc_s.at[k, way, target],
            sc_r.at[k, way, target],
            up if way == 0 else down,
        )

    def summed(k, target, yy):
        return grad[k][place(target, yy, core)] + rb[k][target, yy].astype(F32)

    def tick(k, step):
        back = last - step
        if step == 0:
            sib_copy(k).wait_recv()

        def pass_on(way, target, more):
            @pl.when(more)
            def _():
                passing(k, way, target).wait_recv()
                for yy in range(2):
                    total = summed(k, target, yy) + ci[k][way, target, yy].astype(F32)
                    cs[k][target, yy] = total.astype(BF16)

            @pl.when(jnp.logical_not(more))
            def _():
                for yy in range(2):
                    cs[k][target, yy] = summed(k, target, yy).astype(BF16)

            passing(k, way, target).start()

        pl.when(z <= step)(lambda: pass_on(0, z + back, z > 0))
        pl.when(z >= back)(lambda: pass_on(1, z - back, z < last))

    def last_y(k):
        return rcopy(ysb[k], yrb[k], sy_s.at[k], sy_r.at[k], ypeer)

    def final(k):
        pl.when(z > 0)(lambda: passing(k, 0, z).wait_recv())
        pl.when(z < last)(lambda: passing(k, 1, z).wait_recv())

        def total(yy):
            value = summed(k, z, yy)
            low = jnp.where(z > 0, ci[k][0, z, yy].astype(F32), 0.0)
            high = jnp.where(z < last, ci[k][1, z, yy].astype(F32), 0.0)
            return value + low + high

        ysb[k][...] = total(1 - y).astype(BF16)
        last_y(k).start()
        red[k][y] = total(y)

    def final_recv(k):
        last_y(k).wait_recv()
        red[k][1 - y] = yrb[k][...].astype(F32)

    left, right = pl.ds(0, width // 2), pl.ds(width // 2, width // 2)

    def mix_copy(kind, slot):
        src, where = (
            (mix_s.at[kind, :, 1 - x, :, left], across),
            (mix_s.at[kind, 1 - y, :, :, right], ypeer),
            (mix_t.at[kind, 0], ypeer),
            (mix_t.at[kind, 1], across),
        )[slot]
        dst = mix_r.at[kind, slot] if slot < 2 else mix_u.at[kind, slot - 2]
        return rcopy(src, dst, mx_s.at[kind, slot], mx_r.at[kind, slot], where)

    def mix_send(kind):
        begin(mix_copy(kind, 0))
        begin(mix_copy(kind, 1))

    def mix_pass(kind):
        mix_copy(kind, 0).wait_recv()
        first = mine[kind, (1 - y) * 2 + x, :, : width // 2] + mix_r[kind, 0, 1 - y].astype(F32)
        mix_t[kind, 0] = first.astype(BF16)
        begin(mix_copy(kind, 2))
        mix_copy(kind, 1).wait_recv()
        second = mine[kind, y * 2 + 1 - x, :, width // 2 :] + mix_r[kind, 1, 1 - x].astype(F32)
        mix_t[kind, 1] = second.astype(BF16)
        begin(mix_copy(kind, 3))

    def mix_recv(kind):
        target = (hs_ref, bs_ref)[kind]
        for slot, near in ((0, y), (1, x)):
            mix_copy(kind, 2 + slot).wait_recv()
            columns = slice(slot * (width // 2), (slot + 1) * (width // 2))
            target[:, columns] = (
                mine[kind, y * 2 + x, :, columns]
                + mix_r[kind, slot, near].astype(F32)
                + mix_u[kind, slot].astype(F32)
            )

    def z_copy(step):
        where = at(lax.rem(z + step, n), y, core, x)
        return rcopy(sm_s.at[0], sm_z.at[step - 1], sz_s.at[step - 1], sz_r.at[step - 1], where)

    def small_copy(i, where):
        return rcopy(sm_s.at[i + 1], sm_r.at[i], st_s.at[i], st_r.at[i], where)

    def small_start():
        for step in range(1, n):
            begin(z_copy(step))

    def small_z():
        value = sm_s[0]
        for step in range(1, n):
            z_copy(step).wait_recv()
            value = value + sm_z[step - 1]
        sm_s[1] = value
        begin(small_copy(0, sibling))

    def small_pair():
        small_copy(0, sibling).wait_recv()
        sm_s[2] = sm_s[1] + sm_r[0]
        begin(small_copy(1, ypeer))

    def small_y():
        small_copy(1, ypeer).wait_recv()
        sm_s[3] = sm_s[2] + sm_r[1]
        begin(small_copy(2, across))
        mine_is = z // (n // 2) == y
        small_ref[0] = jnp.where(mine_is, sm_s[2], sm_r[1])

    def small_x():
        small_copy(2, across).wait_recv()
        small_ref[1] = sm_s[3] + sm_r[2]

    def attend_pair(i):
        attend(i // S.heads, i % S.heads)

    send_y(0)
    send_rows(0)
    start_own(0)
    start_own(1)
    send_y(1)
    relay(0, 0)
    params_send()
    relay(1, 0)
    pass_rows(0)
    relay(0, 1)
    send_rows(1)
    tables()
    relay(1, 1)
    params_fan_out()
    start_own(2)
    relay(1, 2)
    send_y(3)
    have_rows(0)
    relay(0, 2)
    units()
    gathered(1)
    send_y(2)
    gathered(0)
    params()
    norms()
    relay(2, 0)
    pass_rows(1)
    project()
    start_own(4)
    norms_turned()
    have_rows(1)
    relay(2, 1)
    project_back()
    attend_pair(0)
    attend_pair(1)
    attend_pair(2)
    turn_cot()
    relay(2, 2)
    start_own(3)
    attend_pair(3)
    relay(4, 0)
    gathered(2)
    hidden()
    weight_grad(ct, act, grad[1], 0)
    to_sibling(1)
    relay(4, 1)
    relay(3, 0)
    attend_pair(4)
    attend_pair(5)
    tick(1, 0)
    weight_grad(ct, att, grad[0], S.qkv)
    weight_grad(n1t, dqkv, grad[0], 0)
    to_sibling(0)
    relay(3, 1)
    tick(1, 1)
    relay(4, 2)
    early()
    tick(0, 0)
    relay(3, 2)
    gathered(4)
    back_hidden(1)
    weight_grad(n2t, du[1], grad[3], 0)
    gathered(3)
    back_hidden(0)
    tick(1, 2)
    to_sibling(3)
    mixed()
    mix_send(0)
    tick(0, 1)
    weight_grad(n2t, du[0], grad[2], 0)
    backward()
    to_sibling(2)
    tick(3, 0)
    small_start()
    mix_send(1)
    tick(2, 0)
    tick(3, 1)
    mix_pass(0)
    final(1)
    tick(2, 1)
    tick(0, 2)
    small_z()
    mix_pass(1)
    tick(3, 2)
    tick(2, 2)
    small_pair()
    final(0)
    final(3)
    final(2)
    small_y()
    final_recv(1)
    mix_recv(0)
    mix_recv(1)
    final_recv(3)
    final_recv(0)
    final_recv(2)
    small_x()

    for copy in sends:
        copy.wait_send()
    for k in range(5):
        for step in range(last):
            for way in range(2):
                there, copy = chain_copy(k, way, step)
                pl.when(there)(lambda: copy().wait_send())
        for block in range(n):
            fan_copy(k, block).wait_send()
    for k in range(4):
        sib_copy(k).wait_send()
        last_y(k).wait_send()
        for step in range(last):
            back = last - step
            pl.when(z <= step)(lambda: passing(k, 0, z + back).wait_send())
            pl.when(z >= back)(lambda: passing(k, 1, z - back).wait_send())


def fused(S, operands):
    dma = pltpu.SemaphoreType.DMA
    full = pl.BlockSpec(memory_space=VMEM)
    hbm = pl.BlockSpec(memory_space=pltpu.HBM)
    n, rows, own, width, T = S.n, S.rows, S.own, S.width, S.tokens
    shape = jax.ShapeDtypeStruct
    grads = [VMEM((width, c), F32) for c in S.gcols]
    parts = [VMEM((n, 2, rows, c), BF16) for c in S.gcols]
    ways = [VMEM((2, n, 2, rows, c), BF16) for c in S.gcols]
    lines = [VMEM((rows, c), BF16) for c in S.gcols]
    head = VMEM((S.heads, T, HEAD), BF16)
    scratch = [
        VMEM((2, rows, S.cols[0]), BF16),
        VMEM((rows, 2 * S.qkv), BF16),
        VMEM((rows, 2 * S.out), BF16),
    ]
    scratch += [VMEM((n, 2, 2, rows, c), BF16) for c in S.cols]
    scratch += [
        VMEM((2, 2, own, width), BF16),
        VMEM((2, 2, own, width), BF16),
        VMEM((2, 8, S.seq), F32),
        VMEM((16, 128), F32),
        VMEM((16, S.up), F32),
        VMEM((T, width), F32),
        VMEM((T, width), BF16),
        VMEM((T, width), BF16),
        VMEM((2, S.seq, S.seq), F32),
        VMEM((T, 128), F32),
        VMEM((T, 128), F32),
        VMEM((n, 2, 2, 16, 128), BF16),
        VMEM((width, T), BF16),
        VMEM((width, T), F32),
        VMEM((width, T), BF16),
        VMEM((width, T), BF16),
        VMEM((own, S.qkv), F32),
        head,
        head,
        head,
        head,
        VMEM((T, S.out), BF16),
        VMEM((T, 128), F32),
        VMEM((T, S.qkv), BF16),
        VMEM((width, S.out), BF16),
        VMEM((T, S.up), BF16),
        VMEM((T, S.up), F32),
        VMEM((T, S.up // 2), BF16),
        VMEM((T, S.up // 2), BF16),
    ]
    scratch += grads + parts + parts + parts + ways + lines + lines
    scratch += [
        VMEM((2, 4, own, width), F32),
        VMEM((2, 2, 2, own, width), BF16),
        VMEM((2, 2, 2, own, width // 2), BF16),
        VMEM((2, 2, own, width // 2), BF16),
        VMEM((2, 2, own, width // 2), BF16),
        VMEM((4, 8, S.up), F32),
        VMEM((n - 1, 8, S.up), F32),
        VMEM((3, 8, S.up), F32),
        dma((7,)),
        dma((4,)),
        dma((4,)),
        dma((5, 2, n)),
        dma((5, 2, n)),
        dma((5, n)),
        dma((5, n)),
        dma((2, 4)),
        dma((2, 4)),
        dma,
        dma,
        dma((4,)),
        dma((4,)),
        dma((4, 2, n)),
        dma((4, 2, n)),
        dma((4,)),
        dma((4,)),
        dma((2, 4)),
        dma((2, 4)),
        dma((3,)),
        dma((3,)),
        dma((n - 1,)),
        dma((n - 1,)),
        dma,
        dma,
        dma((n - 1,)),
        dma((n - 1,)),
        dma,
        dma,
    ]
    return pl.pallas_call(
        functools.partial(fused_kernel, S),
        out_shape=tuple(shape((2, rows, c), F32) for c in S.gcols)
        + (
            shape((own, width), F32),
            shape((own, width), F32),
            shape((2, 8, S.up), F32),
            shape((8, width), F32),
        ),
        in_specs=[hbm, hbm, full] + [hbm] * 4 + [full] * 8,
        out_specs=(full,) * 8,
        scratch_shapes=scratch,
        compiler_params=pltpu.CompilerParams(
            collective_id=2, has_side_effects=True, vmem_limit_bytes=60 * 2**20
        ),
        name="fused",
    )(*operands)


def finish_kernel(
    S,
    red_a,
    red_d,
    red_u,
    red_v,
    hs_ref,
    bs_ref,
    small_ref,
    prm_ref,
    tok_ref,
    cot_ref,
    hid_out,
    inp_out,
    qkv_out,
    qkvb_out,
    outw_out,
    g_out,
    up_out,
    upb_out,
    down_out,
    n1g_out,
    n1b_out,
    n2g_out,
    n2b_out,
    again_out,
):
    dp = lax.axis_index("dp")
    rows, width = S.rows, S.width
    for q in range(2):
        qkv_out[:, q * S.qkv : (q + 1) * S.qkv] = red_a[q, :, : S.qkv]
        middle = q * S.up + S.up // 2
        up_out[:, q * S.up : middle] = red_u[q]
        up_out[:, middle : (q + 1) * S.up] = red_v[q]
        outw_out[:, q * S.out : (q + 1) * S.out] = red_a[q, :, S.qkv : S.att]
        down_out[:, q * S.up : (q + 1) * S.up] = red_d[q]
    values = tok_ref[...].astype(F32)
    unit, inv_std = unit_rows(values)
    hid_out[...] = (values + hs_ref[...] + prm_ref[4:5] + prm_ref[5:6]).astype(BF16)
    total = bs_ref[...]
    mean_term = jnp.mean(total, axis=-1, keepdims=True)
    proj_term = jnp.mean(total * unit, axis=-1, keepdims=True)
    inp_out[...] = cot_ref[...].astype(F32) + inv_std * (total - mean_term - unit * proj_term)

    def shift(block, by):
        return pltpu.roll(block, lax.rem(S.up - by, S.up), 1)

    low = shift(small_ref[1], dp * rows)
    for row, out in enumerate((n1g_out, n1b_out, n2g_out, n2b_out, g_out)):
        out[...] = low[row : row + 1, :rows]
    again_out[...] = low[4:5, :rows]
    place = lax.rem(dp, 2 * S.n)
    own_sums = small_ref[0]
    both = [jnp.broadcast_to(own_sums[i : i + 1], (8, S.up)) for i in (5, 6)]
    qkvb_out[...] = shift(both[0], place * S.qkvb)[0:1, : S.qkvb]
    upb_out[...] = shift(both[1], place * S.upb)[0:1, : S.upb]


def finish(S, operands):
    shape = jax.ShapeDtypeStruct
    row = shape((1, S.rows), F32)
    return pl.pallas_call(
        functools.partial(finish_kernel, S),
        out_shape=(
            shape((S.own, S.width), BF16),
            shape((S.own, S.width), F32),
            shape((S.rows, 2 * S.qkv), F32),
            shape((1, S.qkvb), F32),
            shape((S.rows, 2 * S.out), F32),
            row,
            shape((S.rows, 2 * S.up), F32),
            shape((1, S.upb), F32),
            shape((S.rows, 2 * S.up), F32),
            row,
            row,
            row,
            row,
            row,
        ),
        compiler_params=pltpu.CompilerParams(vmem_limit_bytes=60 * 2**20),
        name="finish",
    )(*operands)


def on_plane(S, args):
    (tokens, segments, positions, cotangent, qkv_weight, qkv_bias, out_weight, out_bias) = args[:8]
    (up_weight, up_bias, down_weight, down_bias, g1, b1, g2, b2) = args[8:]
    made = fused(
        S,
        (
            tokens,
            cotangent,
            positions.reshape(1, -1),
            qkv_weight[0],
            out_weight[0].T,
            up_weight[0],
            down_weight[0].T,
            g1,
            b1,
            g2,
            b2,
            out_bias,
            down_bias,
            qkv_bias,
            up_bias,
        ),
    )
    outs = finish(S, tuple(made) + (tokens, cotangent))
    hid, inp, qkv, qkvb, outw, gsum, upw, upb, downw, n1g, n1b, n2g, n2b, gsum_again = outs
    return (
        hid[None],
        inp,
        qkv[None],
        qkvb,
        outw.T[None],
        gsum,
        upw[None],
        upb,
        downw.T[None],
        gsum_again,
        n1g,
        n1b,
        n2g,
        n2b,
    )


def on_device(
    tokens,
    segments,
    positions,
    cotangent,
    qkv_weight,
    qkv_bias,
    out_weight,
    out_bias,
    up_weight,
    up_bias,
    down_weight,
    down_bias,
    norm1_gain,
    norm1_bias,
    norm2_gain,
    norm2_bias,
):
    dp_size = lax.axis_size("dp")
    n_outer = dp_size // 4
    core = lax.rem(lax.axis_index("dp"), 2)
    x = lax.axis_index("tensor")
    own, width = tokens.shape
    rows = qkv_weight.shape[1]
    seq_len = segments.shape[0]
    plane = Shape(
        n_outer,
        rows,
        own,
        width,
        seq_len,
        qkv_weight.shape[2] // 2,
        out_weight.shape[1] // 2,
        up_weight.shape[2] // 2,
        qkv_bias.shape[1],
        up_bias.shape[1],
    )
    if plane.fits():
        return on_plane(
            plane,
            (
                tokens,
                segments,
                positions,
                cotangent,
                qkv_weight,
                qkv_bias,
                out_weight,
                out_bias,
                up_weight,
                up_bias,
                down_weight,
                down_bias,
                norm1_gain,
                norm1_bias,
                norm2_gain,
                norm2_bias,
            ),
        )
    qkv_q, up_q, out_q = (
        qkv_weight.shape[2] // 2,
        up_weight.shape[2] // 2,
        out_weight.shape[1] // 2,
    )
    sizes = Sizes(rows, up_q, qkv_q, out_q, qkv_bias.shape[1], up_bias.shape[1])
    heads = out_q // HEAD

    def halves(w):
        return jnp.swapaxes(w.reshape(rows, 2, -1), 0, 1)

    def halves_t(w):
        return jnp.swapaxes(w.reshape(2, -1, rows), 1, 2)

    small = jnp.concatenate(
        [
            jnp.stack(
                [
                    norm1_gain[0],
                    norm1_bias[0],
                    norm2_gain[0],
                    norm2_bias[0],
                    out_bias[0],
                    down_bias[0],
                ],
                axis=1,
            ),
            fold(qkv_bias[0], 1, rows, sizes.qb_cols)[0],
            fold(up_bias[0], 1, rows, sizes.ub_cols)[0],
        ],
        axis=1,
    )
    packed = sizes.pack(
        halves(up_weight[0]),
        halves_t(down_weight[0]),
        halves(qkv_weight[0]),
        jnp.broadcast_to(small[None], (2,) + small.shape),
        halves_t(out_weight[0]),
    )
    own_pos = lax.dynamic_slice_in_dim(positions, x * own, own, 0).astype(BF16)
    rows_in = jnp.concatenate(
        [tokens, cotangent, jnp.pad(own_pos[:, None], ((0, 0), (0, 127)))], axis=1
    )
    gathered, group_rows = gather(sizes, n_outer, packed, rows_in)

    flat = gathered.reshape(dp_size * rows, sizes.cols)
    up_w = flat[:, :up_q]
    down_wt = flat[:, up_q : 2 * up_q]
    qkv_w = flat[:, sizes.qkv : sizes.qkv + qkv_q]
    out_wt = flat[:, sizes.out : sizes.out + out_q]
    smalls = flat[:, sizes.small : sizes.small + sizes.n_small].astype(F32)
    vecs = smalls[:, :6].T
    by_dev = smalls.reshape(dp_size, rows, sizes.n_small)
    qb = by_dev[:, :, 6 : 6 + sizes.qb_cols].reshape(dp_size, -1)[:, : sizes.qkvb].reshape(-1)
    ub = by_dev[:, :, 6 + sizes.qb_cols :].reshape(dp_size, -1)[:, : sizes.upb].reshape(-1)
    qkv_b = lax.dynamic_slice_in_dim(qb, core * qkv_q, qkv_q, 0)
    up_b = lax.dynamic_slice_in_dim(ub, core * up_q, up_q, 0)

    group_rows = group_rows.reshape(4 * own, -1)
    count = 4 * own
    seqs = count // seq_len
    xs = group_rows[:, :width].astype(F32)
    cot = group_rows[:, width : 2 * width]
    pos = group_rows[:, 2 * width].astype(F32).reshape(seqs, seq_len)
    cos_tab, sin_tab = rotary_tables(pos)
    query_index = jnp.arange(seq_len, dtype=F32)
    key_index = query_index[None, None, :]
    first_key = query_index[None, :] - pos
    allowed = (
        (key_index <= query_index[None, :, None]) & (key_index >= first_key[:, :, None])
    )[:, None]

    unit, _ = unit_rows(xs)
    n1 = (unit * vecs[0] + vecs[1]).astype(BF16)
    n2 = (unit * vecs[2] + vecs[3]).astype(BF16)
    projected = (dot(n1, qkv_w, 1, 0) + qkv_b).reshape(seqs, seq_len, heads, 3, HEAD)
    projected = jnp.transpose(projected, (3, 0, 2, 1, 4))
    query = rotate(projected[0], cos_tab, sin_tab).astype(BF16)
    key = rotate(projected[1], cos_tab, sin_tab).astype(BF16)
    value = projected[2].astype(BF16)
    scale = HEAD ** (-0.5)

    def ein(spec, a, b):
        return jnp.einsum(spec, a, b, preferred_element_type=F32)

    scores = jnp.where(allowed, ein("shqd,shkd->shqk", query, key) * scale, -jnp.inf)
    peak = jnp.max(scores, axis=-1, keepdims=True)
    log_total = peak + jnp.log(jnp.sum(jnp.exp(scores - peak), axis=-1, keepdims=True))
    weights = jnp.exp(scores - log_total)
    weights_bf = weights.astype(BF16)
    attended = ein("shqk,shkd->shqd", weights_bf, value).astype(BF16)
    attended_flat = jnp.swapaxes(attended, 1, 2).reshape(count, out_q)
    pre = dot(n2, up_w, 1, 0) + up_b
    cumul = 0.5 * (1.0 + jax.scipy.special.erf(pre * 0.7071067811865476))
    act = (pre * cumul).astype(BF16)
    slope = cumul + pre * jnp.exp(-0.5 * pre * pre) * 0.3989422804014327
    mixed = dot(attended_flat, out_wt, 1, 1) + dot(act, down_wt, 1, 1)

    du = (dot(cot, down_wt, 1, 0) * slope).astype(BF16)
    g_upb = jnp.sum(du.astype(F32), axis=0)
    dn2 = dot(du, up_w, 1, 1)
    d_att = dot(cot, out_wt, 1, 0).astype(BF16).reshape(seqs, seq_len, heads, HEAD)
    d_att = jnp.swapaxes(d_att, 1, 2)
    delta = jnp.sum(attended.astype(F32) * d_att.astype(F32), axis=-1, keepdims=True)
    d_value = ein("shqk,shqd->shkd", weights_bf, d_att)
    d_weight = ein("shqd,shkd->shqk", d_att, value)
    d_score = (weights * (d_weight - delta) * scale).astype(BF16)
    d_query = unrotate(ein("shqk,shkd->shqd", d_score, key), cos_tab, sin_tab)
    d_key = unrotate(ein("shqk,shqd->shkd", d_score, query), cos_tab, sin_tab)
    d_qkv = jnp.stack([d_query, d_key, d_value], axis=0).astype(BF16)
    d_qkv = jnp.transpose(d_qkv, (1, 3, 2, 0, 4)).reshape(count, qkv_q)
    g_qkvb = jnp.sum(d_qkv.astype(F32), axis=0)
    dn1 = dot(d_qkv, qkv_w, 1, 1)
    back = dn1 * vecs[0] + dn2 * vecs[2]
    up_rows = cotangent.astype(F32)
    norm_rows = jnp.stack(
        [
            jnp.sum(dn1 * unit, axis=0),
            jnp.sum(dn1, axis=0),
            jnp.sum(dn2 * unit, axis=0),
            jnp.sum(dn2, axis=0),
            jnp.sum(up_rows, axis=0),
            jnp.zeros((width,), F32),
        ],
        axis=1,
    ).reshape(dp_size, rows, 6)
    own_half = jnp.arange(2)[:, None] == core
    qb_full = jnp.where(own_half, g_qkvb[None], 0.0).reshape(-1)
    ub_full = jnp.where(own_half, g_upb[None], 0.0).reshape(-1)
    small_grads = jnp.concatenate(
        [
            norm_rows,
            fold(qb_full, dp_size, rows, sizes.qb_cols),
            fold(ub_full, dp_size, rows, sizes.ub_cols),
        ],
        axis=2,
    )
    small_grads = jnp.pad(
        small_grads,
        (
            (0, 0),
            (0, 0),
            (sizes.small - sizes.tile, sizes.tile_end - sizes.small - sizes.n_small),
        ),
    ).reshape(dp_size // 2, 2, rows, -1)

    def turned(values):
        return values.T.reshape(dp_size // 2, 2, rows, count)

    operands = (
        turned(n2),
        turned(cot),
        turned(n1),
        du,
        act,
        jnp.pad(d_qkv, ((0, 0), (0, sizes.out - sizes.small))),
        attended_flat,
        small_grads,
    )
    reduced, mixed_sum, total, small_sum = scatter(
        sizes,
        n_outer,
        operands,
        mixed.astype(BF16).reshape(2, 2, own, width),
        back.astype(BF16).reshape(2, 2, own, width),
    )

    own_x = tokens.astype(F32)
    own_unit, own_inv = unit_rows(own_x)
    hidden = (own_x + mixed_sum + vecs[4] + vecs[5]).astype(BF16)
    mean_term = jnp.mean(total, axis=-1, keepdims=True)
    proj_term = jnp.mean(total * own_unit, axis=-1, keepdims=True)
    input_grad = up_rows + own_inv * (total - mean_term - own_unit * proj_term)

    def columns(start, size):
        return jnp.swapaxes(reduced[:, :, start : start + size], 0, 1).reshape(rows, 2 * size)

    def columns_t(start, size):
        return jnp.swapaxes(reduced[:, :, start : start + size], 1, 2).reshape(2 * size, rows)

    off = sizes.small - sizes.tile
    fin = small_sum[1, :, off : off + 6].T
    qb_out = small_sum[0, :, off + 6 : off + 6 + sizes.qb_cols].reshape(-1)[: sizes.qkvb]
    ub_at = off + 6 + sizes.qb_cols
    ub_out = small_sum[0, :, ub_at : ub_at + sizes.ub_cols].reshape(-1)[: sizes.upb]
    return (
        hidden[None],
        input_grad,
        columns(sizes.qkv, qkv_q)[None],
        qb_out[None],
        columns_t(sizes.out, out_q)[None],
        fin[4][None],
        columns(0, up_q)[None],
        ub_out[None],
        columns_t(sizes.down, up_q)[None],
        fin[4][None],
        fin[0][None],
        fin[1][None],
        fin[2][None],
        fin[3][None],
    )


def solution(mesh):
    in_specs = (
        P(("dp", "tensor"), None),
        P("dp"),
        P("dp"),
        P(("dp", "tensor"), None),
        P(None, "dp", "tensor"),
        P(None, ("tensor", "dp")),
        P(None, "tensor", "dp"),
        P(None, "dp"),
        P(None, "dp", "tensor"),
        P(None, ("tensor", "dp")),
        P(None, "tensor", "dp"),
        P(None, "dp"),
        P(None, "dp"),
        P(None, "dp"),
        P(None, "dp"),
        P(None, "dp"),
    )
    out_specs = (
        P(None, ("dp", "tensor"), None),
        P(("dp", "tensor"), None),
        P(None, "dp", "tensor"),
        P(None, ("tensor", "dp")),
        P(None, "tensor", "dp"),
        P(None, "dp"),
        P(None, "dp", "tensor"),
        P(None, ("tensor", "dp")),
        P(None, "tensor", "dp"),
        P(None, "dp"),
        P(None, "dp"),
        P(None, "dp"),
        P(None, "dp"),
        P(None, "dp"),
    )
    return jax.shard_map(
        on_device, mesh=mesh, in_specs=in_specs, out_specs=out_specs, check_vma=False
    )
```

```python
import functools

import jax
import jax.numpy as jnp
from jax import lax
from jax.experimental import pallas as pl
from jax.experimental.pallas import tpu as pltpu
from jax.sharding import PartitionSpec as P

HEAD = 64
ROT = 16
EPS = 1e-05
F32 = jnp.float32
BF16 = jnp.bfloat16
VMEM = pltpu.VMEM


def up128(n):
    return -(-n // 128) * 128


class Sizes:
    def __init__(self, rows, up_q, qkv_q, out_q, qkvb, upb):
        self.rows, self.up_q, self.qkv_q, self.out_q = rows, up_q, qkv_q, out_q
        self.qkvb, self.upb = qkvb, upb
        self.qb_cols, self.ub_cols = -(-qkvb // rows), -(-upb // rows)
        self.down = up_q
        self.qkv = 2 * up_q
        self.small = self.qkv + qkv_q
        self.n_small = 6 + self.qb_cols + self.ub_cols
        self.out = up128(self.small + self.n_small)
        self.cols = up128(self.out + out_q)
        self.tile = self.small // 128 * 128
        self.tile_end = self.out

    def pack(self, up, down, qkv, small, out):
        lead = up.shape[:-1]
        gap = self.out - self.small - small.shape[-1]
        tail = self.cols - self.out - self.out_q
        parts = [up, down, qkv, small, jnp.zeros(lead + (gap,), BF16), out]
        if tail:
            parts.append(jnp.zeros(lead + (tail,), BF16))
        return jnp.concatenate([p.astype(BF16) for p in parts], axis=-1)


def places(n_outer):
    dp = lax.axis_index("dp")
    x = lax.axis_index("tensor")
    core = lax.rem(dp, 2)
    chip = dp // 2
    inner = lax.rem(chip, 2)
    outer = chip // 2
    return dp, x, core, chip, inner, outer


def dev(chip, core, x):
    return {"dp": chip * 2 + core, "tensor": x}


def greet(partners, outer, n_outer, up, down):
    barrier = pltpu.get_barrier_semaphore()

    def tell(partner):
        pl.semaphore_signal(
            barrier, inc=1, device_id=partner, device_id_type=pl.DeviceIdType.MESH
        )

    for partner in partners:
        tell(partner)
    pl.when(outer < n_outer - 1)(lambda: tell(up))
    pl.when(outer > 0)(lambda: tell(down))
    chained = jnp.minimum(outer, 1) + jnp.minimum(n_outer - 1 - outer, 1)
    pl.semaphore_wait(barrier, len(partners) + chained)


def rcopy(src, dst, send, recv, where):
    return pltpu.make_async_remote_copy(
        src_ref=src,
        dst_ref=dst,
        send_sem=send,
        recv_sem=recv,
        device_id=where,
        device_id_type=pl.DeviceIdType.MESH,
    )


def partner_list(n_outer):
    dp, x, core, chip, inner, outer = places(n_outer)
    sibling = dev(chip, 1 - core, x)
    across = dev(chip, core, 1 - x)
    diagonal = dev(chip, 1 - core, 1 - x)
    inner_peer = dev(outer * 2 + 1 - inner, core, x)
    up = dev((outer + 1) * 2 + inner, core, x)
    down = dev((outer - 1) * 2 + inner, core, x)
    return sibling, across, diagonal, inner_peer, up, down


def gather_kernel(
    n_outer, p_ref, a_ref, w_ref, t_ref, loc_sem, grp_s, grp_r, sib_s, sib_r, ch_s, ch_r, in_s, in_r
):
    dp, x, core, chip, inner, outer = places(n_outer)
    sibling, across, diagonal, inner_peer, up, down = partner_list(n_outer)
    own_w = pltpu.make_async_copy(p_ref.at[core], w_ref.at[chip, core], loc_sem.at[0])
    own_t = pltpu.make_async_copy(a_ref, t_ref.at[core, x], loc_sem.at[1])
    own_w.start()
    own_t.start()
    greet([sibling, across, diagonal, inner_peer], outer, n_outer, up, down)
    sib = rcopy(p_ref.at[1 - core], w_ref.at[chip, core], sib_s, sib_r, sibling)
    sib.start()
    own_w.wait()
    sib.wait_recv()
    last = n_outer - 1

    def chain(way, step):
        block = outer - step if way == 0 else outer + step
        there = (outer < last) & (block >= 0) if way == 0 else (outer > 0) & (block <= last)
        spot = w_ref.at[block * 2 + inner]
        where = up if way == 0 else down
        return there, lambda: rcopy(spot, spot, ch_s.at[way, step], ch_r.at[way, step], where)

    def arrival(way, step):
        block = outer - 1 - step if way == 0 else outer + 1 + step
        there = block >= 0 if way == 0 else block <= last
        spot = w_ref.at[block * 2 + inner]
        return there, lambda: rcopy(spot, spot, ch_s.at[way, step], ch_r.at[way, step], up)

    def forward(way, step, mine):
        block = outer - 1 - step if way == 0 else outer + 1 + step
        there = block >= 0 if way == 0 else block <= last
        spot = w_ref.at[block * 2 + (inner if mine else 1 - inner)]
        return there, lambda: rcopy(spot, spot, in_s.at[way, step], in_r.at[way, step], inner_peer)

    def act(pair, what):
        there, copy = pair
        pl.when(there)(lambda: what(copy()))

    def start(copy):
        copy.start()

    for way in range(2):
        act(chain(way, 0), start)
    own = w_ref.at[chip]
    mine = rcopy(own, own, in_s.at[0, last], in_r.at[0, last], inner_peer)
    mine.start()
    group = []
    for slot, where in enumerate((sibling, across, diagonal)):
        copy = rcopy(a_ref, t_ref.at[core, x], grp_s.at[slot], grp_r.at[slot], where)
        copy.start()
        group.append(copy)
    for step in range(last):
        for way in range(2):
            act(arrival(way, step), lambda copy: copy.wait_recv())
            if step + 1 < last:
                act(chain(way, step + 1), start)
            act(forward(way, step, True), start)
    for copy in group:
        copy.wait_recv()
    mine.wait_recv()
    for step in range(last):
        for way in range(2):
            act(forward(way, step, False), lambda copy: copy.wait_recv())
    own_t.wait()
    sib.wait_send()
    mine.wait_send()
    for copy in group:
        copy.wait_send()
    for step in range(last):
        for way in range(2):
            act(chain(way, step), lambda copy: copy.wait_send())
            act(forward(way, step, True), lambda copy: copy.wait_send())


def scatter_kernel(
    sizes,
    n_outer,
    n2t_ref,
    cott_ref,
    n1t_ref,
    du_ref,
    act_ref,
    dqkv_ref,
    att_ref,
    small_ref,
    h_ref,
    d_ref,
    r_ref,
    hs_ref,
    ds_ref,
    x_ref,
    first_buf,
    b1,
    send_buf,
    cbuf,
    acc,
    hr,
    small_out,
    small_in,
    grp_s,
    grp_r,
    in_s,
    in_r,
    ch_s,
    ch_r,
    sib_s,
    sib_r,
    sm_s,
    sm_r,
):
    dp, x, core, chip, inner, outer = places(n_outer)
    sibling, across, diagonal, inner_peer, up, down = partner_list(n_outer)
    last = n_outer - 1
    rows = sizes.rows
    lo, hi = sizes.tile, sizes.tile_end

    def block(target, put):
        def product(left, right):
            if rows % 16 == 0:
                lhs = left[target].reshape(2 * rows, -1)
                out = jnp.dot(lhs, right[...], preferred_element_type=F32)
                return out.reshape(2, rows, -1)
            return jnp.stack(
                [
                    jnp.dot(left[target, side], right[...], preferred_element_type=F32)
                    for side in range(2)
                ]
            )

        put(0, sizes.down, product(n2t_ref, du_ref))
        put(sizes.down, sizes.qkv, product(cott_ref, act_ref))
        part = product(n1t_ref, dqkv_ref)
        cut = lo - sizes.qkv
        put(sizes.qkv, lo, part[:, :, :cut])
        put(lo, hi, part[:, :, cut:] + small_ref[target])
        end = sizes.out + sizes.out_q
        put(sizes.out, end, product(cott_ref, att_ref))
        if end < sizes.cols:
            put(end, sizes.cols, jnp.zeros((2, rows, sizes.cols - end), F32))

    def to_acc(start, stop, value):
        acc[:, :, start:stop] = value

    greet([sibling, across, diagonal, inner_peer], outer, n_outer, up, down)
    group = []
    spots = ((sibling, 1 - core, x), (across, core, 1 - x), (diagonal, 1 - core, 1 - x))
    for slot, (where, to_core, to_x) in enumerate(spots):
        for kind, part in enumerate((h_ref, d_ref)):
            copy = rcopy(
                part.at[to_core, to_x],
                hr.at[kind, slot],
                grp_s.at[kind, slot],
                grp_r.at[kind, slot],
                where,
            )
            copy.start()
            group.append(copy)

    def in_order(what):
        @pl.loop(0, last)
        def _(tick):
            back = last - tick
            pl.when(outer <= tick)(lambda: what(0, outer + back))
            pl.when(outer >= back)(lambda: what(1, outer - back))

    def exchange(target):
        return rcopy(
            first_buf.at[target], b1.at[target], in_s.at[target], in_r.at[target], inner_peer
        )

    def passing(way, target):
        return rcopy(
            send_buf.at[target],
            cbuf.at[way, target],
            ch_s.at[way, target],
            ch_r.at[way, target],
            up if way == 0 else down,
        )

    def send_first(target):
        def put(start, stop, value):
            first_buf[target, :, :, start:stop] = value.astype(BF16)

        block(target * 2 + 1 - inner, put)
        exchange(target).start()

    def send_second(way, target):
        block(target * 2 + inner, to_acc)
        exchange(target).wait_recv()
        acc[...] += b1[target].astype(F32)
        started = outer > 0 if way == 0 else outer < last

        @pl.when(started)
        def _():
            passing(way, target).wait_recv()
            acc[...] += cbuf[way, target].astype(F32)

        send_buf[target] = acc[...].astype(BF16)
        passing(way, target).start()

    in_order(lambda way, target: send_first(target))
    send_first(outer)
    in_order(send_second)
    for copy in group:
        copy.wait_recv()
    for kind, (part, out) in enumerate(((h_ref, hs_ref), (d_ref, ds_ref))):
        out[...] = (
            part[core, x].astype(F32)
            + hr[kind, 0].astype(F32)
            + hr[kind, 1].astype(F32)
            + hr[kind, 2].astype(F32)
        )
    block(chip, to_acc)
    exchange(outer).wait_recv()
    acc[...] += b1[outer].astype(F32)
    for way in range(2):

        @pl.when(outer > 0 if way == 0 else outer < last)
        def _():
            passing(way, outer).wait_recv()
            acc[...] += cbuf[way, outer].astype(F32)

    sib = rcopy(acc.at[1 - core], r_ref.at[core], sib_s, sib_r, sibling)
    sib.start()
    r_ref[core] = acc[core]
    sib.wait_recv()
    small_out[...] = r_ref[0, :, lo:hi] + r_ref[1, :, lo:hi]
    small = rcopy(small_out, small_in, sm_s, sm_r, across)
    small.start()
    small.wait_recv()
    x_ref[0] = small_out[...]
    x_ref[1] = small_out[...] + small_in[...]
    sib.wait_send()
    small.wait_send()
    for copy in group:
        copy.wait_send()
    exchange(outer).wait_send()

    def sent(way, target):
        exchange(target).wait_send()
        passing(way, target).wait_send()

    in_order(sent)


def gather(sizes, n_outer, packed, rows):
    dma = pltpu.SemaphoreType.DMA
    full = pl.BlockSpec(memory_space=VMEM)
    return pl.pallas_call(
        functools.partial(gather_kernel, n_outer),
        out_shape=(
            jax.ShapeDtypeStruct((2 * n_outer, 2) + packed.shape[1:], BF16),
            jax.ShapeDtypeStruct((2, 2) + rows.shape, BF16),
        ),
        in_specs=[full, full],
        out_specs=(full, full),
        scratch_shapes=[
            dma((2,)),
            dma((3,)),
            dma((3,)),
            dma,
            dma,
            dma((2, n_outer)),
            dma((2, n_outer)),
            dma((2, n_outer)),
            dma((2, n_outer)),
        ],
        compiler_params=pltpu.CompilerParams(
            collective_id=0, has_side_effects=True, vmem_limit_bytes=60 * 2**20
        ),
        name="gather",
    )(packed, rows)


def scatter(sizes, n_outer, operands, mixed, back):
    dma = pltpu.SemaphoreType.DMA
    full = pl.BlockSpec(memory_space=VMEM)
    block = (2, sizes.rows, sizes.cols)
    width = sizes.tile_end - sizes.tile
    return pl.pallas_call(
        functools.partial(scatter_kernel, sizes, n_outer),
        out_shape=(
            jax.ShapeDtypeStruct(block, F32),
            jax.ShapeDtypeStruct(mixed.shape[2:], F32),
            jax.ShapeDtypeStruct(mixed.shape[2:], F32),
            jax.ShapeDtypeStruct((2, sizes.rows, width), F32),
        ),
        in_specs=[full] * (len(operands) + 2),
        out_specs=(full, full, full, full),
        scratch_shapes=[
            VMEM((n_outer,) + block, BF16),
            VMEM((n_outer,) + block, BF16),
            VMEM((n_outer,) + block, BF16),
            VMEM((2, n_outer) + block, BF16),
            VMEM(block, F32),
            VMEM((2, 3) + mixed.shape[2:], BF16),
            VMEM((sizes.rows, width), F32),
            VMEM((sizes.rows, width), F32),
            dma((2, 3)),
            dma((2, 3)),
            dma((n_outer,)),
            dma((n_outer,)),
            dma((2, n_outer)),
            dma((2, n_outer)),
            dma,
            dma,
            dma,
            dma,
        ],
        compiler_params=pltpu.CompilerParams(
            collective_id=1, has_side_effects=True, vmem_limit_bytes=60 * 2**20
        ),
        name="scatter",
    )(*operands, mixed, back)


def rotary_tables(pos_ids):
    half_rot = ROT // 2
    freq_index = jnp.arange(half_rot, dtype=F32)
    inverse = jnp.power(F32(10000.0), -2.0 * freq_index / ROT)
    angles = pos_ids[..., None] * inverse
    cos_tab = jnp.concatenate([jnp.cos(angles), jnp.cos(angles)], axis=-1)
    sin_tab = jnp.concatenate([jnp.sin(angles), jnp.sin(angles)], axis=-1)
    return (cos_tab[:, None], sin_tab[:, None])


def rotate(values, cos_tab, sin_tab):
    half_rot = ROT // 2
    rotary = values[..., :ROT]
    turned = jnp.concatenate([-rotary[..., half_rot:], rotary[..., :half_rot]], axis=-1)
    return jnp.concatenate([rotary * cos_tab + turned * sin_tab, values[..., ROT:]], axis=-1)


def unrotate(grad_vals, cos_tab, sin_tab):
    half_rot = ROT // 2
    rotary = grad_vals[..., :ROT]
    scaled = rotary * sin_tab
    back_part = jnp.concatenate([scaled[..., half_rot:], -scaled[..., :half_rot]], axis=-1)
    return jnp.concatenate([rotary * cos_tab + back_part, grad_vals[..., ROT:]], axis=-1)


def unit_rows(values):
    centre = values - jnp.mean(values, axis=-1, keepdims=True)
    inv_std = lax.rsqrt(jnp.mean(centre * centre, axis=-1, keepdims=True) + EPS)
    return centre * inv_std, inv_std


def dot(a, b, ca, cb):
    return lax.dot_general(a, b, (((ca,), (cb,)), ((), ())), preferred_element_type=F32)


def fold(vector, count, rows, cols):
    per = vector.shape[0] // count
    padded = jnp.pad(vector.reshape(count, per), ((0, 0), (0, rows * cols - per)))
    return padded.reshape(count, rows, cols)


CHAIN = 4


class Shape:
    def __init__(self, n, rows, own, width, seq, qkv, out, up, qkvb, upb):
        self.n, self.rows, self.own, self.width, self.seq = n, rows, own, width, seq
        self.qkv, self.out, self.up, self.qkvb, self.upb = qkv, out, up, qkvb, upb
        self.heads = out // HEAD
        self.att = qkv + out
        self.tokens = 4 * own
        self.cols = (self.att, up, up // 2, up // 2)
        self.gcols = (self.att, up, up // 2, up // 2)

    def fits(self):
        aligned = [self.own, self.width, self.seq, self.att, self.up]
        return (
            self.rows % 16 == 0
            and all(size % 128 == 0 for size in aligned)
            and self.up % 256 == 0
            and self.n == CHAIN
            and self.own * 2 == self.seq
            and self.att <= self.up
            and self.width <= self.up
            and max(self.rows, self.qkvb, self.upb) <= 128
            and self.n >= 2
            and (self.n * 4) * self.rows == self.width
        )


def fused_kernel(S, *refs):
    refs = list(refs)

    def take(count):
        got = refs[:count]
        del refs[:count]
        return got

    tok_ref, cot_ref, pos_ref, qkv_ref, out_ref, up_ref, down_ref = take(7)
    small_params = take(8)
    red = take(4)
    hs_ref, bs_ref, small_ref, prm_ref = take(4)
    pk, qkv_v, out_v = take(3)
    w = take(4)
    tbuf, cbuf, pbuf, smrow, bias, unit, n1, n2, mask, rot_c, rot_s = take(11)
    sbuf, ct, ut, n1t, n2t = take(5)
    proj, qh, kh, vh, doh, att, dqk, dqkv, outw, act, slope = take(11)
    du = take(2)
    grad, sb, rb, cs, ci, ysb, yrb = (take(4) for _ in range(7))
    mine, mix_s, mix_r, mix_t, mix_u, sm_s, sm_z, sm_r = take(8)
    ld, gy_s, gy_r, gc_s, gc_r, gf_s, gf_r, tk_s, tk_r, ps_s, ps_r = take(11)
    ss_s, ss_r, sc_s, sc_r, sy_s, sy_r, mx_s, mx_r, st_s, st_r, sz_s, sz_r = take(12)
    py_s, py_r, pz_s, pz_r, pf_s, pf_r = take(6)
    w_a, w_u = w[:2]
    n, rows, own, width = S.n, S.rows, S.own, S.width
    last = n - 1
    dp = lax.axis_index("dp")
    x = lax.axis_index("tensor")
    core = lax.rem(dp, 2)
    y = lax.rem(dp // 2, 2)
    z = dp // 4

    def at(zz, yy, cc, xx):
        return {"dp": zz * 4 + yy * 2 + cc, "tensor": xx}

    sibling = at(z, y, 1 - core, x)
    across = at(z, y, core, 1 - x)
    ypeer = at(z, 1 - y, core, x)
    up, down = at(z + 1, y, core, x), at(z - 1, y, core, x)
    sends = []

    def begin(copy):
        copy.start()
        sends.append(copy)
        return copy

    def iota(shape, axis):
        return lax.broadcasted_iota(jnp.int32, shape, axis)

    barrier = pltpu.get_barrier_semaphore()

    def tell(partner):
        pl.semaphore_signal(
            barrier, inc=1, device_id=partner, device_id_type=pl.DeviceIdType.MESH
        )

    for partner in (sibling, across, ypeer):
        tell(partner)
    for step in range(1, n):
        tell(at(lax.rem(z + step, n), y, core, x))
    def load(i, src, dst):
        copy = pltpu.make_async_copy(src, dst, ld.at[i])
        copy.start()
        return copy

    def cut(ref, start, size):
        return ref.at[:, pl.ds(pl.multiple_of(start, 128), size)]

    half = S.up // 2

    def part_of(k, q):
        if k == 0:
            return pk.at[q]
        if k == 1:
            return cut(up_ref, q * S.up, S.up)
        return cut(down_ref, q * S.up + (k - 2) * half, half)

    loads = [load(0, qkv_ref, qkv_v), load(1, out_ref, out_v)]
    own_loads = [load(1 + k, part_of(k, y), w[k].at[z, y, core]) for k in range(1, 4)]
    own_rows = [load(5, tok_ref, tbuf.at[y, x]), load(6, cot_ref, cbuf.at[y, x])]
    row_pos = pos_ref[...].astype(F32)
    pbuf[y] = jnp.broadcast_to(row_pos, pbuf.shape[1:])
    smrow[...] = jnp.zeros_like(smrow)
    for row, part in enumerate(small_params):
        smrow[row : row + 1, : part.shape[1]] = part[...].astype(F32)
    for copy in loads:
        copy.wait()
    for q in range(2):
        pk[q, :, : S.qkv] = qkv_v[:, q * S.qkv : (q + 1) * S.qkv]
        pk[q, :, S.qkv : S.att] = out_v[:, q * S.out : (q + 1) * S.out]
    w[0][z, y, core] = pk[y]
    sbuf[z, y, core] = smrow[...].astype(BF16)

    pl.semaphore_wait(barrier, 3 + last)

    def y_copy(k):
        return rcopy(part_of(k, 1 - y), w[k].at[z, y, core], gy_s.at[k], gy_r.at[k], ypeer)

    def spot_of(k, block):
        if k < 2:
            return w[0].at[block, y if k == 0 else 1 - y, core]
        return w[k - 1].at[block, :, core]

    def chain_copy(k, way, step):
        block = z - step if way == 0 else z + step
        there = (z < last) & (block >= 0) if way == 0 else (z > 0) & (block <= last)
        where = up if way == 0 else down

        def copy():
            spot = spot_of(k, block)
            return rcopy(spot, spot, gc_s.at[k, way, step], gc_r.at[k, way, step], where)

        return there, copy

    def fan_copy(k, block):
        spot = spot_of(k, block)
        return rcopy(spot, spot, gf_s.at[k, block], gf_r.at[k, block], sibling)

    def arrived(way, step):
        block = z - 1 - step if way == 0 else z + 1 + step
        return block, (block >= 0 if way == 0 else block <= last)

    def start_own(k):
        if k > 1:
            own_loads[k - 2].wait()
        if k:
            y_copy(k - 1).wait_recv()
        for way in range(2):
            there, copy = chain_copy(k, way, 0)
            pl.when(there)(lambda: copy().start())
        fan_copy(k, z).start()

    def relay(k, step):
        for way in range(2):
            block, there = arrived(way, step)

            @pl.when(there)
            def _():
                spot = spot_of(k, block)
                rcopy(spot, spot, gc_s.at[k, way, step], gc_r.at[k, way, step], up).wait_recv()

            if step + 1 < last:
                more, copy = chain_copy(k, way, step + 1)
                pl.when(more)(lambda: copy().start())
            pl.when(there)(lambda: fan_copy(k, block).start())

    def gathered(k):
        for block in range(n):
            if k < 2:
                spot = w[0].at[block, y if k == 0 else 1 - y, 1 - core]
            else:
                spot = w[k - 1].at[block, :, 1 - core]
            rcopy(spot, spot, gf_s.at[k, block], gf_r.at[k, block], sibling).wait_recv()

    def params_y():
        mine_spot = sbuf.at[z, y, core]
        return rcopy(mine_spot, mine_spot, py_s, py_r, ypeer)

    def params_z(step, block):
        spot = sbuf.at[block, :, core]
        where = at(lax.rem(z + step, n), y, core, x)
        return rcopy(spot, spot, pz_s.at[step - 1], pz_r.at[step - 1], where)

    def params_fan(which):
        spot = sbuf.at[:, :, which]
        return rcopy(spot, spot, pf_s, pf_r, sibling)

    def params_send():
        params_y().wait_recv()
        for step in range(1, n):
            begin(params_z(step, z))

    def params_fan_out():
        for step in range(1, n):
            params_z(step, lax.rem(z - step + n, n)).wait_recv()
        begin(params_fan(core))

    def send_y(k):
        begin(y_copy(k))

    low, high = pl.ds(0, own // 2), pl.ds(own // 2, own // 2)

    def row_copy(kind, slot):
        src, dst = ((tok_ref, tbuf), (cot_ref, cbuf))[kind]
        where = across if slot in (0, 3) else ypeer
        if slot == 2:
            src, dst = dst.at[y, 1 - x, low], dst.at[y, 1 - x, low]
        elif slot == 3:
            src, dst = dst.at[1 - y, x, high], dst.at[1 - y, x, high]
        else:
            dst = dst.at[y, x]
        return rcopy(src, dst, tk_s.at[kind, slot], tk_r.at[kind, slot], where)

    def send_rows(kind):
        begin(row_copy(kind, 0))
        begin(row_copy(kind, 1))

    def pass_rows(kind):
        row_copy(kind, 0).wait_recv()
        begin(row_copy(kind, 2))
        row_copy(kind, 1).wait_recv()
        begin(row_copy(kind, 3))

    def have_rows(kind):
        own_rows[kind].wait()
        row_copy(kind, 2).wait_recv()
        row_copy(kind, 3).wait_recv()

    begin(params_y())
    pos_copy = begin(rcopy(pbuf.at[y], pbuf.at[y], ps_s, ps_r, ypeer))

    lane = iota((own, 128), 1)
    spin = lax.rem(lane, HEAD)

    def tables():
        pos_copy.wait_recv()
        freq = jnp.zeros((1, 128), F32)
        which = lax.rem(iota((1, 128), 1), ROT // 2)
        for i in range(ROT // 2):
            freq = jnp.where(which == i, 10000.0 ** (-2.0 * i / ROT), freq)
        query = iota((S.seq, S.seq), 0).astype(F32)
        key = iota((S.seq, S.seq), 1).astype(F32)
        spin_s = lax.rem(iota((S.seq, 128), 1), HEAD)
        for s in range(2):
            line = jnp.where(query == key, pbuf[s, 0:1, :], 0.0)
            column = jnp.sum(line, axis=1, keepdims=True)
            seen = (key <= query) & (key >= query - column)
            mask[s] = jnp.where(seen, 0.0, -jnp.inf)
            angles = column * freq
            sines = jnp.sin(angles)
            rot_c[s * S.seq : (s + 1) * S.seq] = jnp.where(spin_s < ROT, jnp.cos(angles), 1.0)
            rot_s[s * S.seq : (s + 1) * S.seq] = jnp.where(
                spin_s < ROT // 2, -sines, jnp.where(spin_s < ROT, sines, 0.0)
            )

    def blocks(body):
        pl.loop(0, 4)(lambda g: body(g, pl.ds(pl.multiple_of(g * own, own), own)))

    def units():
        def body(g, part):
            value = unit_rows(tbuf[g // 2, lax.rem(g, 2)].astype(F32))[0]
            unit[part] = value
            ut[:, part] = value.T

        blocks(body)

    def turn_cot():
        def body(g, part):
            ct[:, part] = cbuf[g // 2, lax.rem(g, 2)].T

        blocks(body)

    def params():
        params_fan(1 - core).wait_recv()
        total = jnp.zeros((8, S.up), F32)
        for j in range(4 * n):
            piece = sbuf[j // 4, (j // 2) % 2, j % 2].astype(F32)[0:8]
            wide = jnp.concatenate([piece, jnp.zeros((8, S.up - 128), F32)], axis=1)
            total = total + (pltpu.roll(wide, j * rows, 1) if j else wide)
        prm_ref[...] = total[:, :width]
        q_total = jnp.zeros((8, S.up), F32)
        u_total = jnp.zeros((8, S.up), F32)
        for j in range(2 * n):
            there = y * (n // 2) + j // 4
            piece = sbuf[there, (j // 2) % 2, j % 2].astype(F32)[0:8]
            wide = jnp.concatenate([piece, jnp.zeros((8, S.up - 128), F32)], axis=1)
            q_total = q_total + (pltpu.roll(wide, j * S.qkvb, 1) if j else wide)
            u_total = u_total + (pltpu.roll(wide, j * S.upb, 1) if j else wide)
        bias[0:8] = q_total
        bias[8:16] = u_total

    def flat(ref, start, stop):
        return ref[:, :, :, :, start:stop].reshape(4 * n * rows, stop - start)

    def norms():
        sm_s[0] = jnp.zeros(sm_s.shape[1:], F32)

        def body(g, part):
            value = unit[part]
            n1[part] = (value * prm_ref[0:1] + prm_ref[1:2]).astype(BF16)
            n2[part] = (value * prm_ref[2:3] + prm_ref[3:4]).astype(BF16)

        blocks(body)

    def norms_turned():
        tall = jnp.concatenate([prm_ref[...], jnp.zeros((120, width), F32)], axis=0)
        tall = tall.T
        for i in range(width // 128):
            spot = slice(i * 128, (i + 1) * 128)
            value, param = ut[spot], tall[spot]
            n1t[spot] = (value * param[:, 0:1] + param[:, 1:2]).astype(BF16)
            n2t[spot] = (value * param[:, 2:3] + param[:, 3:4]).astype(BF16)

    def turn(values, part, sign):
        ahead, behind = pltpu.roll(values, 128 - ROT // 2, 1), pltpu.roll(values, ROT // 2, 1)
        other = jnp.where(spin < ROT // 2, ahead, behind) * rot_s[part]
        return values * rot_c[part] + (other if sign > 0 else -other)

    def project():
        outw[...] = flat(w_a, S.qkv, S.att)

        def body(g, part):
            proj[...] = dot(n1[part], flat(w_a, 0, S.qkv), 1, 0) + bias[6:7, : S.qkv]
            for h in range(S.heads):
                base = h * 3 * HEAD
                pair = turn(proj[:, base : base + 2 * HEAD], part, 1).astype(BF16)
                qh[h, part] = pair[:, :HEAD]
                kh[h, part] = pair[:, HEAD:]
                vh[h, part] = proj[:, base + 2 * HEAD : base + 3 * HEAD].astype(BF16)
        blocks(body)

    def project_back():
        def body(g, part):
            grads = dot(cbuf[g // 2, lax.rem(g, 2)], outw[...], 1, 0).astype(BF16)
            for h in range(S.heads):
                doh[h, part] = grads[:, h * HEAD : (h + 1) * HEAD]

        blocks(body)

    scale = HEAD ** (-0.5)

    def attend(s, h):
        part = slice(s * S.seq, (s + 1) * S.seq)
        q, k, v, dout = qh[h, part], kh[h, part], vh[h, part], doh[h, part]
        scores = dot(q, k, 1, 1) * scale + mask[s]
        raised = jnp.exp(scores - jnp.max(scores, axis=-1, keepdims=True))
        weights = raised * (1.0 / jnp.sum(raised, axis=-1, keepdims=True))
        weights_bf = weights.astype(BF16)
        got = dot(weights_bf, v, 1, 0).astype(BF16)
        att[part, h * HEAD : (h + 1) * HEAD] = got
        delta = jnp.sum(got.astype(F32) * dout.astype(F32), axis=-1, keepdims=True)
        d_score = (weights * (dot(dout, v, 1, 1) - delta) * scale).astype(BF16)
        dqk[part, :HEAD] = dot(d_score, k, 1, 0)
        dqk[part, HEAD:] = dot(d_score, q, 0, 0)
        base = h * 3 * HEAD
        dqkv[part, base + 2 * HEAD : base + 3 * HEAD] = dot(weights_bf, dout, 0, 0).astype(BF16)
        for half in range(2):
            piece = slice(s * S.seq + half * own, s * S.seq + (half + 1) * own)
            dqkv[piece, base : base + 2 * HEAD] = turn(dqk[piece], piece, -1).astype(BF16)

    def weight_grad(left, right, target, start):
        size = right.shape[1]

        @pl.loop(0, width // 128)
        def _(i):
            spot = pl.ds(pl.multiple_of(i * 128, 128), 128)
            target[spot, start : start + size] = dot(left[spot], right[...], 1, 0)

    def hidden():
        def body(g, part):
            pre = dot(n2[part], flat(w_u, 0, S.up), 1, 0) + bias[15:16, : S.up]
            cumul = 0.5 * (1.0 + lax.erf(pre * 0.7071067811865476))
            act[part] = (pre * cumul).astype(BF16)
            slope[part] = cumul + pre * jnp.exp(-0.5 * pre * pre) * 0.3989422804014327

        blocks(body)

    def back_hidden(i):
        def body(g, part):
            d_act = dot(cbuf[g // 2, lax.rem(g, 2)], flat(w[2 + i], 0, half), 1, 0)
            value = (d_act * slope[part, i * half : (i + 1) * half]).astype(BF16)
            du[i][part] = value
            sm_s[0, 6:7, i * half : (i + 1) * half] += col_sum(value.astype(F32))

        blocks(body)

    def col_sum(values):
        return jnp.sum(values, axis=0, keepdims=True)

    def early():
        sm_s[0, 4:5, :width] = col_sum(cot_ref_v().astype(F32))

        def body(g, part):
            mine[0, g] = dot(att[part], outw[...], 1, 1)
            grads = dqkv[part]
            dn1 = dot(grads, flat(w_a, 0, S.qkv), 1, 1)
            mine[1, g] = dn1 * prm_ref[0:1]
            sm_s[0, 0:1, :width] += col_sum(dn1 * unit[part])
            sm_s[0, 1:2, :width] += col_sum(dn1)
            sm_s[0, 5:6, : S.qkv] += col_sum(grads.astype(F32))

        blocks(body)

    def cot_ref_v():
        return cbuf[y, x]

    def mixed():
        def body(g, part):
            value = mine[0, g]
            for i in range(2):
                columns = act[part, i * half : (i + 1) * half]
                value = value + dot(columns, flat(w[2 + i], 0, half), 1, 1)
            mine[0, g] = value
            mix_s[0, g // 2, lax.rem(g, 2)] = value.astype(BF16)

        blocks(body)

    def backward():
        def body(g, part):
            dn2 = dot(du[0][part], flat(w_u, 0, half), 1, 1)
            dn2 = dn2 + dot(du[1][part], flat(w_u, half, S.up), 1, 1)
            value = mine[1, g] + dn2 * prm_ref[2:3]
            mine[1, g] = value
            mix_s[1, g // 2, lax.rem(g, 2)] = value.astype(BF16)
            sm_s[0, 2:3, :width] += col_sum(dn2 * unit[part])
            sm_s[0, 3:4, :width] += col_sum(dn2)

        blocks(body)

    def sib_copy(k):
        return rcopy(sb[k], rb[k], ss_s.at[k], ss_r.at[k], sibling)

    def place(zz, yy, cc):
        return pl.ds(pl.multiple_of(((zz * 2 + yy) * 2 + cc) * rows, 16), rows)

    def to_sibling(k):
        @pl.loop(0, n)
        def _(zz):
            for yy in range(2):
                sb[k][zz, yy] = grad[k][place(zz, yy, 1 - core)].astype(BF16)

        sib_copy(k).start()

    def passing(k, way, target, yy):
        return rcopy(
            cs[k].at[target, yy],
            ci[k].at[way, target, yy],
            sc_s.at[k, way, target, yy],
            sc_r.at[k, way, target, yy],
            up if way == 0 else down,
        )

    def summed(k, target, yy):
        return grad[k][place(target, yy, core)] + rb[k][target, yy].astype(F32)

    halves = (1 - y, y)

    def tick(k, step):
        back = last - step
        if step == 0:
            sib_copy(k).wait_recv()

        def pass_on(way, target, more):
            for yy in halves:

                @pl.when(more)
                def _():
                    passing(k, way, target, yy).wait_recv()
                    total = summed(k, target, yy) + ci[k][way, target, yy].astype(F32)
                    cs[k][target, yy] = total.astype(BF16)

                @pl.when(jnp.logical_not(more))
                def _():
                    cs[k][target, yy] = summed(k, target, yy).astype(BF16)

                passing(k, way, target, yy).start()

        pl.when(z <= step)(lambda: pass_on(0, z + back, z > 0))
        pl.when(z >= back)(lambda: pass_on(1, z - back, z < last))

    def last_y(k):
        return rcopy(ysb[k], yrb[k], sy_s.at[k], sy_r.at[k], ypeer)

    def final(k):
        def total(yy):
            pl.when(z > 0)(lambda: passing(k, 0, z, yy).wait_recv())
            pl.when(z < last)(lambda: passing(k, 1, z, yy).wait_recv())
            value = summed(k, z, yy)
            low = jnp.where(z > 0, ci[k][0, z, yy].astype(F32), 0.0)
            high = jnp.where(z < last, ci[k][1, z, yy].astype(F32), 0.0)
            return value + low + high

        ysb[k][...] = total(1 - y).astype(BF16)
        last_y(k).start()
        red[k][y] = total(y)

    def final_recv(k):
        last_y(k).wait_recv()
        red[k][1 - y] = yrb[k][...].astype(F32)

    left, right = pl.ds(0, width // 2), pl.ds(width // 2, width // 2)

    def mix_copy(kind, slot):
        src, where = (
            (mix_s.at[kind, :, 1 - x, :, left], across),
            (mix_s.at[kind, 1 - y, :, :, right], ypeer),
            (mix_t.at[kind, 0], ypeer),
            (mix_t.at[kind, 1], across),
        )[slot]
        dst = mix_r.at[kind, slot] if slot < 2 else mix_u.at[kind, slot - 2]
        return rcopy(src, dst, mx_s.at[kind, slot], mx_r.at[kind, slot], where)

    def mix_send(kind):
        begin(mix_copy(kind, 0))
        begin(mix_copy(kind, 1))

    def mix_pass(kind):
        mix_copy(kind, 0).wait_recv()
        first = mine[kind, (1 - y) * 2 + x, :, : width // 2] + mix_r[kind, 0, 1 - y].astype(F32)
        mix_t[kind, 0] = first.astype(BF16)
        begin(mix_copy(kind, 2))
        mix_copy(kind, 1).wait_recv()
        second = mine[kind, y * 2 + 1 - x, :, width // 2 :] + mix_r[kind, 1, 1 - x].astype(F32)
        mix_t[kind, 1] = second.astype(BF16)
        begin(mix_copy(kind, 3))

    def mix_recv(kind):
        target = (hs_ref, bs_ref)[kind]
        for slot, near in ((0, y), (1, x)):
            mix_copy(kind, 2 + slot).wait_recv()
            columns = slice(slot * (width // 2), (slot + 1) * (width // 2))
            target[:, columns] = (
                mine[kind, y * 2 + x, :, columns]
                + mix_r[kind, slot, near].astype(F32)
                + mix_u[kind, slot].astype(F32)
            )

    def z_copy(step):
        where = at(lax.rem(z + step, n), y, core, x)
        return rcopy(sm_s.at[0], sm_z.at[step - 1], sz_s.at[step - 1], sz_r.at[step - 1], where)

    def small_copy(i, where):
        return rcopy(sm_s.at[i + 1], sm_r.at[i], st_s.at[i], st_r.at[i], where)

    def small_start():
        for step in range(1, n):
            begin(z_copy(step))

    def small_z():
        value = sm_s[0]
        for step in range(1, n):
            z_copy(step).wait_recv()
            value = value + sm_z[step - 1]
        sm_s[1] = value
        begin(small_copy(0, sibling))

    def small_pair():
        small_copy(0, sibling).wait_recv()
        sm_s[2] = sm_s[1] + sm_r[0]
        begin(small_copy(1, ypeer))

    def small_y():
        small_copy(1, ypeer).wait_recv()
        sm_s[3] = sm_s[2] + sm_r[1]
        begin(small_copy(2, across))
        mine_is = z // (n // 2) == y
        small_ref[0] = jnp.where(mine_is, sm_s[2], sm_r[1])

    def small_x():
        small_copy(2, across).wait_recv()
        small_ref[1] = sm_s[3] + sm_r[2]

    def attend_pair(i):
        attend(i // S.heads, i % S.heads)

    send_y(0)
    send_rows(0)
    start_own(0)
    start_own(1)
    send_y(1)
    relay(0, 0)
    params_send()
    relay(1, 0)
    pass_rows(0)
    relay(0, 1)
    send_rows(1)
    tables()
    relay(1, 1)
    params_fan_out()
    start_own(2)
    relay(1, 2)
    send_y(3)
    have_rows(0)
    relay(0, 2)
    units()
    gathered(1)
    send_y(2)
    gathered(0)
    params()
    norms()
    relay(2, 0)
    pass_rows(1)
    project()
    start_own(4)
    norms_turned()
    have_rows(1)
    relay(2, 1)
    project_back()
    attend_pair(0)
    attend_pair(1)
    attend_pair(2)
    turn_cot()
    relay(2, 2)
    start_own(3)
    attend_pair(3)
    relay(4, 0)
    gathered(2)
    hidden()
    weight_grad(ct, act, grad[1], 0)
    to_sibling(1)
    relay(4, 1)
    relay(3, 0)
    attend_pair(4)
    attend_pair(5)
    tick(1, 0)
    weight_grad(ct, att, grad[0], S.qkv)
    weight_grad(n1t, dqkv, grad[0], 0)
    to_sibling(0)
    relay(3, 1)
    tick(1, 1)
    relay(4, 2)
    early()
    tick(0, 0)
    relay(3, 2)
    gathered(4)
    back_hidden(1)
    weight_grad(n2t, du[1], grad[3], 0)
    gathered(3)
    tick(1, 2)
    to_sibling(3)
    mixed()
    tick(3, 0)
    back_hidden(0)
    mix_send(0)
    tick(0, 1)
    weight_grad(n2t, du[0], grad[2], 0)
    backward()
    to_sibling(2)
    small_start()
    mix_send(1)
    tick(2, 0)
    tick(3, 1)
    mix_pass(0)
    final(1)
    tick(2, 1)
    tick(0, 2)
    small_z()
    mix_pass(1)
    tick(3, 2)
    tick(2, 2)
    small_pair()
    final(0)
    final(3)
    final(2)
    small_y()
    final_recv(1)
    mix_recv(0)
    mix_recv(1)
    final_recv(3)
    final_recv(0)
    final_recv(2)
    small_x()

    for copy in sends:
        copy.wait_send()
    for k in range(5):
        for step in range(last):
            for way in range(2):
                there, copy = chain_copy(k, way, step)
                pl.when(there)(lambda: copy().wait_send())
        for block in range(n):
            fan_copy(k, block).wait_send()
    for k in range(4):
        sib_copy(k).wait_send()
        last_y(k).wait_send()
        for step in range(last):
            back = last - step
            for yy in halves:
                pl.when(z <= step)(lambda: passing(k, 0, z + back, yy).wait_send())
                pl.when(z >= back)(lambda: passing(k, 1, z - back, yy).wait_send())


def fused(S, operands):
    dma = pltpu.SemaphoreType.DMA
    full = pl.BlockSpec(memory_space=VMEM)
    hbm = pl.BlockSpec(memory_space=pltpu.HBM)
    n, rows, own, width, T = S.n, S.rows, S.own, S.width, S.tokens
    shape = jax.ShapeDtypeStruct
    grads = [VMEM((width, c), F32) for c in S.gcols]
    parts = [VMEM((n, 2, rows, c), BF16) for c in S.gcols]
    ways = [VMEM((2, n, 2, rows, c), BF16) for c in S.gcols]
    lines = [VMEM((rows, c), BF16) for c in S.gcols]
    head = VMEM((S.heads, T, HEAD), BF16)
    scratch = [
        VMEM((2, rows, S.cols[0]), BF16),
        VMEM((rows, 2 * S.qkv), BF16),
        VMEM((rows, 2 * S.out), BF16),
    ]
    scratch += [VMEM((n, 2, 2, rows, c), BF16) for c in S.cols]
    scratch += [
        VMEM((2, 2, own, width), BF16),
        VMEM((2, 2, own, width), BF16),
        VMEM((2, 8, S.seq), F32),
        VMEM((16, 128), F32),
        VMEM((16, S.up), F32),
        VMEM((T, width), F32),
        VMEM((T, width), BF16),
        VMEM((T, width), BF16),
        VMEM((2, S.seq, S.seq), F32),
        VMEM((T, 128), F32),
        VMEM((T, 128), F32),
        VMEM((n, 2, 2, 16, 128), BF16),
        VMEM((width, T), BF16),
        VMEM((width, T), F32),
        VMEM((width, T), BF16),
        VMEM((width, T), BF16),
        VMEM((own, S.qkv), F32),
        head,
        head,
        head,
        head,
        VMEM((T, S.out), BF16),
        VMEM((T, 128), F32),
        VMEM((T, S.qkv), BF16),
        VMEM((width, S.out), BF16),
        VMEM((T, S.up), BF16),
        VMEM((T, S.up), F32),
        VMEM((T, S.up // 2), BF16),
        VMEM((T, S.up // 2), BF16),
    ]
    scratch += grads + parts + parts + parts + ways + lines + lines
    scratch += [
        VMEM((2, 4, own, width), F32),
        VMEM((2, 2, 2, own, width), BF16),
        VMEM((2, 2, 2, own, width // 2), BF16),
        VMEM((2, 2, own, width // 2), BF16),
        VMEM((2, 2, own, width // 2), BF16),
        VMEM((4, 8, S.up), F32),
        VMEM((n - 1, 8, S.up), F32),
        VMEM((3, 8, S.up), F32),
        dma((7,)),
        dma((4,)),
        dma((4,)),
        dma((5, 2, n)),
        dma((5, 2, n)),
        dma((5, n)),
        dma((5, n)),
        dma((2, 4)),
        dma((2, 4)),
        dma,
        dma,
        dma((4,)),
        dma((4,)),
        dma((4, 2, n, 2)),
        dma((4, 2, n, 2)),
        dma((4,)),
        dma((4,)),
        dma((2, 4)),
        dma((2, 4)),
        dma((3,)),
        dma((3,)),
        dma((n - 1,)),
        dma((n - 1,)),
        dma,
        dma,
        dma((n - 1,)),
        dma((n - 1,)),
        dma,
        dma,
    ]
    return pl.pallas_call(
        functools.partial(fused_kernel, S),
        out_shape=tuple(shape((2, rows, c), F32) for c in S.gcols)
        + (
            shape((own, width), F32),
            shape((own, width), F32),
            shape((2, 8, S.up), F32),
            shape((8, width), F32),
        ),
        in_specs=[hbm, hbm, full] + [hbm] * 4 + [full] * 8,
        out_specs=(full,) * 8,
        scratch_shapes=scratch,
        compiler_params=pltpu.CompilerParams(
            collective_id=2, has_side_effects=True, vmem_limit_bytes=46 * 2**20
        ),
        name="fused",
    )(*operands)


def finish_kernel(
    S,
    red_a,
    red_d,
    red_u,
    red_v,
    hs_ref,
    bs_ref,
    small_ref,
    prm_ref,
    tok_ref,
    cot_ref,
    hid_out,
    inp_out,
    qkv_out,
    qkvb_out,
    outw_out,
    g_out,
    up_out,
    upb_out,
    down_out,
    n1g_out,
    n1b_out,
    n2g_out,
    n2b_out,
    again_out,
):
    dp = lax.axis_index("dp")
    rows, width = S.rows, S.width
    for q in range(2):
        qkv_out[:, q * S.qkv : (q + 1) * S.qkv] = red_a[q, :, : S.qkv]
        middle = q * S.up + S.gcols[2]
        up_out[:, q * S.up : middle] = red_u[q]
        up_out[:, middle : (q + 1) * S.up] = red_v[q]
        outw_out[:, q * S.out : (q + 1) * S.out] = red_a[q, :, S.qkv : S.att]
        down_out[:, q * S.up : (q + 1) * S.up] = red_d[q]
    values = tok_ref[...].astype(F32)
    unit, inv_std = unit_rows(values)
    hid_out[...] = (values + hs_ref[...] + prm_ref[4:5] + prm_ref[5:6]).astype(BF16)
    total = bs_ref[...]
    mean_term = jnp.mean(total, axis=-1, keepdims=True)
    proj_term = jnp.mean(total * unit, axis=-1, keepdims=True)
    inp_out[...] = cot_ref[...].astype(F32) + inv_std * (total - mean_term - unit * proj_term)

    def shift(block, by):
        return pltpu.roll(block, lax.rem(S.up - by, S.up), 1)

    low = shift(small_ref[1], dp * rows)
    for row, out in enumerate((n1g_out, n1b_out, n2g_out, n2b_out, g_out)):
        out[...] = low[row : row + 1, :rows]
    again_out[...] = low[4:5, :rows]
    place = lax.rem(dp, 2 * S.n)
    own_sums = small_ref[0]
    both = [jnp.broadcast_to(own_sums[i : i + 1], (8, S.up)) for i in (5, 6)]
    qkvb_out[...] = shift(both[0], place * S.qkvb)[0:1, : S.qkvb]
    upb_out[...] = shift(both[1], place * S.upb)[0:1, : S.upb]


def finish(S, operands):
    shape = jax.ShapeDtypeStruct
    row = shape((1, S.rows), F32)
    return pl.pallas_call(
        functools.partial(finish_kernel, S),
        out_shape=(
            shape((S.own, S.width), BF16),
            shape((S.own, S.width), F32),
            shape((S.rows, 2 * S.qkv), F32),
            shape((1, S.qkvb), F32),
            shape((S.rows, 2 * S.out), F32),
            row,
            shape((S.rows, 2 * S.up), F32),
            shape((1, S.upb), F32),
            shape((S.rows, 2 * S.up), F32),
            row,
            row,
            row,
            row,
            row,
        ),
        compiler_params=pltpu.CompilerParams(vmem_limit_bytes=40 * 2**20),
        name="finish",
    )(*operands)


def on_plane(S, args):
    (tokens, segments, positions, cotangent, qkv_weight, qkv_bias, out_weight, out_bias) = args[:8]
    (up_weight, up_bias, down_weight, down_bias, g1, b1, g2, b2) = args[8:]
    def stay(array):
        return pltpu.with_memory_space_constraint(array, pltpu.HBM)

    made = fused(
        S,
        (
            stay(tokens),
            stay(cotangent),
            positions.reshape(1, -1),
            stay(qkv_weight[0]),
            stay(out_weight[0].T),
            stay(up_weight[0]),
            stay(down_weight[0].T),
            g1,
            b1,
            g2,
            b2,
            out_bias,
            down_bias,
            qkv_bias,
            up_bias,
        ),
    )
    outs = finish(S, tuple(made) + (tokens, cotangent))
    hid, inp, qkv, qkvb, outw, gsum, upw, upb, downw, n1g, n1b, n2g, n2b, gsum_again = outs
    return (
        hid[None],
        inp,
        qkv[None],
        qkvb,
        outw.T[None],
        gsum,
        upw[None],
        upb,
        downw.T[None],
        gsum_again,
        n1g,
        n1b,
        n2g,
        n2b,
    )


def on_device(
    tokens,
    segments,
    positions,
    cotangent,
    qkv_weight,
    qkv_bias,
    out_weight,
    out_bias,
    up_weight,
    up_bias,
    down_weight,
    down_bias,
    norm1_gain,
    norm1_bias,
    norm2_gain,
    norm2_bias,
):
    dp_size = lax.axis_size("dp")
    n_outer = dp_size // 4
    core = lax.rem(lax.axis_index("dp"), 2)
    x = lax.axis_index("tensor")
    own, width = tokens.shape
    rows = qkv_weight.shape[1]
    seq_len = segments.shape[0]
    plane = Shape(
        n_outer,
        rows,
        own,
        width,
        seq_len,
        qkv_weight.shape[2] // 2,
        out_weight.shape[1] // 2,
        up_weight.shape[2] // 2,
        qkv_bias.shape[1],
        up_bias.shape[1],
    )
    if plane.fits():
        return on_plane(
            plane,
            (
                tokens,
                segments,
                positions,
                cotangent,
                qkv_weight,
                qkv_bias,
                out_weight,
                out_bias,
                up_weight,
                up_bias,
                down_weight,
                down_bias,
                norm1_gain,
                norm1_bias,
                norm2_gain,
                norm2_bias,
            ),
        )
    qkv_q, up_q, out_q = (
        qkv_weight.shape[2] // 2,
        up_weight.shape[2] // 2,
        out_weight.shape[1] // 2,
    )
    sizes = Sizes(rows, up_q, qkv_q, out_q, qkv_bias.shape[1], up_bias.shape[1])
    heads = out_q // HEAD

    def halves(w):
        return jnp.swapaxes(w.reshape(rows, 2, -1), 0, 1)

    def halves_t(w):
        return jnp.swapaxes(w.reshape(2, -1, rows), 1, 2)

    small = jnp.concatenate(
        [
            jnp.stack(
                [
                    norm1_gain[0],
                    norm1_bias[0],
                    norm2_gain[0],
                    norm2_bias[0],
                    out_bias[0],
                    down_bias[0],
                ],
                axis=1,
            ),
            fold(qkv_bias[0], 1, rows, sizes.qb_cols)[0],
            fold(up_bias[0], 1, rows, sizes.ub_cols)[0],
        ],
        axis=1,
    )
    packed = sizes.pack(
        halves(up_weight[0]),
        halves_t(down_weight[0]),
        halves(qkv_weight[0]),
        jnp.broadcast_to(small[None], (2,) + small.shape),
        halves_t(out_weight[0]),
    )
    own_pos = lax.dynamic_slice_in_dim(positions, x * own, own, 0).astype(BF16)
    rows_in = jnp.concatenate(
        [tokens, cotangent, jnp.pad(own_pos[:, None], ((0, 0), (0, 127)))], axis=1
    )
    gathered, group_rows = gather(sizes, n_outer, packed, rows_in)

    flat = gathered.reshape(dp_size * rows, sizes.cols)
    up_w = flat[:, :up_q]
    down_wt = flat[:, up_q : 2 * up_q]
    qkv_w = flat[:, sizes.qkv : sizes.qkv + qkv_q]
    out_wt = flat[:, sizes.out : sizes.out + out_q]
    smalls = flat[:, sizes.small : sizes.small + sizes.n_small].astype(F32)
    vecs = smalls[:, :6].T
    by_dev = smalls.reshape(dp_size, rows, sizes.n_small)
    qb = by_dev[:, :, 6 : 6 + sizes.qb_cols].reshape(dp_size, -1)[:, : sizes.qkvb].reshape(-1)
    ub = by_dev[:, :, 6 + sizes.qb_cols :].reshape(dp_size, -1)[:, : sizes.upb].reshape(-1)
    qkv_b = lax.dynamic_slice_in_dim(qb, core * qkv_q, qkv_q, 0)
    up_b = lax.dynamic_slice_in_dim(ub, core * up_q, up_q, 0)

    group_rows = group_rows.reshape(4 * own, -1)
    count = 4 * own
    seqs = count // seq_len
    xs = group_rows[:, :width].astype(F32)
    cot = group_rows[:, width : 2 * width]
    pos = group_rows[:, 2 * width].astype(F32).reshape(seqs, seq_len)
    cos_tab, sin_tab = rotary_tables(pos)
    query_index = jnp.arange(seq_len, dtype=F32)
    key_index = query_index[None, None, :]
    first_key = query_index[None, :] - pos
    allowed = (
        (key_index <= query_index[None, :, None]) & (key_index >= first_key[:, :, None])
    )[:, None]

    unit, _ = unit_rows(xs)
    n1 = (unit * vecs[0] + vecs[1]).astype(BF16)
    n2 = (unit * vecs[2] + vecs[3]).astype(BF16)
    projected = (dot(n1, qkv_w, 1, 0) + qkv_b).reshape(seqs, seq_len, heads, 3, HEAD)
    projected = jnp.transpose(projected, (3, 0, 2, 1, 4))
    query = rotate(projected[0], cos_tab, sin_tab).astype(BF16)
    key = rotate(projected[1], cos_tab, sin_tab).astype(BF16)
    value = projected[2].astype(BF16)
    scale = HEAD ** (-0.5)

    def ein(spec, a, b):
        return jnp.einsum(spec, a, b, preferred_element_type=F32)

    scores = jnp.where(allowed, ein("shqd,shkd->shqk", query, key) * scale, -jnp.inf)
    peak = jnp.max(scores, axis=-1, keepdims=True)
    log_total = peak + jnp.log(jnp.sum(jnp.exp(scores - peak), axis=-1, keepdims=True))
    weights = jnp.exp(scores - log_total)
    weights_bf = weights.astype(BF16)
    attended = ein("shqk,shkd->shqd", weights_bf, value).astype(BF16)
    attended_flat = jnp.swapaxes(attended, 1, 2).reshape(count, out_q)
    pre = dot(n2, up_w, 1, 0) + up_b
    cumul = 0.5 * (1.0 + jax.scipy.special.erf(pre * 0.7071067811865476))
    act = (pre * cumul).astype(BF16)
    slope = cumul + pre * jnp.exp(-0.5 * pre * pre) * 0.3989422804014327
    mixed = dot(attended_flat, out_wt, 1, 1) + dot(act, down_wt, 1, 1)

    du = (dot(cot, down_wt, 1, 0) * slope).astype(BF16)
    g_upb = jnp.sum(du.astype(F32), axis=0)
    dn2 = dot(du, up_w, 1, 1)
    d_att = dot(cot, out_wt, 1, 0).astype(BF16).reshape(seqs, seq_len, heads, HEAD)
    d_att = jnp.swapaxes(d_att, 1, 2)
    delta = jnp.sum(attended.astype(F32) * d_att.astype(F32), axis=-1, keepdims=True)
    d_value = ein("shqk,shqd->shkd", weights_bf, d_att)
    d_weight = ein("shqd,shkd->shqk", d_att, value)
    d_score = (weights * (d_weight - delta) * scale).astype(BF16)
    d_query = unrotate(ein("shqk,shkd->shqd", d_score, key), cos_tab, sin_tab)
    d_key = unrotate(ein("shqk,shqd->shkd", d_score, query), cos_tab, sin_tab)
    d_qkv = jnp.stack([d_query, d_key, d_value], axis=0).astype(BF16)
    d_qkv = jnp.transpose(d_qkv, (1, 3, 2, 0, 4)).reshape(count, qkv_q)
    g_qkvb = jnp.sum(d_qkv.astype(F32), axis=0)
    dn1 = dot(d_qkv, qkv_w, 1, 1)
    back = dn1 * vecs[0] + dn2 * vecs[2]
    up_rows = cotangent.astype(F32)
    norm_rows = jnp.stack(
        [
            jnp.sum(dn1 * unit, axis=0),
            jnp.sum(dn1, axis=0),
            jnp.sum(dn2 * unit, axis=0),
            jnp.sum(dn2, axis=0),
            jnp.sum(up_rows, axis=0),
            jnp.zeros((width,), F32),
        ],
        axis=1,
    ).reshape(dp_size, rows, 6)
    own_half = jnp.arange(2)[:, None] == core
    qb_full = jnp.where(own_half, g_qkvb[None], 0.0).reshape(-1)
    ub_full = jnp.where(own_half, g_upb[None], 0.0).reshape(-1)
    small_grads = jnp.concatenate(
        [
            norm_rows,
            fold(qb_full, dp_size, rows, sizes.qb_cols),
            fold(ub_full, dp_size, rows, sizes.ub_cols),
        ],
        axis=2,
    )
    small_grads = jnp.pad(
        small_grads,
        (
            (0, 0),
            (0, 0),
            (sizes.small - sizes.tile, sizes.tile_end - sizes.small - sizes.n_small),
        ),
    ).reshape(dp_size // 2, 2, rows, -1)

    def turned(values):
        return values.T.reshape(dp_size // 2, 2, rows, count)

    operands = (
        turned(n2),
        turned(cot),
        turned(n1),
        du,
        act,
        jnp.pad(d_qkv, ((0, 0), (0, sizes.out - sizes.small))),
        attended_flat,
        small_grads,
    )
    reduced, mixed_sum, total, small_sum = scatter(
        sizes,
        n_outer,
        operands,
        mixed.astype(BF16).reshape(2, 2, own, width),
        back.astype(BF16).reshape(2, 2, own, width),
    )

    own_x = tokens.astype(F32)
    own_unit, own_inv = unit_rows(own_x)
    hidden = (own_x + mixed_sum + vecs[4] + vecs[5]).astype(BF16)
    mean_term = jnp.mean(total, axis=-1, keepdims=True)
    proj_term = jnp.mean(total * own_unit, axis=-1, keepdims=True)
    input_grad = up_rows + own_inv * (total - mean_term - own_unit * proj_term)

    def columns(start, size):
        return jnp.swapaxes(reduced[:, :, start : start + size], 0, 1).reshape(rows, 2 * size)

    def columns_t(start, size):
        return jnp.swapaxes(reduced[:, :, start : start + size], 1, 2).reshape(2 * size, rows)

    off = sizes.small - sizes.tile
    fin = small_sum[1, :, off : off + 6].T
    qb_out = small_sum[0, :, off + 6 : off + 6 + sizes.qb_cols].reshape(-1)[: sizes.qkvb]
    ub_at = off + 6 + sizes.qb_cols
    ub_out = small_sum[0, :, ub_at : ub_at + sizes.ub_cols].reshape(-1)[: sizes.upb]
    return (
        hidden[None],
        input_grad,
        columns(sizes.qkv, qkv_q)[None],
        qb_out[None],
        columns_t(sizes.out, out_q)[None],
        fin[4][None],
        columns(0, up_q)[None],
        ub_out[None],
        columns_t(sizes.down, up_q)[None],
        fin[4][None],
        fin[0][None],
        fin[1][None],
        fin[2][None],
        fin[3][None],
    )


def solution(mesh):
    in_specs = (
        P(("dp", "tensor"), None),
        P("dp"),
        P("dp"),
        P(("dp", "tensor"), None),
        P(None, "dp", "tensor"),
        P(None, ("tensor", "dp")),
        P(None, "tensor", "dp"),
        P(None, "dp"),
        P(None, "dp", "tensor"),
        P(None, ("tensor", "dp")),
        P(None, "tensor", "dp"),
        P(None, "dp"),
        P(None, "dp"),
        P(None, "dp"),
        P(None, "dp"),
        P(None, "dp"),
    )
    out_specs = (
        P(None, ("dp", "tensor"), None),
        P(("dp", "tensor"), None),
        P(None, "dp", "tensor"),
        P(None, ("tensor", "dp")),
        P(None, "tensor", "dp"),
        P(None, "dp"),
        P(None, "dp", "tensor"),
        P(None, ("tensor", "dp")),
        P(None, "tensor", "dp"),
        P(None, "dp"),
        P(None, "dp"),
        P(None, "dp"),
        P(None, "dp"),
        P(None, "dp"),
    )
    return jax.shard_map(
        on_device, mesh=mesh, in_specs=in_specs, out_specs=out_specs, check_vma=False
    )
```

```python
import functools

import jax
import jax.numpy as jnp
from jax import lax
from jax.experimental import pallas as pl
from jax.experimental.pallas import tpu as pltpu
from jax.sharding import PartitionSpec as P

HEAD = 64
ROT = 16
EPS = 1e-05
F32 = jnp.float32
BF16 = jnp.bfloat16
VMEM = pltpu.VMEM


def up128(n):
    return -(-n // 128) * 128


class Sizes:
    def __init__(self, rows, up_q, qkv_q, out_q, qkvb, upb):
        self.rows, self.up_q, self.qkv_q, self.out_q = rows, up_q, qkv_q, out_q
        self.qkvb, self.upb = qkvb, upb
        self.qb_cols, self.ub_cols = -(-qkvb // rows), -(-upb // rows)
        self.down = up_q
        self.qkv = 2 * up_q
        self.small = self.qkv + qkv_q
        self.n_small = 6 + self.qb_cols + self.ub_cols
        self.out = up128(self.small + self.n_small)
        self.cols = up128(self.out + out_q)
        self.tile = self.small // 128 * 128
        self.tile_end = self.out

    def pack(self, up, down, qkv, small, out):
        lead = up.shape[:-1]
        gap = self.out - self.small - small.shape[-1]
        tail = self.cols - self.out - self.out_q
        parts = [up, down, qkv, small, jnp.zeros(lead + (gap,), BF16), out]
        if tail:
            parts.append(jnp.zeros(lead + (tail,), BF16))
        return jnp.concatenate([p.astype(BF16) for p in parts], axis=-1)


def places(n_outer):
    dp = lax.axis_index("dp")
    x = lax.axis_index("tensor")
    core = lax.rem(dp, 2)
    chip = dp // 2
    inner = lax.rem(chip, 2)
    outer = chip // 2
    return dp, x, core, chip, inner, outer


def dev(chip, core, x):
    return {"dp": chip * 2 + core, "tensor": x}


def greet(partners, outer, n_outer, up, down):
    barrier = pltpu.get_barrier_semaphore()

    def tell(partner):
        pl.semaphore_signal(
            barrier, inc=1, device_id=partner, device_id_type=pl.DeviceIdType.MESH
        )

    for partner in partners:
        tell(partner)
    pl.when(outer < n_outer - 1)(lambda: tell(up))
    pl.when(outer > 0)(lambda: tell(down))
    chained = jnp.minimum(outer, 1) + jnp.minimum(n_outer - 1 - outer, 1)
    pl.semaphore_wait(barrier, len(partners) + chained)


def rcopy(src, dst, send, recv, where):
    return pltpu.make_async_remote_copy(
        src_ref=src,
        dst_ref=dst,
        send_sem=send,
        recv_sem=recv,
        device_id=where,
        device_id_type=pl.DeviceIdType.MESH,
    )


def partner_list(n_outer):
    dp, x, core, chip, inner, outer = places(n_outer)
    sibling = dev(chip, 1 - core, x)
    across = dev(chip, core, 1 - x)
    diagonal = dev(chip, 1 - core, 1 - x)
    inner_peer = dev(outer * 2 + 1 - inner, core, x)
    up = dev((outer + 1) * 2 + inner, core, x)
    down = dev((outer - 1) * 2 + inner, core, x)
    return sibling, across, diagonal, inner_peer, up, down


def gather_kernel(
    n_outer, p_ref, a_ref, w_ref, t_ref, loc_sem, grp_s, grp_r, sib_s, sib_r, ch_s, ch_r, in_s, in_r
):
    dp, x, core, chip, inner, outer = places(n_outer)
    sibling, across, diagonal, inner_peer, up, down = partner_list(n_outer)
    own_w = pltpu.make_async_copy(p_ref.at[core], w_ref.at[chip, core], loc_sem.at[0])
    own_t = pltpu.make_async_copy(a_ref, t_ref.at[core, x], loc_sem.at[1])
    own_w.start()
    own_t.start()
    greet([sibling, across, diagonal, inner_peer], outer, n_outer, up, down)
    sib = rcopy(p_ref.at[1 - core], w_ref.at[chip, core], sib_s, sib_r, sibling)
    sib.start()
    own_w.wait()
    sib.wait_recv()
    last = n_outer - 1

    def chain(way, step):
        block = outer - step if way == 0 else outer + step
        there = (outer < last) & (block >= 0) if way == 0 else (outer > 0) & (block <= last)
        spot = w_ref.at[block * 2 + inner]
        where = up if way == 0 else down
        return there, lambda: rcopy(spot, spot, ch_s.at[way, step], ch_r.at[way, step], where)

    def arrival(way, step):
        block = outer - 1 - step if way == 0 else outer + 1 + step
        there = block >= 0 if way == 0 else block <= last
        spot = w_ref.at[block * 2 + inner]
        return there, lambda: rcopy(spot, spot, ch_s.at[way, step], ch_r.at[way, step], up)

    def forward(way, step, mine):
        block = outer - 1 - step if way == 0 else outer + 1 + step
        there = block >= 0 if way == 0 else block <= last
        spot = w_ref.at[block * 2 + (inner if mine else 1 - inner)]
        return there, lambda: rcopy(spot, spot, in_s.at[way, step], in_r.at[way, step], inner_peer)

    def act(pair, what):
        there, copy = pair
        pl.when(there)(lambda: what(copy()))

    def start(copy):
        copy.start()

    for way in range(2):
        act(chain(way, 0), start)
    own = w_ref.at[chip]
    mine = rcopy(own, own, in_s.at[0, last], in_r.at[0, last], inner_peer)
    mine.start()
    group = []
    for slot, where in enumerate((sibling, across, diagonal)):
        copy = rcopy(a_ref, t_ref.at[core, x], grp_s.at[slot], grp_r.at[slot], where)
        copy.start()
        group.append(copy)
    for step in range(last):
        for way in range(2):
            act(arrival(way, step), lambda copy: copy.wait_recv())
            if step + 1 < last:
                act(chain(way, step + 1), start)
            act(forward(way, step, True), start)
    for copy in group:
        copy.wait_recv()
    mine.wait_recv()
    for step in range(last):
        for way in range(2):
            act(forward(way, step, False), lambda copy: copy.wait_recv())
    own_t.wait()
    sib.wait_send()
    mine.wait_send()
    for copy in group:
        copy.wait_send()
    for step in range(last):
        for way in range(2):
            act(chain(way, step), lambda copy: copy.wait_send())
            act(forward(way, step, True), lambda copy: copy.wait_send())


def scatter_kernel(
    sizes,
    n_outer,
    n2t_ref,
    cott_ref,
    n1t_ref,
    du_ref,
    act_ref,
    dqkv_ref,
    att_ref,
    small_ref,
    h_ref,
    d_ref,
    r_ref,
    hs_ref,
    ds_ref,
    x_ref,
    first_buf,
    b1,
    send_buf,
    cbuf,
    acc,
    hr,
    small_out,
    small_in,
    grp_s,
    grp_r,
    in_s,
    in_r,
    ch_s,
    ch_r,
    sib_s,
    sib_r,
    sm_s,
    sm_r,
):
    dp, x, core, chip, inner, outer = places(n_outer)
    sibling, across, diagonal, inner_peer, up, down = partner_list(n_outer)
    last = n_outer - 1
    rows = sizes.rows
    lo, hi = sizes.tile, sizes.tile_end

    def block(target, put):
        def product(left, right):
            if rows % 16 == 0:
                lhs = left[target].reshape(2 * rows, -1)
                out = jnp.dot(lhs, right[...], preferred_element_type=F32)
                return out.reshape(2, rows, -1)
            return jnp.stack(
                [
                    jnp.dot(left[target, side], right[...], preferred_element_type=F32)
                    for side in range(2)
                ]
            )

        put(0, sizes.down, product(n2t_ref, du_ref))
        put(sizes.down, sizes.qkv, product(cott_ref, act_ref))
        part = product(n1t_ref, dqkv_ref)
        cut = lo - sizes.qkv
        put(sizes.qkv, lo, part[:, :, :cut])
        put(lo, hi, part[:, :, cut:] + small_ref[target])
        end = sizes.out + sizes.out_q
        put(sizes.out, end, product(cott_ref, att_ref))
        if end < sizes.cols:
            put(end, sizes.cols, jnp.zeros((2, rows, sizes.cols - end), F32))

    def to_acc(start, stop, value):
        acc[:, :, start:stop] = value

    greet([sibling, across, diagonal, inner_peer], outer, n_outer, up, down)
    group = []
    spots = ((sibling, 1 - core, x), (across, core, 1 - x), (diagonal, 1 - core, 1 - x))
    for slot, (where, to_core, to_x) in enumerate(spots):
        for kind, part in enumerate((h_ref, d_ref)):
            copy = rcopy(
                part.at[to_core, to_x],
                hr.at[kind, slot],
                grp_s.at[kind, slot],
                grp_r.at[kind, slot],
                where,
            )
            copy.start()
            group.append(copy)

    def in_order(what):
        @pl.loop(0, last)
        def _(tick):
            back = last - tick
            pl.when(outer <= tick)(lambda: what(0, outer + back))
            pl.when(outer >= back)(lambda: what(1, outer - back))

    def exchange(target):
        return rcopy(
            first_buf.at[target], b1.at[target], in_s.at[target], in_r.at[target], inner_peer
        )

    def passing(way, target):
        return rcopy(
            send_buf.at[target],
            cbuf.at[way, target],
            ch_s.at[way, target],
            ch_r.at[way, target],
            up if way == 0 else down,
        )

    def send_first(target):
        def put(start, stop, value):
            first_buf[target, :, :, start:stop] = value.astype(BF16)

        block(target * 2 + 1 - inner, put)
        exchange(target).start()

    def send_second(way, target):
        block(target * 2 + inner, to_acc)
        exchange(target).wait_recv()
        acc[...] += b1[target].astype(F32)
        started = outer > 0 if way == 0 else outer < last

        @pl.when(started)
        def _():
            passing(way, target).wait_recv()
            acc[...] += cbuf[way, target].astype(F32)

        send_buf[target] = acc[...].astype(BF16)
        passing(way, target).start()

    in_order(lambda way, target: send_first(target))
    send_first(outer)
    in_order(send_second)
    for copy in group:
        copy.wait_recv()
    for kind, (part, out) in enumerate(((h_ref, hs_ref), (d_ref, ds_ref))):
        out[...] = (
            part[core, x].astype(F32)
            + hr[kind, 0].astype(F32)
            + hr[kind, 1].astype(F32)
            + hr[kind, 2].astype(F32)
        )
    block(chip, to_acc)
    exchange(outer).wait_recv()
    acc[...] += b1[outer].astype(F32)
    for way in range(2):

        @pl.when(outer > 0 if way == 0 else outer < last)
        def _():
            passing(way, outer).wait_recv()
            acc[...] += cbuf[way, outer].astype(F32)

    sib = rcopy(acc.at[1 - core], r_ref.at[core], sib_s, sib_r, sibling)
    sib.start()
    r_ref[core] = acc[core]
    sib.wait_recv()
    small_out[...] = r_ref[0, :, lo:hi] + r_ref[1, :, lo:hi]
    small = rcopy(small_out, small_in, sm_s, sm_r, across)
    small.start()
    small.wait_recv()
    x_ref[0] = small_out[...]
    x_ref[1] = small_out[...] + small_in[...]
    sib.wait_send()
    small.wait_send()
    for copy in group:
        copy.wait_send()
    exchange(outer).wait_send()

    def sent(way, target):
        exchange(target).wait_send()
        passing(way, target).wait_send()

    in_order(sent)


def gather(sizes, n_outer, packed, rows):
    dma = pltpu.SemaphoreType.DMA
    full = pl.BlockSpec(memory_space=VMEM)
    return pl.pallas_call(
        functools.partial(gather_kernel, n_outer),
        out_shape=(
            jax.ShapeDtypeStruct((2 * n_outer, 2) + packed.shape[1:], BF16),
            jax.ShapeDtypeStruct((2, 2) + rows.shape, BF16),
        ),
        in_specs=[full, full],
        out_specs=(full, full),
        scratch_shapes=[
            dma((2,)),
            dma((3,)),
            dma((3,)),
            dma,
            dma,
            dma((2, n_outer)),
            dma((2, n_outer)),
            dma((2, n_outer)),
            dma((2, n_outer)),
        ],
        compiler_params=pltpu.CompilerParams(
            collective_id=0, has_side_effects=True, vmem_limit_bytes=60 * 2**20
        ),
        name="gather",
    )(packed, rows)


def scatter(sizes, n_outer, operands, mixed, back):
    dma = pltpu.SemaphoreType.DMA
    full = pl.BlockSpec(memory_space=VMEM)
    block = (2, sizes.rows, sizes.cols)
    width = sizes.tile_end - sizes.tile
    return pl.pallas_call(
        functools.partial(scatter_kernel, sizes, n_outer),
        out_shape=(
            jax.ShapeDtypeStruct(block, F32),
            jax.ShapeDtypeStruct(mixed.shape[2:], F32),
            jax.ShapeDtypeStruct(mixed.shape[2:], F32),
            jax.ShapeDtypeStruct((2, sizes.rows, width), F32),
        ),
        in_specs=[full] * (len(operands) + 2),
        out_specs=(full, full, full, full),
        scratch_shapes=[
            VMEM((n_outer,) + block, BF16),
            VMEM((n_outer,) + block, BF16),
            VMEM((n_outer,) + block, BF16),
            VMEM((2, n_outer) + block, BF16),
            VMEM(block, F32),
            VMEM((2, 3) + mixed.shape[2:], BF16),
            VMEM((sizes.rows, width), F32),
            VMEM((sizes.rows, width), F32),
            dma((2, 3)),
            dma((2, 3)),
            dma((n_outer,)),
            dma((n_outer,)),
            dma((2, n_outer)),
            dma((2, n_outer)),
            dma,
            dma,
            dma,
            dma,
        ],
        compiler_params=pltpu.CompilerParams(
            collective_id=1, has_side_effects=True, vmem_limit_bytes=60 * 2**20
        ),
        name="scatter",
    )(*operands, mixed, back)


def rotary_tables(pos_ids):
    half_rot = ROT // 2
    freq_index = jnp.arange(half_rot, dtype=F32)
    inverse = jnp.power(F32(10000.0), -2.0 * freq_index / ROT)
    angles = pos_ids[..., None] * inverse
    cos_tab = jnp.concatenate([jnp.cos(angles), jnp.cos(angles)], axis=-1)
    sin_tab = jnp.concatenate([jnp.sin(angles), jnp.sin(angles)], axis=-1)
    return (cos_tab[:, None], sin_tab[:, None])


def rotate(values, cos_tab, sin_tab):
    half_rot = ROT // 2
    rotary = values[..., :ROT]
    turned = jnp.concatenate([-rotary[..., half_rot:], rotary[..., :half_rot]], axis=-1)
    return jnp.concatenate([rotary * cos_tab + turned * sin_tab, values[..., ROT:]], axis=-1)


def unrotate(grad_vals, cos_tab, sin_tab):
    half_rot = ROT // 2
    rotary = grad_vals[..., :ROT]
    scaled = rotary * sin_tab
    back_part = jnp.concatenate([scaled[..., half_rot:], -scaled[..., :half_rot]], axis=-1)
    return jnp.concatenate([rotary * cos_tab + back_part, grad_vals[..., ROT:]], axis=-1)


def unit_rows(values):
    centre = values - jnp.mean(values, axis=-1, keepdims=True)
    inv_std = lax.rsqrt(jnp.mean(centre * centre, axis=-1, keepdims=True) + EPS)
    return centre * inv_std, inv_std


def dot(a, b, ca, cb):
    return lax.dot_general(a, b, (((ca,), (cb,)), ((), ())), preferred_element_type=F32)


def fold(vector, count, rows, cols):
    per = vector.shape[0] // count
    padded = jnp.pad(vector.reshape(count, per), ((0, 0), (0, rows * cols - per)))
    return padded.reshape(count, rows, cols)


CHAIN = 4


class Shape:
    def __init__(self, n, rows, own, width, seq, qkv, out, up, qkvb, upb):
        self.n, self.rows, self.own, self.width, self.seq = n, rows, own, width, seq
        self.qkv, self.out, self.up, self.qkvb, self.upb = qkv, out, up, qkvb, upb
        self.heads = out // HEAD
        self.att = qkv + out
        self.tokens = 4 * own
        self.cols = (self.att, up, up // 2, up // 2)
        self.gcols = (self.att, up, up // 2, up // 2)

    def fits(self):
        aligned = [self.own, self.width, self.seq, self.att, self.up]
        return (
            self.rows % 16 == 0
            and all(size % 128 == 0 for size in aligned)
            and self.up % 256 == 0
            and self.n == CHAIN
            and self.own * 2 == self.seq
            and self.att <= self.up
            and self.width <= self.up
            and max(self.rows, self.qkvb, self.upb) <= 128
            and self.n >= 2
            and (self.n * 4) * self.rows == self.width
        )


def fused_kernel(S, *refs):
    refs = list(refs)

    def take(count):
        got = refs[:count]
        del refs[:count]
        return got

    tok_ref, cot_ref, pos_ref, qkv_ref, out_ref, up_ref, down_ref = take(7)
    small_params = take(8)
    red = take(4)
    hs_ref, bs_ref, small_ref, prm_ref = take(4)
    pk, qkv_v, out_v = take(3)
    w = take(4)
    tbuf, cbuf, pbuf, smrow, bias, unit, n1, n2, mask, rot_c, rot_s = take(11)
    sbuf, ct, ut, n1t, n2t = take(5)
    proj, qh, kh, vh, doh, att, dqk, dqkv, outw, act, slope = take(11)
    du = take(2)
    grad, sb, rb, cs, ci, ysb, yrb = (take(4) for _ in range(7))
    mine, mix_s, mix_r, mix_t, mix_u, sm_s, sm_z, sm_r = take(8)
    ld, gy_s, gy_r, gc_s, gc_r, gf_s, gf_r, tk_s, tk_r, ps_s, ps_r = take(11)
    ss_s, ss_r, sc_s, sc_r, sy_s, sy_r, mx_s, mx_r, st_s, st_r, sz_s, sz_r = take(12)
    py_s, py_r, pz_s, pz_r, pf_s, pf_r = take(6)
    w_a, w_u = w[:2]
    n, rows, own, width = S.n, S.rows, S.own, S.width
    last = n - 1
    dp = lax.axis_index("dp")
    x = lax.axis_index("tensor")
    core = lax.rem(dp, 2)
    y = lax.rem(dp // 2, 2)
    z = dp // 4

    def at(zz, yy, cc, xx):
        return {"dp": zz * 4 + yy * 2 + cc, "tensor": xx}

    sibling = at(z, y, 1 - core, x)
    across = at(z, y, core, 1 - x)
    ypeer = at(z, 1 - y, core, x)
    up, down = at(z + 1, y, core, x), at(z - 1, y, core, x)
    sends = []

    def begin(copy):
        copy.start()
        sends.append(copy)
        return copy

    def iota(shape, axis):
        return lax.broadcasted_iota(jnp.int32, shape, axis)

    barrier = pltpu.get_barrier_semaphore()

    def tell(partner):
        pl.semaphore_signal(
            barrier, inc=1, device_id=partner, device_id_type=pl.DeviceIdType.MESH
        )

    for partner in (sibling, across, ypeer):
        tell(partner)
    for step in range(1, n):
        tell(at(lax.rem(z + step, n), y, core, x))
    def load(i, src, dst):
        copy = pltpu.make_async_copy(src, dst, ld.at[i])
        copy.start()
        return copy

    def cut(ref, start, size):
        return ref.at[:, pl.ds(pl.multiple_of(start, 128), size)]

    half = S.up // 2

    def part_of(k, q):
        if k == 0:
            return pk.at[q]
        if k == 1:
            return cut(up_ref, q * S.up, S.up)
        return cut(down_ref, q * S.up + (k - 2) * half, half)

    loads = [load(0, qkv_ref, qkv_v), load(1, out_ref, out_v)]
    own_loads = [load(1 + k, part_of(k, y), w[k].at[z, y, core]) for k in range(1, 4)]
    own_rows = [load(5, tok_ref, tbuf.at[y, x]), load(6, cot_ref, cbuf.at[y, x])]
    row_pos = pos_ref[...].astype(F32)
    pbuf[y] = jnp.broadcast_to(row_pos, pbuf.shape[1:])
    smrow[...] = jnp.zeros_like(smrow)
    for row, part in enumerate(small_params):
        smrow[row : row + 1, : part.shape[1]] = part[...].astype(F32)
    for copy in loads:
        copy.wait()
    for q in range(2):
        pk[q, :, : S.qkv] = qkv_v[:, q * S.qkv : (q + 1) * S.qkv]
        pk[q, :, S.qkv : S.att] = out_v[:, q * S.out : (q + 1) * S.out]
    w[0][z, y, core] = pk[y]
    sbuf[z, y, core] = smrow[...].astype(BF16)

    pl.semaphore_wait(barrier, 3 + last)

    def y_copy(k):
        return rcopy(part_of(k, 1 - y), w[k].at[z, y, core], gy_s.at[k], gy_r.at[k], ypeer)

    def spot_of(k, block):
        if k < 2:
            return w[0].at[block, y if k == 0 else 1 - y, core]
        return w[k - 1].at[block, :, core]

    def chain_copy(k, way, step):
        block = z - step if way == 0 else z + step
        there = (z < last) & (block >= 0) if way == 0 else (z > 0) & (block <= last)
        where = up if way == 0 else down

        def copy():
            spot = spot_of(k, block)
            return rcopy(spot, spot, gc_s.at[k, way, step], gc_r.at[k, way, step], where)

        return there, copy

    def fan_copy(k, block):
        spot = spot_of(k, block)
        return rcopy(spot, spot, gf_s.at[k, block], gf_r.at[k, block], sibling)

    def arrived(way, step):
        block = z - 1 - step if way == 0 else z + 1 + step
        return block, (block >= 0 if way == 0 else block <= last)

    def start_own(k):
        if k > 1:
            own_loads[k - 2].wait()
        if k:
            y_copy(k - 1).wait_recv()
        for way in range(2):
            there, copy = chain_copy(k, way, 0)
            pl.when(there)(lambda: copy().start())
        fan_copy(k, z).start()

    def relay(k, step):
        for way in range(2):
            block, there = arrived(way, step)

            @pl.when(there)
            def _():
                spot = spot_of(k, block)
                rcopy(spot, spot, gc_s.at[k, way, step], gc_r.at[k, way, step], up).wait_recv()

            if step + 1 < last:
                more, copy = chain_copy(k, way, step + 1)
                pl.when(more)(lambda: copy().start())
            pl.when(there)(lambda: fan_copy(k, block).start())

    def gathered(k):
        for block in range(n):
            if k < 2:
                spot = w[0].at[block, y if k == 0 else 1 - y, 1 - core]
            else:
                spot = w[k - 1].at[block, :, 1 - core]
            rcopy(spot, spot, gf_s.at[k, block], gf_r.at[k, block], sibling).wait_recv()

    def params_y():
        mine_spot = sbuf.at[z, y, core]
        return rcopy(mine_spot, mine_spot, py_s, py_r, ypeer)

    def params_z(step, block):
        spot = sbuf.at[block, :, core]
        where = at(lax.rem(z + step, n), y, core, x)
        return rcopy(spot, spot, pz_s.at[step - 1], pz_r.at[step - 1], where)

    def params_fan(which):
        spot = sbuf.at[:, :, which]
        return rcopy(spot, spot, pf_s, pf_r, sibling)

    def params_send():
        params_y().wait_recv()
        for step in range(1, n):
            begin(params_z(step, z))

    def params_fan_out():
        for step in range(1, n):
            params_z(step, lax.rem(z - step + n, n)).wait_recv()
        begin(params_fan(core))

    def send_y(k):
        begin(y_copy(k))

    low, high = pl.ds(0, own // 2), pl.ds(own // 2, own // 2)

    def row_copy(kind, slot):
        src, dst = ((tok_ref, tbuf), (cot_ref, cbuf))[kind]
        where = across if slot in (0, 3) else ypeer
        if slot == 2:
            src, dst = dst.at[y, 1 - x, low], dst.at[y, 1 - x, low]
        elif slot == 3:
            src, dst = dst.at[1 - y, x, high], dst.at[1 - y, x, high]
        else:
            dst = dst.at[y, x]
        return rcopy(src, dst, tk_s.at[kind, slot], tk_r.at[kind, slot], where)

    def send_rows(kind):
        begin(row_copy(kind, 0))
        begin(row_copy(kind, 1))

    def pass_rows(kind):
        row_copy(kind, 0).wait_recv()
        begin(row_copy(kind, 2))
        row_copy(kind, 1).wait_recv()
        begin(row_copy(kind, 3))

    def have_rows(kind):
        own_rows[kind].wait()
        row_copy(kind, 2).wait_recv()
        row_copy(kind, 3).wait_recv()

    begin(params_y())
    pos_copy = begin(rcopy(pbuf.at[y], pbuf.at[y], ps_s, ps_r, ypeer))

    lane = iota((own, 128), 1)
    spin = lax.rem(lane, HEAD)

    def tables():
        pos_copy.wait_recv()
        freq = jnp.zeros((1, 128), F32)
        which = lax.rem(iota((1, 128), 1), ROT // 2)
        for i in range(ROT // 2):
            freq = jnp.where(which == i, 10000.0 ** (-2.0 * i / ROT), freq)
        query = iota((S.seq, S.seq), 0).astype(F32)
        key = iota((S.seq, S.seq), 1).astype(F32)
        spin_s = lax.rem(iota((S.seq, 128), 1), HEAD)
        for s in range(2):
            line = jnp.where(query == key, pbuf[s, 0:1, :], 0.0)
            column = jnp.sum(line, axis=1, keepdims=True)
            seen = (key <= query) & (key >= query - column)
            mask[s] = jnp.where(seen, 0.0, -jnp.inf)
            angles = column * freq
            sines = jnp.sin(angles)
            rot_c[s * S.seq : (s + 1) * S.seq] = jnp.where(spin_s < ROT, jnp.cos(angles), 1.0)
            rot_s[s * S.seq : (s + 1) * S.seq] = jnp.where(
                spin_s < ROT // 2, -sines, jnp.where(spin_s < ROT, sines, 0.0)
            )

    def blocks(body):
        pl.loop(0, 4)(lambda g: body(g, pl.ds(pl.multiple_of(g * own, own), own)))

    def units():
        def body(g, part):
            value = unit_rows(tbuf[g // 2, lax.rem(g, 2)].astype(F32))[0]
            unit[part] = value
            ut[:, part] = value.T

        blocks(body)

    def turn_cot():
        def body(g, part):
            ct[:, part] = cbuf[g // 2, lax.rem(g, 2)].T

        blocks(body)

    def params():
        params_fan(1 - core).wait_recv()
        total = jnp.zeros((8, S.up), F32)
        for j in range(4 * n):
            piece = sbuf[j // 4, (j // 2) % 2, j % 2].astype(F32)[0:8]
            wide = jnp.concatenate([piece, jnp.zeros((8, S.up - 128), F32)], axis=1)
            total = total + (pltpu.roll(wide, j * rows, 1) if j else wide)
        prm_ref[...] = total[:, :width]
        q_total = jnp.zeros((8, S.up), F32)
        u_total = jnp.zeros((8, S.up), F32)
        for j in range(2 * n):
            there = y * (n // 2) + j // 4
            piece = sbuf[there, (j // 2) % 2, j % 2].astype(F32)[0:8]
            wide = jnp.concatenate([piece, jnp.zeros((8, S.up - 128), F32)], axis=1)
            q_total = q_total + (pltpu.roll(wide, j * S.qkvb, 1) if j else wide)
            u_total = u_total + (pltpu.roll(wide, j * S.upb, 1) if j else wide)
        bias[0:8] = q_total
        bias[8:16] = u_total

    def flat(ref, start, stop):
        return ref[:, :, :, :, start:stop].reshape(4 * n * rows, stop - start)

    def norms():
        sm_s[0] = jnp.zeros(sm_s.shape[1:], F32)

        def body(g, part):
            value = unit[part]
            n1[part] = (value * prm_ref[0:1] + prm_ref[1:2]).astype(BF16)
            n2[part] = (value * prm_ref[2:3] + prm_ref[3:4]).astype(BF16)

        blocks(body)

    def norms_turned():
        tall = jnp.concatenate([prm_ref[...], jnp.zeros((120, width), F32)], axis=0)
        tall = tall.T
        for i in range(width // 128):
            spot = slice(i * 128, (i + 1) * 128)
            value, param = ut[spot], tall[spot]
            n1t[spot] = (value * param[:, 0:1] + param[:, 1:2]).astype(BF16)
            n2t[spot] = (value * param[:, 2:3] + param[:, 3:4]).astype(BF16)

    def turn(values, part, sign):
        ahead, behind = pltpu.roll(values, 128 - ROT // 2, 1), pltpu.roll(values, ROT // 2, 1)
        other = jnp.where(spin < ROT // 2, ahead, behind) * rot_s[part]
        return values * rot_c[part] + (other if sign > 0 else -other)

    def project():
        outw[...] = flat(w_a, S.qkv, S.att)

        def body(g, part):
            proj[...] = dot(n1[part], flat(w_a, 0, S.qkv), 1, 0) + bias[6:7, : S.qkv]
            for h in range(S.heads):
                base = h * 3 * HEAD
                pair = turn(proj[:, base : base + 2 * HEAD], part, 1).astype(BF16)
                qh[h, part] = pair[:, :HEAD]
                kh[h, part] = pair[:, HEAD:]
                vh[h, part] = proj[:, base + 2 * HEAD : base + 3 * HEAD].astype(BF16)
        blocks(body)

    def project_back():
        def body(g, part):
            grads = dot(cbuf[g // 2, lax.rem(g, 2)], outw[...], 1, 0).astype(BF16)
            for h in range(S.heads):
                doh[h, part] = grads[:, h * HEAD : (h + 1) * HEAD]

        blocks(body)

    scale = HEAD ** (-0.5)

    def attend(s, h):
        part = slice(s * S.seq, (s + 1) * S.seq)
        q, k, v, dout = qh[h, part], kh[h, part], vh[h, part], doh[h, part]
        scores = dot(q, k, 1, 1) * scale + mask[s]
        raised = jnp.exp(scores - jnp.max(scores, axis=-1, keepdims=True))
        weights = raised * (1.0 / jnp.sum(raised, axis=-1, keepdims=True))
        weights_bf = weights.astype(BF16)
        got = dot(weights_bf, v, 1, 0).astype(BF16)
        att[part, h * HEAD : (h + 1) * HEAD] = got
        delta = jnp.sum(got.astype(F32) * dout.astype(F32), axis=-1, keepdims=True)
        d_score = (weights * (dot(dout, v, 1, 1) - delta) * scale).astype(BF16)
        dqk[part, :HEAD] = dot(d_score, k, 1, 0)
        dqk[part, HEAD:] = dot(d_score, q, 0, 0)
        base = h * 3 * HEAD
        dqkv[part, base + 2 * HEAD : base + 3 * HEAD] = dot(weights_bf, dout, 0, 0).astype(BF16)
        for half in range(2):
            piece = slice(s * S.seq + half * own, s * S.seq + (half + 1) * own)
            dqkv[piece, base : base + 2 * HEAD] = turn(dqk[piece], piece, -1).astype(BF16)

    def weight_grad(left, right, target, start):
        size = right.shape[1]

        @pl.loop(0, width // 128)
        def _(i):
            spot = pl.ds(pl.multiple_of(i * 128, 128), 128)
            target[spot, start : start + size] = dot(left[spot], right[...], 1, 0)

    def hidden():
        def body(g, part):
            pre = dot(n2[part], flat(w_u, 0, S.up), 1, 0) + bias[15:16, : S.up]
            cumul = 0.5 * (1.0 + lax.erf(pre * 0.7071067811865476))
            act[part] = (pre * cumul).astype(BF16)
            slope[part] = cumul + pre * jnp.exp(-0.5 * pre * pre) * 0.3989422804014327

        blocks(body)

    def back_hidden(i):
        def body(g, part):
            d_act = dot(cbuf[g // 2, lax.rem(g, 2)], flat(w[2 + i], 0, half), 1, 0)
            value = (d_act * slope[part, i * half : (i + 1) * half]).astype(BF16)
            du[i][part] = value
            sm_s[0, 6:7, i * half : (i + 1) * half] += col_sum(value.astype(F32))

        blocks(body)

    def col_sum(values):
        return jnp.sum(values, axis=0, keepdims=True)

    def early():
        sm_s[0, 4:5, :width] = col_sum(cot_ref_v().astype(F32))

        def body(g, part):
            mine[0, g] = dot(att[part], outw[...], 1, 1)
            grads = dqkv[part]
            dn1 = dot(grads, flat(w_a, 0, S.qkv), 1, 1)
            mine[1, g] = dn1 * prm_ref[0:1]
            sm_s[0, 0:1, :width] += col_sum(dn1 * unit[part])
            sm_s[0, 1:2, :width] += col_sum(dn1)
            sm_s[0, 5:6, : S.qkv] += col_sum(grads.astype(F32))

        blocks(body)

    def cot_ref_v():
        return cbuf[y, x]

    def mixed():
        def body(g, part):
            value = mine[0, g]
            for i in range(2):
                columns = act[part, i * half : (i + 1) * half]
                value = value + dot(columns, flat(w[2 + i], 0, half), 1, 1)
            mine[0, g] = value
            mix_s[0, g // 2, lax.rem(g, 2)] = value.astype(BF16)

        blocks(body)

    def backward():
        def body(g, part):
            dn2 = dot(du[0][part], flat(w_u, 0, half), 1, 1)
            dn2 = dn2 + dot(du[1][part], flat(w_u, half, S.up), 1, 1)
            value = mine[1, g] + dn2 * prm_ref[2:3]
            mine[1, g] = value
            mix_s[1, g // 2, lax.rem(g, 2)] = value.astype(BF16)
            sm_s[0, 2:3, :width] += col_sum(dn2 * unit[part])
            sm_s[0, 3:4, :width] += col_sum(dn2)

        blocks(body)

    def sib_copy(k):
        return rcopy(sb[k], rb[k], ss_s.at[k], ss_r.at[k], sibling)

    def place(zz, yy, cc):
        return pl.ds(pl.multiple_of(((zz * 2 + yy) * 2 + cc) * rows, 16), rows)

    def to_sibling(k):
        @pl.loop(0, n)
        def _(zz):
            for yy in range(2):
                sb[k][zz, yy] = grad[k][place(zz, yy, 1 - core)].astype(BF16)

        sib_copy(k).start()

    def passing(k, way, target, yy):
        return rcopy(
            cs[k].at[target, yy],
            ci[k].at[way, target, yy],
            sc_s.at[k, way, target, yy],
            sc_r.at[k, way, target, yy],
            up if way == 0 else down,
        )

    def summed(k, target, yy):
        return grad[k][place(target, yy, core)] + rb[k][target, yy].astype(F32)

    halves = (1 - y, y)

    def tick(k, step):
        back = last - step
        if step == 0:
            sib_copy(k).wait_recv()

        def pass_on(way, target, more):
            for yy in halves:

                @pl.when(more)
                def _():
                    passing(k, way, target, yy).wait_recv()
                    total = summed(k, target, yy) + ci[k][way, target, yy].astype(F32)
                    cs[k][target, yy] = total.astype(BF16)

                @pl.when(jnp.logical_not(more))
                def _():
                    cs[k][target, yy] = summed(k, target, yy).astype(BF16)

                passing(k, way, target, yy).start()

        pl.when(z <= step)(lambda: pass_on(0, z + back, z > 0))
        pl.when(z >= back)(lambda: pass_on(1, z - back, z < last))

    def last_y(k):
        return rcopy(ysb[k], yrb[k], sy_s.at[k], sy_r.at[k], ypeer)

    def final(k):
        def total(yy):
            pl.when(z > 0)(lambda: passing(k, 0, z, yy).wait_recv())
            pl.when(z < last)(lambda: passing(k, 1, z, yy).wait_recv())
            value = summed(k, z, yy)
            low = jnp.where(z > 0, ci[k][0, z, yy].astype(F32), 0.0)
            high = jnp.where(z < last, ci[k][1, z, yy].astype(F32), 0.0)
            return value + low + high

        ysb[k][...] = total(1 - y).astype(BF16)
        last_y(k).start()
        red[k][y] = total(y)

    def final_recv(k):
        last_y(k).wait_recv()
        red[k][1 - y] = yrb[k][...].astype(F32)

    left, right = pl.ds(0, width // 2), pl.ds(width // 2, width // 2)

    def mix_copy(kind, slot):
        src, where = (
            (mix_s.at[kind, :, 1 - x, :, left], across),
            (mix_s.at[kind, 1 - y, :, :, right], ypeer),
            (mix_t.at[kind, 0], ypeer),
            (mix_t.at[kind, 1], across),
        )[slot]
        dst = mix_r.at[kind, slot] if slot < 2 else mix_u.at[kind, slot - 2]
        return rcopy(src, dst, mx_s.at[kind, slot], mx_r.at[kind, slot], where)

    def mix_send(kind):
        begin(mix_copy(kind, 0))
        begin(mix_copy(kind, 1))

    def mix_pass(kind):
        mix_copy(kind, 0).wait_recv()
        first = mine[kind, (1 - y) * 2 + x, :, : width // 2] + mix_r[kind, 0, 1 - y].astype(F32)
        mix_t[kind, 0] = first.astype(BF16)
        begin(mix_copy(kind, 2))
        mix_copy(kind, 1).wait_recv()
        second = mine[kind, y * 2 + 1 - x, :, width // 2 :] + mix_r[kind, 1, 1 - x].astype(F32)
        mix_t[kind, 1] = second.astype(BF16)
        begin(mix_copy(kind, 3))

    def mix_recv(kind):
        target = (hs_ref, bs_ref)[kind]
        for slot, near in ((0, y), (1, x)):
            mix_copy(kind, 2 + slot).wait_recv()
            columns = slice(slot * (width // 2), (slot + 1) * (width // 2))
            target[:, columns] = (
                mine[kind, y * 2 + x, :, columns]
                + mix_r[kind, slot, near].astype(F32)
                + mix_u[kind, slot].astype(F32)
            )

    def z_copy(step):
        where = at(lax.rem(z + step, n), y, core, x)
        return rcopy(sm_s.at[0], sm_z.at[step - 1], sz_s.at[step - 1], sz_r.at[step - 1], where)

    def small_copy(i, where):
        return rcopy(sm_s.at[i + 1], sm_r.at[i], st_s.at[i], st_r.at[i], where)

    def small_start():
        for step in range(1, n):
            begin(z_copy(step))

    def small_z():
        value = sm_s[0]
        for step in range(1, n):
            z_copy(step).wait_recv()
            value = value + sm_z[step - 1]
        sm_s[1] = value
        begin(small_copy(0, sibling))

    def small_pair():
        small_copy(0, sibling).wait_recv()
        sm_s[2] = sm_s[1] + sm_r[0]
        begin(small_copy(1, ypeer))

    def small_y():
        small_copy(1, ypeer).wait_recv()
        sm_s[3] = sm_s[2] + sm_r[1]
        begin(small_copy(2, across))
        mine_is = z // (n // 2) == y
        small_ref[0] = jnp.where(mine_is, sm_s[2], sm_r[1])

    def small_x():
        small_copy(2, across).wait_recv()
        small_ref[1] = sm_s[3] + sm_r[2]

    def attend_pair(i):
        attend(i // S.heads, i % S.heads)

    send_y(0)
    send_rows(0)
    start_own(0)
    start_own(1)
    send_y(1)
    relay(0, 0)
    params_send()
    relay(1, 0)
    pass_rows(0)
    relay(0, 1)
    send_rows(1)
    tables()
    relay(1, 1)
    params_fan_out()
    start_own(2)
    relay(1, 2)
    send_y(3)
    have_rows(0)
    relay(0, 2)
    units()
    gathered(1)
    send_y(2)
    gathered(0)
    params()
    norms()
    relay(2, 0)
    pass_rows(1)
    project()
    start_own(4)
    norms_turned()
    have_rows(1)
    relay(2, 1)
    project_back()
    attend_pair(0)
    attend_pair(1)
    attend_pair(2)
    turn_cot()
    relay(2, 2)
    start_own(3)
    attend_pair(3)
    relay(4, 0)
    gathered(2)
    hidden()
    weight_grad(ct, act, grad[1], 0)
    to_sibling(1)
    relay(4, 1)
    relay(3, 0)
    attend_pair(4)
    attend_pair(5)
    tick(1, 0)
    weight_grad(ct, att, grad[0], S.qkv)
    weight_grad(n1t, dqkv, grad[0], 0)
    to_sibling(0)
    relay(3, 1)
    tick(1, 1)
    relay(4, 2)
    early()
    tick(0, 0)
    relay(3, 2)
    gathered(4)
    back_hidden(1)
    weight_grad(n2t, du[1], grad[3], 0)
    gathered(3)
    tick(1, 2)
    to_sibling(3)
    mixed()
    tick(3, 0)
    back_hidden(0)
    mix_send(0)
    tick(0, 1)
    weight_grad(n2t, du[0], grad[2], 0)
    backward()
    to_sibling(2)
    small_start()
    mix_send(1)
    tick(2, 0)
    tick(3, 1)
    mix_pass(0)
    final(1)
    tick(2, 1)
    tick(0, 2)
    small_z()
    mix_pass(1)
    tick(3, 2)
    tick(2, 2)
    small_pair()
    final(0)
    small_y()
    final(3)
    final(2)
    final_recv(1)
    mix_recv(0)
    mix_recv(1)
    final_recv(3)
    final_recv(0)
    final_recv(2)
    small_x()

    for copy in sends:
        copy.wait_send()
    for k in range(5):
        for step in range(last):
            for way in range(2):
                there, copy = chain_copy(k, way, step)
                pl.when(there)(lambda: copy().wait_send())
        for block in range(n):
            fan_copy(k, block).wait_send()
    for k in range(4):
        sib_copy(k).wait_send()
        last_y(k).wait_send()
        for step in range(last):
            back = last - step
            for yy in halves:
                pl.when(z <= step)(lambda: passing(k, 0, z + back, yy).wait_send())
                pl.when(z >= back)(lambda: passing(k, 1, z - back, yy).wait_send())


def fused(S, operands):
    dma = pltpu.SemaphoreType.DMA
    full = pl.BlockSpec(memory_space=VMEM)
    hbm = pl.BlockSpec(memory_space=pltpu.HBM)
    n, rows, own, width, T = S.n, S.rows, S.own, S.width, S.tokens
    shape = jax.ShapeDtypeStruct
    grads = [VMEM((width, c), F32) for c in S.gcols]
    parts = [VMEM((n, 2, rows, c), BF16) for c in S.gcols]
    ways = [VMEM((2, n, 2, rows, c), BF16) for c in S.gcols]
    lines = [VMEM((rows, c), BF16) for c in S.gcols]
    head = VMEM((S.heads, T, HEAD), BF16)
    scratch = [
        VMEM((2, rows, S.cols[0]), BF16),
        VMEM((rows, 2 * S.qkv), BF16),
        VMEM((rows, 2 * S.out), BF16),
    ]
    scratch += [VMEM((n, 2, 2, rows, c), BF16) for c in S.cols]
    scratch += [
        VMEM((2, 2, own, width), BF16),
        VMEM((2, 2, own, width), BF16),
        VMEM((2, 8, S.seq), F32),
        VMEM((16, 128), F32),
        VMEM((16, S.up), F32),
        VMEM((T, width), F32),
        VMEM((T, width), BF16),
        VMEM((T, width), BF16),
        VMEM((2, S.seq, S.seq), F32),
        VMEM((T, 128), F32),
        VMEM((T, 128), F32),
        VMEM((n, 2, 2, 16, 128), BF16),
        VMEM((width, T), BF16),
        VMEM((width, T), F32),
        VMEM((width, T), BF16),
        VMEM((width, T), BF16),
        VMEM((own, S.qkv), F32),
        head,
        head,
        head,
        head,
        VMEM((T, S.out), BF16),
        VMEM((T, 128), F32),
        VMEM((T, S.qkv), BF16),
        VMEM((width, S.out), BF16),
        VMEM((T, S.up), BF16),
        VMEM((T, S.up), F32),
        VMEM((T, S.up // 2), BF16),
        VMEM((T, S.up // 2), BF16),
    ]
    scratch += grads + parts + parts + parts + ways + lines + lines
    scratch += [
        VMEM((2, 4, own, width), F32),
        VMEM((2, 2, 2, own, width), BF16),
        VMEM((2, 2, 2, own, width // 2), BF16),
        VMEM((2, 2, own, width // 2), BF16),
        VMEM((2, 2, own, width // 2), BF16),
        VMEM((4, 8, S.up), F32),
        VMEM((n - 1, 8, S.up), F32),
        VMEM((3, 8, S.up), F32),
        dma((7,)),
        dma((4,)),
        dma((4,)),
        dma((5, 2, n)),
        dma((5, 2, n)),
        dma((5, n)),
        dma((5, n)),
        dma((2, 4)),
        dma((2, 4)),
        dma,
        dma,
        dma((4,)),
        dma((4,)),
        dma((4, 2, n, 2)),
        dma((4, 2, n, 2)),
        dma((4,)),
        dma((4,)),
        dma((2, 4)),
        dma((2, 4)),
        dma((3,)),
        dma((3,)),
        dma((n - 1,)),
        dma((n - 1,)),
        dma,
        dma,
        dma((n - 1,)),
        dma((n - 1,)),
        dma,
        dma,
    ]
    return pl.pallas_call(
        functools.partial(fused_kernel, S),
        out_shape=tuple(shape((2, rows, c), F32) for c in S.gcols)
        + (
            shape((own, width), F32),
            shape((own, width), F32),
            shape((2, 8, S.up), F32),
            shape((8, width), F32),
        ),
        in_specs=[hbm, hbm, full] + [hbm] * 4 + [full] * 8,
        out_specs=(full,) * 8,
        scratch_shapes=scratch,
        compiler_params=pltpu.CompilerParams(
            collective_id=2, has_side_effects=True, vmem_limit_bytes=46 * 2**20
        ),
        name="fused",
    )(*operands)


def finish_kernel(
    S,
    red_a,
    red_d,
    red_u,
    red_v,
    hs_ref,
    bs_ref,
    small_ref,
    prm_ref,
    tok_ref,
    cot_ref,
    hid_out,
    inp_out,
    qkv_out,
    qkvb_out,
    outw_out,
    g_out,
    up_out,
    upb_out,
    down_out,
    n1g_out,
    n1b_out,
    n2g_out,
    n2b_out,
    again_out,
):
    dp = lax.axis_index("dp")
    rows, width = S.rows, S.width
    for q in range(2):
        qkv_out[:, q * S.qkv : (q + 1) * S.qkv] = red_a[q, :, : S.qkv]
        middle = q * S.up + S.gcols[2]
        up_out[:, q * S.up : middle] = red_u[q]
        up_out[:, middle : (q + 1) * S.up] = red_v[q]
        outw_out[:, q * S.out : (q + 1) * S.out] = red_a[q, :, S.qkv : S.att]
        down_out[:, q * S.up : (q + 1) * S.up] = red_d[q]
    values = tok_ref[...].astype(F32)
    unit, inv_std = unit_rows(values)
    hid_out[...] = (values + hs_ref[...] + prm_ref[4:5] + prm_ref[5:6]).astype(BF16)
    total = bs_ref[...]
    mean_term = jnp.mean(total, axis=-1, keepdims=True)
    proj_term = jnp.mean(total * unit, axis=-1, keepdims=True)
    inp_out[...] = cot_ref[...].astype(F32) + inv_std * (total - mean_term - unit * proj_term)

    def shift(block, by):
        return pltpu.roll(block, lax.rem(S.up - by, S.up), 1)

    low = shift(small_ref[1], dp * rows)
    for row, out in enumerate((n1g_out, n1b_out, n2g_out, n2b_out, g_out)):
        out[...] = low[row : row + 1, :rows]
    again_out[...] = low[4:5, :rows]
    place = lax.rem(dp, 2 * S.n)
    own_sums = small_ref[0]
    both = [jnp.broadcast_to(own_sums[i : i + 1], (8, S.up)) for i in (5, 6)]
    qkvb_out[...] = shift(both[0], place * S.qkvb)[0:1, : S.qkvb]
    upb_out[...] = shift(both[1], place * S.upb)[0:1, : S.upb]


def finish(S, operands):
    shape = jax.ShapeDtypeStruct
    row = shape((1, S.rows), F32)
    return pl.pallas_call(
        functools.partial(finish_kernel, S),
        out_shape=(
            shape((S.own, S.width), BF16),
            shape((S.own, S.width), F32),
            shape((S.rows, 2 * S.qkv), F32),
            shape((1, S.qkvb), F32),
            shape((S.rows, 2 * S.out), F32),
            row,
            shape((S.rows, 2 * S.up), F32),
            shape((1, S.upb), F32),
            shape((S.rows, 2 * S.up), F32),
            row,
            row,
            row,
            row,
            row,
        ),
        compiler_params=pltpu.CompilerParams(vmem_limit_bytes=40 * 2**20),
        name="finish",
    )(*operands)


def on_plane(S, args):
    (tokens, segments, positions, cotangent, qkv_weight, qkv_bias, out_weight, out_bias) = args[:8]
    (up_weight, up_bias, down_weight, down_bias, g1, b1, g2, b2) = args[8:]
    def stay(array):
        return pltpu.with_memory_space_constraint(array, pltpu.HBM)

    made = fused(
        S,
        (
            stay(tokens),
            stay(cotangent),
            positions.reshape(1, -1),
            stay(qkv_weight[0]),
            stay(out_weight[0].T),
            stay(up_weight[0]),
            stay(down_weight[0].T),
            g1,
            b1,
            g2,
            b2,
            out_bias,
            down_bias,
            qkv_bias,
            up_bias,
        ),
    )
    outs = finish(S, tuple(made) + (tokens, cotangent))
    hid, inp, qkv, qkvb, outw, gsum, upw, upb, downw, n1g, n1b, n2g, n2b, gsum_again = outs
    return (
        hid[None],
        inp,
        qkv[None],
        qkvb,
        outw.T[None],
        gsum,
        upw[None],
        upb,
        downw.T[None],
        gsum_again,
        n1g,
        n1b,
        n2g,
        n2b,
    )


def on_device(
    tokens,
    segments,
    positions,
    cotangent,
    qkv_weight,
    qkv_bias,
    out_weight,
    out_bias,
    up_weight,
    up_bias,
    down_weight,
    down_bias,
    norm1_gain,
    norm1_bias,
    norm2_gain,
    norm2_bias,
):
    dp_size = lax.axis_size("dp")
    n_outer = dp_size // 4
    core = lax.rem(lax.axis_index("dp"), 2)
    x = lax.axis_index("tensor")
    own, width = tokens.shape
    rows = qkv_weight.shape[1]
    seq_len = segments.shape[0]
    plane = Shape(
        n_outer,
        rows,
        own,
        width,
        seq_len,
        qkv_weight.shape[2] // 2,
        out_weight.shape[1] // 2,
        up_weight.shape[2] // 2,
        qkv_bias.shape[1],
        up_bias.shape[1],
    )
    if plane.fits():
        return on_plane(
            plane,
            (
                tokens,
                segments,
                positions,
                cotangent,
                qkv_weight,
                qkv_bias,
                out_weight,
                out_bias,
                up_weight,
                up_bias,
                down_weight,
                down_bias,
                norm1_gain,
                norm1_bias,
                norm2_gain,
                norm2_bias,
            ),
        )
    qkv_q, up_q, out_q = (
        qkv_weight.shape[2] // 2,
        up_weight.shape[2] // 2,
        out_weight.shape[1] // 2,
    )
    sizes = Sizes(rows, up_q, qkv_q, out_q, qkv_bias.shape[1], up_bias.shape[1])
    heads = out_q // HEAD

    def halves(w):
        return jnp.swapaxes(w.reshape(rows, 2, -1), 0, 1)

    def halves_t(w):
        return jnp.swapaxes(w.reshape(2, -1, rows), 1, 2)

    small = jnp.concatenate(
        [
            jnp.stack(
                [
                    norm1_gain[0],
                    norm1_bias[0],
                    norm2_gain[0],
                    norm2_bias[0],
                    out_bias[0],
                    down_bias[0],
                ],
                axis=1,
            ),
            fold(qkv_bias[0], 1, rows, sizes.qb_cols)[0],
            fold(up_bias[0], 1, rows, sizes.ub_cols)[0],
        ],
        axis=1,
    )
    packed = sizes.pack(
        halves(up_weight[0]),
        halves_t(down_weight[0]),
        halves(qkv_weight[0]),
        jnp.broadcast_to(small[None], (2,) + small.shape),
        halves_t(out_weight[0]),
    )
    own_pos = lax.dynamic_slice_in_dim(positions, x * own, own, 0).astype(BF16)
    rows_in = jnp.concatenate(
        [tokens, cotangent, jnp.pad(own_pos[:, None], ((0, 0), (0, 127)))], axis=1
    )
    gathered, group_rows = gather(sizes, n_outer, packed, rows_in)

    flat = gathered.reshape(dp_size * rows, sizes.cols)
    up_w = flat[:, :up_q]
    down_wt = flat[:, up_q : 2 * up_q]
    qkv_w = flat[:, sizes.qkv : sizes.qkv + qkv_q]
    out_wt = flat[:, sizes.out : sizes.out + out_q]
    smalls = flat[:, sizes.small : sizes.small + sizes.n_small].astype(F32)
    vecs = smalls[:, :6].T
    by_dev = smalls.reshape(dp_size, rows, sizes.n_small)
    qb = by_dev[:, :, 6 : 6 + sizes.qb_cols].reshape(dp_size, -1)[:, : sizes.qkvb].reshape(-1)
    ub = by_dev[:, :, 6 + sizes.qb_cols :].reshape(dp_size, -1)[:, : sizes.upb].reshape(-1)
    qkv_b = lax.dynamic_slice_in_dim(qb, core * qkv_q, qkv_q, 0)
    up_b = lax.dynamic_slice_in_dim(ub, core * up_q, up_q, 0)

    group_rows = group_rows.reshape(4 * own, -1)
    count = 4 * own
    seqs = count // seq_len
    xs = group_rows[:, :width].astype(F32)
    cot = group_rows[:, width : 2 * width]
    pos = group_rows[:, 2 * width].astype(F32).reshape(seqs, seq_len)
    cos_tab, sin_tab = rotary_tables(pos)
    query_index = jnp.arange(seq_len, dtype=F32)
    key_index = query_index[None, None, :]
    first_key = query_index[None, :] - pos
    allowed = (
        (key_index <= query_index[None, :, None]) & (key_index >= first_key[:, :, None])
    )[:, None]

    unit, _ = unit_rows(xs)
    n1 = (unit * vecs[0] + vecs[1]).astype(BF16)
    n2 = (unit * vecs[2] + vecs[3]).astype(BF16)
    projected = (dot(n1, qkv_w, 1, 0) + qkv_b).reshape(seqs, seq_len, heads, 3, HEAD)
    projected = jnp.transpose(projected, (3, 0, 2, 1, 4))
    query = rotate(projected[0], cos_tab, sin_tab).astype(BF16)
    key = rotate(projected[1], cos_tab, sin_tab).astype(BF16)
    value = projected[2].astype(BF16)
    scale = HEAD ** (-0.5)

    def ein(spec, a, b):
        return jnp.einsum(spec, a, b, preferred_element_type=F32)

    scores = jnp.where(allowed, ein("shqd,shkd->shqk", query, key) * scale, -jnp.inf)
    peak = jnp.max(scores, axis=-1, keepdims=True)
    log_total = peak + jnp.log(jnp.sum(jnp.exp(scores - peak), axis=-1, keepdims=True))
    weights = jnp.exp(scores - log_total)
    weights_bf = weights.astype(BF16)
    attended = ein("shqk,shkd->shqd", weights_bf, value).astype(BF16)
    attended_flat = jnp.swapaxes(attended, 1, 2).reshape(count, out_q)
    pre = dot(n2, up_w, 1, 0) + up_b
    cumul = 0.5 * (1.0 + jax.scipy.special.erf(pre * 0.7071067811865476))
    act = (pre * cumul).astype(BF16)
    slope = cumul + pre * jnp.exp(-0.5 * pre * pre) * 0.3989422804014327
    mixed = dot(attended_flat, out_wt, 1, 1) + dot(act, down_wt, 1, 1)

    du = (dot(cot, down_wt, 1, 0) * slope).astype(BF16)
    g_upb = jnp.sum(du.astype(F32), axis=0)
    dn2 = dot(du, up_w, 1, 1)
    d_att = dot(cot, out_wt, 1, 0).astype(BF16).reshape(seqs, seq_len, heads, HEAD)
    d_att = jnp.swapaxes(d_att, 1, 2)
    delta = jnp.sum(attended.astype(F32) * d_att.astype(F32), axis=-1, keepdims=True)
    d_value = ein("shqk,shqd->shkd", weights_bf, d_att)
    d_weight = ein("shqd,shkd->shqk", d_att, value)
    d_score = (weights * (d_weight - delta) * scale).astype(BF16)
    d_query = unrotate(ein("shqk,shkd->shqd", d_score, key), cos_tab, sin_tab)
    d_key = unrotate(ein("shqk,shqd->shkd", d_score, query), cos_tab, sin_tab)
    d_qkv = jnp.stack([d_query, d_key, d_value], axis=0).astype(BF16)
    d_qkv = jnp.transpose(d_qkv, (1, 3, 2, 0, 4)).reshape(count, qkv_q)
    g_qkvb = jnp.sum(d_qkv.astype(F32), axis=0)
    dn1 = dot(d_qkv, qkv_w, 1, 1)
    back = dn1 * vecs[0] + dn2 * vecs[2]
    up_rows = cotangent.astype(F32)
    norm_rows = jnp.stack(
        [
            jnp.sum(dn1 * unit, axis=0),
            jnp.sum(dn1, axis=0),
            jnp.sum(dn2 * unit, axis=0),
            jnp.sum(dn2, axis=0),
            jnp.sum(up_rows, axis=0),
            jnp.zeros((width,), F32),
        ],
        axis=1,
    ).reshape(dp_size, rows, 6)
    own_half = jnp.arange(2)[:, None] == core
    qb_full = jnp.where(own_half, g_qkvb[None], 0.0).reshape(-1)
    ub_full = jnp.where(own_half, g_upb[None], 0.0).reshape(-1)
    small_grads = jnp.concatenate(
        [
            norm_rows,
            fold(qb_full, dp_size, rows, sizes.qb_cols),
            fold(ub_full, dp_size, rows, sizes.ub_cols),
        ],
        axis=2,
    )
    small_grads = jnp.pad(
        small_grads,
        (
            (0, 0),
            (0, 0),
            (sizes.small - sizes.tile, sizes.tile_end - sizes.small - sizes.n_small),
        ),
    ).reshape(dp_size // 2, 2, rows, -1)

    def turned(values):
        return values.T.reshape(dp_size // 2, 2, rows, count)

    operands = (
        turned(n2),
        turned(cot),
        turned(n1),
        du,
        act,
        jnp.pad(d_qkv, ((0, 0), (0, sizes.out - sizes.small))),
        attended_flat,
        small_grads,
    )
    reduced, mixed_sum, total, small_sum = scatter(
        sizes,
        n_outer,
        operands,
        mixed.astype(BF16).reshape(2, 2, own, width),
        back.astype(BF16).reshape(2, 2, own, width),
    )

    own_x = tokens.astype(F32)
    own_unit, own_inv = unit_rows(own_x)
    hidden = (own_x + mixed_sum + vecs[4] + vecs[5]).astype(BF16)
    mean_term = jnp.mean(total, axis=-1, keepdims=True)
    proj_term = jnp.mean(total * own_unit, axis=-1, keepdims=True)
    input_grad = up_rows + own_inv * (total - mean_term - own_unit * proj_term)

    def columns(start, size):
        return jnp.swapaxes(reduced[:, :, start : start + size], 0, 1).reshape(rows, 2 * size)

    def columns_t(start, size):
        return jnp.swapaxes(reduced[:, :, start : start + size], 1, 2).reshape(2 * size, rows)

    off = sizes.small - sizes.tile
    fin = small_sum[1, :, off : off + 6].T
    qb_out = small_sum[0, :, off + 6 : off + 6 + sizes.qb_cols].reshape(-1)[: sizes.qkvb]
    ub_at = off + 6 + sizes.qb_cols
    ub_out = small_sum[0, :, ub_at : ub_at + sizes.ub_cols].reshape(-1)[: sizes.upb]
    return (
        hidden[None],
        input_grad,
        columns(sizes.qkv, qkv_q)[None],
        qb_out[None],
        columns_t(sizes.out, out_q)[None],
        fin[4][None],
        columns(0, up_q)[None],
        ub_out[None],
        columns_t(sizes.down, up_q)[None],
        fin[4][None],
        fin[0][None],
        fin[1][None],
        fin[2][None],
        fin[3][None],
    )


def solution(mesh):
    in_specs = (
        P(("dp", "tensor"), None),
        P("dp"),
        P("dp"),
        P(("dp", "tensor"), None),
        P(None, "dp", "tensor"),
        P(None, ("tensor", "dp")),
        P(None, "tensor", "dp"),
        P(None, "dp"),
        P(None, "dp", "tensor"),
        P(None, ("tensor", "dp")),
        P(None, "tensor", "dp"),
        P(None, "dp"),
        P(None, "dp"),
        P(None, "dp"),
        P(None, "dp"),
        P(None, "dp"),
    )
    out_specs = (
        P(None, ("dp", "tensor"), None),
        P(("dp", "tensor"), None),
        P(None, "dp", "tensor"),
        P(None, ("tensor", "dp")),
        P(None, "tensor", "dp"),
        P(None, "dp"),
        P(None, "dp", "tensor"),
        P(None, ("tensor", "dp")),
        P(None, "tensor", "dp"),
        P(None, "dp"),
        P(None, "dp"),
        P(None, "dp"),
        P(None, "dp"),
        P(None, "dp"),
    )
    return jax.shard_map(
        on_device, mesh=mesh, in_specs=in_specs, out_specs=out_specs, check_vma=False
    )
```
